256 devices in a mesh: seq: 64 (over z, x, core), head: 4 (over y).
Axes of the slice: x: 4, y: 4, z: 8, core: 2. Of those that a mesh axis runs over, the one named last changes fastest.
Arguments:
- queries: bfloat16 [768, 65536], P('head', 'seq'), may hold values from -6 to 6
- keys: bfloat16 [768, 65536], P('head', 'seq'), may hold values from -6 to 6
- values: bfloat16 [768, 65536], P('head', 'seq'), may hold values from -36 to 36
- slide_lengths: int32 [64], replicated, may hold values from 1 to 16384, 65536 in all
- norm_gain: float32 [768], P('head'), may hold values from 0.1 to 1.9
- norm_bias: float32 [768], P('head'), may hold values from -3 to 3
Outputs:
- encoded: bfloat16 [768, 65536], P('head', 'seq')
The draws below stay inside these ranges and needn't reach their ends.
Inputs may be any that keep to these rules, and one draw needn't show every extreme that they name: `slide_lengths`: positive slide lengths that sum to 65536; the longest is exactly 16384.
All inputs are finite; a program needn't handle non-finite values.
Results may differ from the reference program's by a relative error of at most 0.0041.
Values may be sent and summed in bfloat16 or wider, within the bound.
A program may use at most 128 MiB of HBM per device.

```python
import math
import jax
import jax.numpy as jnp
import numpy as np
from jax import lax

D = 768
NH = 16
HD = 48
SEG = 1024
TOKENS = 65536
NSLIDES = 64
LONGEST = 16384


def draw_queries(key, part):
    base = jnp.clip(jax.random.normal(jax.random.fold_in(key, 1), (TOKENS, D), jnp.float32), -6.0, 6.0)
    return base.T.astype(jnp.bfloat16)


def draw_keys(key, part):
    base = jnp.clip(jax.random.normal(jax.random.fold_in(key, 2), (TOKENS, D), jnp.float32), -6.0, 6.0)
    return base.T.astype(jnp.bfloat16)


def draw_values(key, part):
    head_of = (jnp.arange(D) // HD).astype(jnp.float32)
    rising = jnp.exp(math.log(3.0) * head_of / (NH - 1))
    column = jnp.exp(jax.random.uniform(jax.random.fold_in(key, 5), (D,), minval=math.log(0.5), maxval=math.log(2.0)))
    base = jnp.clip(jax.random.normal(jax.random.fold_in(key, 6), (TOKENS, D), jnp.float32), -6.0, 6.0)
    return (base * rising[None, :] * column[None, :]).T.astype(jnp.bfloat16)


def levels(key, shape, cuts, smallest, high):
    level, own = 1.0, jax.random.fold_in(key, 6)
    for axis_at, shards_of in cuts:
        heights = jnp.exp(jax.random.uniform(jax.random.fold_in(own, axis_at), (shards_of,), jnp.float32, smallest / len(cuts), high / len(cuts)))
        level = level * jnp.repeat(heights, shape[axis_at] // shards_of).reshape([-1 if axis == axis_at else 1 for axis in range(len(shape))])
    return level


def profile(count, total, limit, skew):
    weights = [(1 << 20) // math.isqrt(rank ** skew) + 1 for rank in range(2, count + 1)]
    rest, holding = total - limit - (count - 1), [1] * (count - 1)
    while rest > 0:
        free = [i for i in range(count - 1) if holding[i] < limit]
        pool, budget = sum([weights[i] for i in free]), rest
        for i in free:
            addition = min(limit - holding[i], max(1, budget * weights[i] // pool), rest)
            holding[i] = holding[i] + addition
            rest = rest - addition
    return np.array([limit] + holding)


def uneven_parts(key, number_of, total, bound, lean):
    if number_of == 2:
        one = jax.random.randint(key, (), max(1, total - bound), min(bound, total - 1) + 1)
        return jnp.stack([one, total - one])
    lengths = jnp.asarray(profile(number_of, total, bound, lean), jnp.int32)
    pairs = (number_of - 1) // 2
    giver, sink = lengths[1:1 + 2 * pairs:2], lengths[2:2 + 2 * pairs:2]
    margin = jnp.minimum(giver - 1, bound - sink)
    moved = jax.random.randint(jax.random.fold_in(key, 1), (pairs,), 0, 1 << 20) % (margin + 1)
    lengths = lengths.at[1:1 + 2 * pairs:2].set(giver - moved).at[2:2 + 2 * pairs:2].set(sink + moved)
    return lengths[jax.random.permutation(jax.random.fold_in(key, 2), number_of)]


def noise(stream_key, dims, deviation, most, split=(), kind=jnp.bfloat16):
    values = deviation * jax.random.normal(stream_key, dims, jnp.float32)
    if split:
        values = values * levels(stream_key, dims, split, -0.22, 0.18)
    return jnp.clip(values, -most, most).astype(kind)


def setup_inputs(seed: int = 0) -> dict:
    arg_keys = jax.random.split(jax.random.key(seed), 7)
    queries = draw_queries(jax.random.fold_in(arg_keys[6], 71), 0)
    keys = draw_keys(jax.random.fold_in(arg_keys[6], 71), 0)
    values = draw_values(jax.random.fold_in(arg_keys[6], 71), 0)
    slide_lengths = uneven_parts(arg_keys[3], NSLIDES, TOKENS, LONGEST, 2).astype(jnp.int32)
    norm_gain = jnp.clip(1.0 + 0.18 * jax.random.normal(arg_keys[4], (D,), jnp.float32), 0.1, 1.9)
    norm_bias = noise(arg_keys[5], (D,), 0.5, 3.0, ((0, 4),), jnp.float32)
    return dict(queries=queries, keys=keys, values=values, slide_lengths=slide_lengths, norm_gain=norm_gain, norm_bias=norm_bias)


def slide_of(positions, slide_ends):
    return lax.optimization_barrier(jnp.sum((positions[..., None] >= slide_ends).astype(jnp.int32), axis=-1))

def attend_head(segment_items):
    query_rows, key_rows, value_rows, query_slide, key_slide = segment_items
    score_scale = 1.0 / math.sqrt(HD)
    scores = jnp.dot(query_rows, key_rows.T, preferred_element_type=jnp.float32) * score_scale
    scores = jnp.where(query_slide[:, None] == key_slide[None, :], scores, -1e+30)
    row_peak = lax.optimization_barrier(jnp.max(scores, axis=-1))
    probabilities = jnp.exp(scores - row_peak[:, None])
    totals = lax.optimization_barrier(jnp.sum(probabilities, axis=-1))
    weighted = jnp.dot(probabilities.astype(jnp.bfloat16), value_rows, preferred_element_type=jnp.float32)
    return (row_peak, totals, weighted)

def reference(queries, keys, values, slide_lengths, norm_gain, norm_bias):
    queries = queries.T
    keys = keys.T
    values = values.T
    slide_ends = jnp.cumsum(slide_lengths)

    def one_head(head_index):
        q_head = lax.dynamic_slice_in_dim(queries, head_index * HD, HD, 1)
        k_head = lax.dynamic_slice_in_dim(keys, head_index * HD, HD, 1)
        v_head = lax.dynamic_slice_in_dim(values, head_index * HD, HD, 1)
        running_peak = None
        weight = None
        accumulated = None
        for branch in range(4):
            dilation = 4 ** branch
            seg_span = min(SEG * dilation, TOKENS)
            seg_keys = seg_span // dilation
            compact_count = TOKENS // dilation
            offset = head_index % dilation

            def choose(matrix):
                shaped = matrix.reshape(compact_count, dilation, HD)
                return lax.dynamic_slice_in_dim(shaped, offset, 1, 1)[:, 0]
            compact_pos = dilation * jnp.arange(compact_count, dtype=jnp.int32) + offset
            compact_slide = slide_of(compact_pos, slide_ends)
            segment_count = TOKENS // seg_span
            items = (choose(q_head).reshape(segment_count, seg_keys, HD), choose(k_head).reshape(segment_count, seg_keys, HD), choose(v_head).reshape(segment_count, seg_keys, HD), compact_slide.reshape(segment_count, seg_keys), compact_slide.reshape(segment_count, seg_keys))
            row_peak, totals, weighted = lax.map(attend_head, items)
            row_peak = row_peak.reshape(compact_count)
            totals = totals.reshape(compact_count)
            weighted = weighted.reshape(compact_count, HD)
            chosen = jnp.arange(dilation, dtype=jnp.int32)[None, :] == offset
            peak_full = jnp.where(chosen, row_peak[:, None], jnp.float32(-1e+30)).reshape(TOKENS)
            total_full = jnp.where(chosen, totals[:, None], jnp.float32(0.0)).reshape(TOKENS)
            mixed_full = jnp.where(chosen[:, :, None], weighted[:, None, :], jnp.float32(0.0)).reshape(TOKENS, HD)
            if running_peak is None:
                running_peak, weight, accumulated = (peak_full, total_full, mixed_full)
            else:
                newest = jnp.maximum(running_peak, peak_full)
                keep_old = jnp.exp(running_peak - newest)
                keep_new = jnp.exp(peak_full - newest)
                weight = weight * keep_old + total_full * keep_new
                accumulated = accumulated * keep_old[:, None] + mixed_full * keep_new[:, None]
                running_peak = newest
        return accumulated / weight[:, None]
    per_head = lax.map(one_head, jnp.arange(NH, dtype=jnp.int32))
    attended = jnp.transpose(per_head, (1, 0, 2)).reshape(TOKENS, D)
    row_mean = lax.optimization_barrier(jnp.sum(attended, axis=1)) / D
    variance = lax.optimization_barrier(jnp.sum(attended * attended, axis=1)) / D - row_mean * row_mean
    normed = (attended - row_mean[:, None]) * lax.rsqrt(variance + 1e-05)[:, None]
    return (normed * norm_gain + norm_bias).astype(jnp.bfloat16).T
```

```python
import math

import jax
import jax.numpy as jnp
import numpy as np
from jax import lax
from jax.sharding import Mesh
from jax.sharding import PartitionSpec as P

D = 768
HD = 48
SEG = 1024
SEQ_AXES = ("zh", "zl", "xh", "xl", "c")


def to_digit_order(x):
    lead = x.shape[:-1]
    x = x.reshape(lead + (16, 4, 4, 4))
    n = len(lead)
    x = jnp.transpose(x, tuple(range(n)) + (n + 3, n + 2, n + 1, n))
    return x.reshape(lead + (1024,))


def from_digit_order(x):
    lead = x.shape[:-1]
    x = x.reshape(lead + (4, 4, 4, 16))
    n = len(lead)
    x = jnp.transpose(x, tuple(range(n)) + (n + 3, n + 2, n + 1, n))
    return x.reshape(lead + (1024,))


def slide_of(positions, slide_ends):
    return jnp.sum((positions[..., None] >= slide_ends).astype(jnp.int32), axis=-1)


def attend(q, k, v, q_slide, k_slide):
    scale = 1.0 / math.sqrt(HD)
    s = jnp.einsum("hdq,hdk->hqk", q, k, preferred_element_type=jnp.float32) * scale
    s = jnp.where(q_slide[:, :, None] == k_slide[:, None, :], s, -1e30)
    m = jnp.max(s, axis=-1)
    p = jnp.exp(s - m[..., None])
    l = jnp.sum(p, axis=-1)
    o = jnp.einsum("hqk,hdk->hdq", p.astype(jnp.bfloat16), v, preferred_element_type=jnp.float32)
    return m, l, o


def merge(a, b):
    ma, la, oa = a
    mb, lb, ob = b
    mn = jnp.maximum(ma, mb)
    ea = jnp.exp(ma - mn)
    eb = jnp.exp(mb - mn)
    return mn, la * ea + lb * eb, oa * ea[:, None, :] + ob * eb[:, None, :]


def per_device(queries, keys, values, slide_lengths, norm_gain, norm_bias):
    heads = queries.shape[0] // HD
    seq = lax.axis_index(SEQ_AXES)
    hy = lax.axis_index("head")
    slide_ends = jnp.cumsum(slide_lengths)
    q = to_digit_order(queries).reshape(heads, HD, 1024)
    k = to_digit_order(keys).reshape(heads, HD, 1024)
    v = to_digit_order(values).reshape(heads, HD, 1024)
    local_pos = to_digit_order(jnp.arange(1024, dtype=jnp.int32))

    def pos_of(device, index):
        return device * 1024 + local_pos[index]

    base0 = pos_of(seq, jnp.arange(1024))
    slide0 = slide_of(base0, slide_ends)
    r0 = attend(q, k, v, jnp.broadcast_to(slide0, (heads, 1024)), jnp.broadcast_to(slide0, (heads, 1024)))

    results = []
    for branch, (count, axes) in enumerate(
        [(256, ("xl", "c")), (64, ("zl", "xh", "xl", "c")), (16, SEQ_AXES)], start=1
    ):
        group = 1024 // count
        starts = [j * 256 + (hy * 64 if branch >= 2 else 0) for j in range(heads)]
        qs = jnp.stack([lax.dynamic_slice_in_dim(q[j], starts[j], count, 1) for j in range(heads)])
        ks = jnp.stack([lax.dynamic_slice_in_dim(k[j], starts[j], count, 1) for j in range(heads)])
        vs = jnp.stack([lax.dynamic_slice_in_dim(v[j], starts[j], count, 1) for j in range(heads)])
        kv = lax.all_gather(jnp.stack([ks, vs]), axes, axis=3, tiled=True)
        idx = jnp.stack([starts[j] + jnp.arange(count) for j in range(heads)])
        q_slide = slide_of(pos_of(seq, idx), slide_ends)
        first = seq // group * group
        members = first + jnp.arange(group)
        k_pos = pos_of(members[None, :, None], idx[:, None, :]).reshape(heads, 1024)
        k_slide = slide_of(k_pos, slide_ends)
        results.append((attend(qs, kv[0], kv[1], q_slide, k_slide), starts, count))

    (r3, _, _), (r2, _, _), (r1, _, _) = results[2], results[1], results[0]
    head2 = tuple(x[..., :16] for x in r2)
    m23 = merge(head2, r3)
    r2 = tuple(jnp.concatenate([a, b[..., 16:]], axis=-1) for a, b in zip(m23, r2))
    mid1 = tuple(lax.dynamic_slice_in_dim(x, hy * 64, 64, x.ndim - 1) for x in r1)
    m12 = merge(mid1, r2)
    r1 = tuple(lax.dynamic_update_slice_in_dim(x, y, hy * 64, x.ndim - 1) for x, y in zip(r1, m12))
    blocks0 = tuple(x.reshape(x.shape[:-1] + (4, 256)) for x in r0)
    out_m, out_l, out_o = [], [], []
    for j in range(heads):
        parts = []
        for blk in range(4):
            cur = (blocks0[0][j : j + 1, blk], blocks0[1][j : j + 1, blk], blocks0[2][j : j + 1, :, blk])
            if blk == j:
                cur = merge(cur, (r1[0][j : j + 1], r1[1][j : j + 1], r1[2][j : j + 1]))
            parts.append(cur)
        out_l.append(jnp.concatenate([p_[1] for p_ in parts], axis=-1))
        out_o.append(jnp.concatenate([p_[2] for p_ in parts], axis=-1))
    total = jnp.concatenate(out_l, axis=0)
    part = jnp.concatenate(out_o, axis=0)
    attended = (part / total[:, None, :]).reshape(heads * HD, 1024)
    sums = lax.psum(
        jnp.stack([jnp.sum(attended, axis=0), jnp.sum(attended * attended, axis=0)]), "head"
    )
    mean = sums[0] / D
    var = sums[1] / D - mean * mean
    normed = (attended - mean[None, :]) * lax.rsqrt(var + 1e-05)[None, :]
    out = (normed * norm_gain[:, None] + norm_bias[:, None]).astype(jnp.bfloat16)
    return from_digit_order(out)


def solution(mesh):
    devices = np.asarray(mesh.devices).reshape(4, 2, 2, 2, 2, mesh.devices.shape[1])
    fine = Mesh(devices, SEQ_AXES + ("head",))
    placed = (P("head", SEQ_AXES),) * 3 + (P(), P("head"), P("head"))
    return jax.shard_map(
        per_device, mesh=fine, in_specs=placed, out_specs=P("head", SEQ_AXES), check_vma=False
    )
```

```python
import math

import jax
import jax.numpy as jnp
import numpy as np
from jax import lax
from jax.sharding import Mesh
from jax.sharding import PartitionSpec as P

D = 768
HD = 48
SEG = 1024
SEQ_AXES = ("zh", "zl", "xh", "xl", "c")


def to_digit_order(x):
    lead = x.shape[:-1]
    x = x.reshape(lead + (16, 4, 4, 4))
    n = len(lead)
    x = jnp.transpose(x, tuple(range(n)) + (n + 3, n + 2, n + 1, n))
    return x.reshape(lead + (1024,))


def from_digit_order(x):
    lead = x.shape[:-1]
    x = x.reshape(lead + (4, 4, 4, 16))
    n = len(lead)
    x = jnp.transpose(x, tuple(range(n)) + (n + 3, n + 2, n + 1, n))
    return x.reshape(lead + (1024,))


def slide_of(positions, slide_ends):
    return jnp.sum((positions[..., None] >= slide_ends).astype(jnp.int32), axis=-1)


def attend(q, k, v, q_slide, k_slide):
    scale = 1.0 / math.sqrt(HD)
    s = jnp.einsum("hdq,hdk->hqk", q, k, preferred_element_type=jnp.float32) * scale
    s = jnp.where(q_slide[:, :, None] == k_slide[:, None, :], s, -1e30)
    m = jnp.max(s, axis=-1)
    p = jnp.exp(s - m[..., None])
    l = jnp.sum(p, axis=-1)
    o = jnp.einsum("hqk,hdk->hdq", p.astype(jnp.bfloat16), v, preferred_element_type=jnp.float32)
    return m, l, o


def collect(block, group, seq):
    for bit in range(group.bit_length() - 1):
        mask = 2**bit
        pairs = [(i, i ^ mask) for i in range(64)]
        partner = lax.ppermute(block, SEQ_AXES, pairs)
        upper = seq // mask % 2 == 1
        block = jnp.where(
            upper,
            jnp.concatenate([partner, block], axis=-1),
            jnp.concatenate([block, partner], axis=-1),
        )
    return block


def head_sum(x):
    for mask in (1, 2):
        x = x + lax.ppermute(x, "head", [(i, i ^ mask) for i in range(4)])
    return x


def merge(a, b):
    ma, la, oa = a
    mb, lb, ob = b
    mn = jnp.maximum(ma, mb)
    ea = jnp.exp(ma - mn)
    eb = jnp.exp(mb - mn)
    return mn, la * ea + lb * eb, oa * ea[:, None, :] + ob * eb[:, None, :]


def per_device(queries, keys, values, slide_lengths, norm_gain, norm_bias):
    heads = queries.shape[0] // HD
    seq = lax.axis_index(SEQ_AXES)
    hy = lax.axis_index("head")
    slide_ends = jnp.cumsum(slide_lengths)
    q = to_digit_order(queries).reshape(heads, HD, 1024)
    k = to_digit_order(keys).reshape(heads, HD, 1024)
    v = to_digit_order(values).reshape(heads, HD, 1024)

    def pos_of(device, index):
        local = 64 * (index % 16) + 16 * (index // 16 % 4) + 4 * (index // 64 % 4) + index // 256
        return device * 1024 + local

    base0 = pos_of(seq, jnp.arange(1024))
    slide0 = slide_of(base0, slide_ends)
    r0 = attend(q, k, v, jnp.broadcast_to(slide0, (heads, 1024)), jnp.broadcast_to(slide0, (heads, 1024)))

    results = []
    for branch, (count, axes) in enumerate(
        [(256, ("xl", "c")), (64, ("zl", "xh", "xl", "c")), (16, SEQ_AXES)], start=1
    ):
        group = 1024 // count
        starts = [j * 256 + (hy * 64 if branch >= 2 else 0) for j in range(heads)]
        qs = jnp.stack([lax.dynamic_slice_in_dim(q[j], starts[j], count, 1) for j in range(heads)])
        ks = jnp.stack([lax.dynamic_slice_in_dim(k[j], starts[j], count, 1) for j in range(heads)])
        vs = jnp.stack([lax.dynamic_slice_in_dim(v[j], starts[j], count, 1) for j in range(heads)])
        kv = collect(jnp.stack([ks, vs]), group, seq)
        idx = jnp.stack([starts[j] + jnp.arange(count) for j in range(heads)])
        q_slide = slide_of(pos_of(seq, idx), slide_ends)
        first = seq // group * group
        members = first + jnp.arange(group)
        k_pos = pos_of(members[None, :, None], idx[:, None, :]).reshape(heads, 1024)
        k_slide = slide_of(k_pos, slide_ends)
        results.append((attend(qs, kv[0], kv[1], q_slide, k_slide), starts, count))

    (r3, _, _), (r2, _, _), (r1, _, _) = results[2], results[1], results[0]
    head2 = tuple(x[..., :16] for x in r2)
    m23 = merge(head2, r3)
    r2 = tuple(jnp.concatenate([a, b[..., 16:]], axis=-1) for a, b in zip(m23, r2))
    mid1 = tuple(lax.dynamic_slice_in_dim(x, hy * 64, 64, x.ndim - 1) for x in r1)
    m12 = merge(mid1, r2)
    r1 = tuple(lax.dynamic_update_slice_in_dim(x, y, hy * 64, x.ndim - 1) for x, y in zip(r1, m12))
    blocks0 = tuple(x.reshape(x.shape[:-1] + (4, 256)) for x in r0)
    out_m, out_l, out_o = [], [], []
    for j in range(heads):
        parts = []
        for blk in range(4):
            cur = (blocks0[0][j : j + 1, blk], blocks0[1][j : j + 1, blk], blocks0[2][j : j + 1, :, blk])
            if blk == j:
                cur = merge(cur, (r1[0][j : j + 1], r1[1][j : j + 1], r1[2][j : j + 1]))
            parts.append(cur)
        out_l.append(jnp.concatenate([p_[1] for p_ in parts], axis=-1))
        out_o.append(jnp.concatenate([p_[2] for p_ in parts], axis=-1))
    total = jnp.concatenate(out_l, axis=0)
    part = jnp.concatenate(out_o, axis=0)
    attended = (part / total[:, None, :]).reshape(heads * HD, 1024)
    sums = head_sum(jnp.stack([jnp.sum(attended, axis=0), jnp.sum(attended * attended, axis=0)]))
    mean = sums[0] / D
    var = sums[1] / D - mean * mean
    normed = (attended - mean[None, :]) * lax.rsqrt(var + 1e-05)[None, :]
    out = (normed * norm_gain[:, None] + norm_bias[:, None]).astype(jnp.bfloat16)
    return from_digit_order(out)


def solution(mesh):
    devices = np.asarray(mesh.devices).reshape(4, 2, 2, 2, 2, mesh.devices.shape[1])
    fine = Mesh(devices, SEQ_AXES + ("head",))
    placed = (P("head", SEQ_AXES),) * 3 + (P(), P("head"), P("head"))
    return jax.shard_map(
        per_device, mesh=fine, in_specs=placed, out_specs=P("head", SEQ_AXES), check_vma=False
    )
```

```python
import math

import jax
import jax.numpy as jnp
from jax import lax
from jax.experimental import pallas as pl
from jax.experimental.pallas import tpu as pltpu
from jax.sharding import PartitionSpec as P

D = 768
HD = 48
SEG = 1024
LOCAL = 1024
MESH = pl.DeviceIdType.MESH
BRANCHES = ((256, 4), (64, 16), (16, 64))


def to_token_major(x, heads):
    x = x.reshape(heads, HD, 16, 4, 4, 4)
    x = jnp.transpose(x, (0, 5, 4, 3, 2, 1))
    return x.reshape(heads, LOCAL, HD)


def from_token_major(x, heads):
    x = x.reshape(heads, 4, 4, 4, 16, HD)
    x = jnp.transpose(x, (0, 5, 4, 3, 2, 1))
    return x.reshape(heads * HD, LOCAL)


def pos_of(device, index):
    local = 64 * (index % 16) + 16 * (index // 16 % 4) + 4 * (index // 64 % 4) + index // 256
    return device * LOCAL + local


def slide_of(positions, slide_ends):
    return jnp.sum((positions[..., None] >= slide_ends).astype(jnp.int32), axis=-1)


def attention_kernel(
    q_ref, k_ref, v_ref, s1_ref, s2_ref, s3_ref,
    sq0_ref, sk0_ref, sq1_ref, sk1_ref, sq2_ref, sk2_ref, sq3_ref, sk3_ref,
    out_ref,
    kv1, kv2, kv3, m_acc, l_acc, send_sem, recv_sem, local_sem,
):
    heads = q_ref.shape[0]
    devices = lax.axis_size("seq")
    me = lax.axis_index("seq")
    hy = lax.axis_index("head")
    scale = 1.0 / math.sqrt(HD)
    sends = (s1_ref, s2_ref, s3_ref)
    bufs = (kv1, kv2, kv3)

    barrier = pltpu.get_barrier_semaphore()

    def greet(o, carry):
        pl.semaphore_signal(barrier, inc=1, device_id=(lax.rem(me + o, devices), hy), device_id_type=MESH)
        return carry

    lax.fori_loop(1, devices, greet, 0)
    pl.semaphore_wait(barrier, devices - 1)

    def window(b, start, rows):
        return bufs[b].at[:, :, pl.ds(start, rows), :]

    locals_ = []
    for b, (count, group) in enumerate(BRANCHES):
        member = lax.rem(me, group)
        cp = pltpu.make_async_copy(sends[b], window(b, pl.multiple_of(member * count, 16), count), local_sem.at[b])
        cp.start()
        locals_.append(cp)
    for b, (count, group) in enumerate(BRANCHES):
        member = lax.rem(me, group)
        first = me - member

        def push(o, carry, b=b, count=count, group=group, member=member, first=first):
            target = first + lax.rem(member + o, group)
            pltpu.make_async_remote_copy(
                src_ref=sends[b],
                dst_ref=window(b, pl.multiple_of(member * count, 16), count),
                send_sem=send_sem.at[b],
                recv_sem=recv_sem.at[b],
                device_id=(target, hy),
                device_id_type=MESH,
            ).start()
            return carry

        lax.fori_loop(1, group, push, 0)

    def attend(q, k, v, sq, sk):
        s = lax.dot_general(q, k, (((1,), (1,)), ((), ())), preferred_element_type=jnp.float32) * scale
        s = jnp.where(sq == sk, s, -1e30)
        m = jnp.max(s, axis=-1, keepdims=True)
        p = jnp.exp(s - m)
        l = jnp.sum(p, axis=-1, keepdims=True)
        o = jnp.dot(p.astype(jnp.bfloat16), v, preferred_element_type=jnp.float32)
        return m, l, o

    chunk = 256
    per_head = LOCAL // chunk

    def branch0(i, carry):
        j = i // per_head
        rows = pl.ds(pl.multiple_of(i % per_head * chunk, chunk), chunk)
        m, l, o = attend(q_ref[j, rows], k_ref[j], v_ref[j], sq0_ref[rows], sk0_ref[...])
        m_acc[j, rows] = m
        l_acc[j, rows] = l
        out_ref[j, rows] = o
        return carry

    lax.fori_loop(0, heads * per_head, branch0, 0)

    for b, (count, group) in enumerate(BRANCHES):
        locals_[b].wait()
        pltpu.make_async_copy(window(b, 0, (group - 1) * count), window(b, 0, (group - 1) * count), recv_sem.at[b]).wait()
        sq_ref, sk_ref = ((sq1_ref, sk1_ref), (sq2_ref, sk2_ref), (sq3_ref, sk3_ref))[b]

        def branch(j, carry, b=b, count=count, sq_ref=sq_ref, sk_ref=sk_ref):
            start = j * 256 + (hy * 64 if b >= 1 else 0)
            rows = pl.ds(pl.multiple_of(start, 16), count)
            m_new, l_new, o_new = attend(
                q_ref[j, rows], bufs[b][0, j], bufs[b][1, j], sq_ref[j], sk_ref[j]
            )
            m_old = m_acc[j, rows]
            mn = jnp.maximum(m_old, m_new)
            keep_old = jnp.exp(m_old - mn)
            keep_new = jnp.exp(m_new - mn)
            m_acc[j, rows] = mn
            l_acc[j, rows] = l_acc[j, rows] * keep_old + l_new * keep_new
            out_ref[j, rows] = out_ref[j, rows] * keep_old + o_new * keep_new
            return carry

        lax.fori_loop(0, heads, branch, 0)

    def finish(j, carry):
        out_ref[j] = out_ref[j] / l_acc[j]
        return carry

    lax.fori_loop(0, heads, finish, 0)

    for b, (count, group) in enumerate(BRANCHES):
        pltpu.make_async_copy(window(b, 0, (group - 1) * count), window(b, 0, (group - 1) * count), send_sem.at[b]).wait()


def head_sum(x):
    for mask in (1, 2):
        x = x + lax.ppermute(x, "head", [(i, i ^ mask) for i in range(4)])
    return x


def per_device(queries, keys, values, slide_lengths, norm_gain, norm_bias):
    heads = queries.shape[0] // HD
    seq = lax.axis_index("seq")
    hy = lax.axis_index("head")
    slide_ends = jnp.cumsum(slide_lengths)
    q = to_token_major(queries, heads)
    k = to_token_major(keys, heads)
    v = to_token_major(values, heads)

    slide0 = slide_of(pos_of(seq, jnp.arange(LOCAL)), slide_ends)
    sends, slides = [], []
    for b, (count, group) in enumerate(BRANCHES):
        starts = [j * 256 + (hy * 64 if b >= 1 else 0) for j in range(heads)]
        ks = jnp.stack([lax.dynamic_slice_in_dim(k[j], starts[j], count, 0) for j in range(heads)])
        vs = jnp.stack([lax.dynamic_slice_in_dim(v[j], starts[j], count, 0) for j in range(heads)])
        sends.append(jnp.stack([ks, vs]))
        idx = jnp.stack([starts[j] + jnp.arange(count) for j in range(heads)])
        q_slide = slide_of(pos_of(seq, idx), slide_ends)
        first = seq // group * group
        members = first + jnp.arange(group)
        k_slide = slide_of(pos_of(members[None, :, None], idx[:, None, :]), slide_ends)
        slides += [q_slide.reshape(heads, count, 1), k_slide.reshape(heads, 1, group * count)]

    vmem = pl.BlockSpec(memory_space=pltpu.VMEM)
    attended = pl.pallas_call(
        attention_kernel,
        out_shape=jax.ShapeDtypeStruct((heads, LOCAL, HD), jnp.float32),
        in_specs=[vmem] * 14,
        out_specs=vmem,
        scratch_shapes=[
            pltpu.VMEM((2, heads, LOCAL, HD), jnp.bfloat16),
            pltpu.VMEM((2, heads, LOCAL, HD), jnp.bfloat16),
            pltpu.VMEM((2, heads, LOCAL, HD), jnp.bfloat16),
            pltpu.VMEM((heads, LOCAL, 1), jnp.float32),
            pltpu.VMEM((heads, LOCAL, 1), jnp.float32),
            pltpu.SemaphoreType.DMA((3,)),
            pltpu.SemaphoreType.DMA((3,)),
            pltpu.SemaphoreType.DMA((3,)),
        ],
        compiler_params=pltpu.CompilerParams(
            collective_id=0, has_side_effects=True, vmem_limit_bytes=60 * 1024 * 1024
        ),
    )(q, k, v, *sends, slide0.reshape(LOCAL, 1), slide0.reshape(1, LOCAL), *slides)

    feats = jnp.sum(attended, axis=(0, 2))
    squares = jnp.sum(attended * attended, axis=(0, 2))
    sums = head_sum(jnp.stack([feats, squares]))
    mean = sums[0] / D
    var = sums[1] / D - mean * mean
    normed = (attended - mean[None, :, None]) * lax.rsqrt(var + 1e-05)[None, :, None]
    gain = norm_gain.reshape(heads, 1, HD)
    bias = norm_bias.reshape(heads, 1, HD)
    out = (normed * gain + bias).astype(jnp.bfloat16)
    return from_token_major(out, heads)


def solution(mesh):
    placed = (P("head", "seq"),) * 3 + (P(), P("head"), P("head"))
    return jax.shard_map(
        per_device, mesh=mesh, in_specs=placed, out_specs=P("head", "seq"), check_vma=False
    )
```

```python
import math

import jax
import jax.numpy as jnp
from jax import lax
from jax.experimental import pallas as pl
from jax.experimental.pallas import tpu as pltpu
from jax.sharding import PartitionSpec as P

D = 768
HD = 48
SEG = 1024
LOCAL = 1024
MESH = pl.DeviceIdType.MESH
BRANCHES = ((256, 4), (64, 16), (16, 64))
SHIFT = 64


def to_token_major(x):
    f = x.shape[0]
    x = x.reshape(f, 16, 4, 4, 4)
    x = jnp.transpose(x, (4, 3, 2, 1, 0))
    return x.reshape(LOCAL, f)


def from_token_major(x):
    f = x.shape[1]
    x = x.reshape(4, 4, 4, 16, f)
    x = jnp.transpose(x, (4, 3, 2, 1, 0))
    return x.reshape(f, LOCAL)


def pos_of(device, index):
    local = 64 * (index % 16) + 16 * (index // 16 % 4) + 4 * (index // 64 % 4) + index // 256
    return device * LOCAL + local


def slide_of(positions, slide_ends):
    return jnp.sum((positions[..., None] >= slide_ends).astype(jnp.int32), axis=-1)


def attention_kernel(
    q_ref, kv_ref, s1_ref, s2_ref, s3_ref, sq_ref, sk_ref,
    out_ref,
    kv1, kv2, kv3, m_acc, l_acc, send_sem, recv_sem, local_sem,
):
    heads = 4
    me = lax.axis_index("seq")
    hy = lax.axis_index("head")
    devices = lax.axis_size("seq")
    scale = 1.0 / math.sqrt(HD)
    sends = (s1_ref, s2_ref, s3_ref)
    bufs = (kv1, kv2, kv3)
    width = heads * HD

    barrier = pltpu.get_barrier_semaphore()

    def greet(o, carry):
        pl.semaphore_signal(barrier, inc=1, device_id=(lax.rem(me + o, devices), hy), device_id_type=MESH)
        return carry

    lax.fori_loop(1, devices, greet, 0)
    pl.semaphore_wait(barrier, devices - 1)

    def window(b, start, rows):
        return bufs[b].at[pl.ds(pl.multiple_of(start, 16), rows), :]

    locals_ = []
    for b, (count, group) in enumerate(BRANCHES):
        member = lax.rem(me, group)
        cp = pltpu.make_async_copy(sends[b], window(b, member * count, count), local_sem.at[b])
        cp.start()
        locals_.append(cp)
    for b, (count, group) in enumerate(BRANCHES):
        member = lax.rem(me, group)
        first = me - member

        def push(o, carry, b=b, count=count, group=group, member=member, first=first):
            target = first + lax.rem(member + o, group)
            pltpu.make_async_remote_copy(
                src_ref=sends[b],
                dst_ref=window(b, member * count, count),
                send_sem=send_sem.at[b],
                recv_sem=recv_sem.at[b],
                device_id=(target, hy),
                device_id_type=MESH,
            ).start()
            return carry

        lax.fori_loop(1, group, push, 0)

    q_lane = lax.broadcasted_iota(jnp.int32, (1, 256), 1) // HD
    o_lane = (lax.broadcasted_iota(jnp.int32, (1, 256), 1) - SHIFT) // HD

    def attend(q, j, kv, same):
        qz = jnp.where(q_lane == j, q, jnp.zeros_like(q))
        s = lax.dot_general(qz, kv[:, :256], (((1,), (1,)), ((), ())), preferred_element_type=jnp.float32)
        s = jnp.where(same, s * scale, -1e30)
        m = jnp.max(s, axis=-1, keepdims=True)
        p = jnp.exp(s - m)
        l = jnp.sum(p, axis=-1, keepdims=True)
        o = jnp.dot(p.astype(jnp.bfloat16), kv[:, 128:], preferred_element_type=jnp.float32)
        return m, l, o

    chunk = 256

    def branch0(i, carry):
        rows = pl.ds(pl.multiple_of(i * chunk, chunk), chunk)
        q = q_ref[rows]
        kv = kv_ref[...]
        same = sq_ref[rows] == sk_ref[0]
        mm = ll = oo = None
        for j in range(heads):
            m, l, o = attend(q, j, kv, same)
            if j == 0:
                mm = jnp.broadcast_to(m, (chunk, 256))
                ll = jnp.broadcast_to(l, (chunk, 256))
                oo = o
            else:
                pick = o_lane == j
                mm = jnp.where(pick, m, mm)
                ll = jnp.where(pick, l, ll)
                oo = jnp.where(pick, o, oo)
        m_acc[rows] = mm
        l_acc[rows] = ll
        out_ref[rows] = oo
        return carry

    lax.fori_loop(0, LOCAL // chunk, branch0, 0)

    for b, (count, group) in enumerate(BRANCHES):
        locals_[b].wait()
        pltpu.make_async_copy(window(b, 0, (group - 1) * count), window(b, 0, (group - 1) * count), recv_sem.at[b]).wait()

        def branch(j, carry, b=b, count=count):
            start = j * 256 + (hy * 64 if b >= 1 else 0)
            rows = pl.ds(pl.multiple_of(start, 16), count)
            same = sq_ref[rows] == sk_ref[1 + b * heads + j]
            m_new, l_new, o_new = attend(q_ref[rows], j, bufs[b][...], same)
            m_old = m_acc[rows]
            mn = jnp.maximum(m_old, m_new)
            keep_old = jnp.exp(m_old - mn)
            keep_new = jnp.exp(m_new - mn)
            pick = o_lane == j
            m_acc[rows] = jnp.where(pick, mn, m_old)
            l_acc[rows] = jnp.where(pick, l_acc[rows] * keep_old + l_new * keep_new, l_acc[rows])
            out_ref[rows] = jnp.where(pick, out_ref[rows] * keep_old + o_new * keep_new, out_ref[rows])
            return carry

        lax.fori_loop(0, heads, branch, 0)

    def finish(i, carry):
        rows = pl.ds(pl.multiple_of(i * chunk, chunk), chunk)
        out_ref[rows] = out_ref[rows] / l_acc[rows]
        return carry

    lax.fori_loop(0, LOCAL // chunk, finish, 0)

    for b, (count, group) in enumerate(BRANCHES):
        pltpu.make_async_copy(window(b, 0, (group - 1) * count), window(b, 0, (group - 1) * count), send_sem.at[b]).wait()


def head_sum(x):
    for mask in (1, 2):
        x = x + lax.ppermute(x, "head", [(i, i ^ mask) for i in range(4)])
    return x


def per_device(queries, keys, values, slide_lengths, norm_gain, norm_bias):
    heads = queries.shape[0] // HD
    width = heads * HD
    seq = lax.axis_index("seq")
    hy = lax.axis_index("head")
    slide_ends = jnp.cumsum(slide_lengths)
    q = to_token_major(jnp.concatenate([queries, jnp.zeros((256 - width, LOCAL), queries.dtype)]))
    kv = to_token_major(jnp.concatenate([keys, values]))
    kv_lane = jnp.arange(2 * width) % width // HD

    positions = [pos_of(seq, jnp.arange(LOCAL))]
    sends = []
    for b, (count, group) in enumerate(BRANCHES):
        starts = [j * 256 + (hy * 64 if b >= 1 else 0) for j in range(heads)]
        chunk = jnp.zeros((count, 2 * width), kv.dtype)
        for j in range(heads):
            piece = lax.dynamic_slice_in_dim(kv, starts[j], count, 0)
            chunk = jnp.where(kv_lane[None, :] == j, piece, chunk)
        sends.append(chunk)
        first = seq // group * group
        members = first + jnp.arange(group)
        for j in range(heads):
            idx = starts[j] + jnp.arange(count)
            positions.append(pos_of(members[:, None], idx[None, :]).reshape(group * count))
    slides = slide_of(jnp.stack(positions), slide_ends)

    vmem = pl.BlockSpec(memory_space=pltpu.VMEM)
    acc = pl.pallas_call(
        attention_kernel,
        out_shape=jax.ShapeDtypeStruct((LOCAL, 256), jnp.float32),
        in_specs=[vmem] * 7,
        out_specs=vmem,
        scratch_shapes=[
            pltpu.VMEM((LOCAL, 2 * width), jnp.bfloat16),
            pltpu.VMEM((LOCAL, 2 * width), jnp.bfloat16),
            pltpu.VMEM((LOCAL, 2 * width), jnp.bfloat16),
            pltpu.VMEM((LOCAL, 256), jnp.float32),
            pltpu.VMEM((LOCAL, 256), jnp.float32),
            pltpu.SemaphoreType.DMA((3,)),
            pltpu.SemaphoreType.DMA((3,)),
            pltpu.SemaphoreType.DMA((3,)),
        ],
        compiler_params=pltpu.CompilerParams(
            collective_id=0, has_side_effects=True, vmem_limit_bytes=60 * 1024 * 1024
        ),
    )(q, kv, *sends, slides[0].reshape(LOCAL, 1), slides.reshape(-1, 1, LOCAL))

    attended = acc[:, SHIFT : SHIFT + width]
    feats = jnp.sum(attended, axis=1)
    squares = jnp.sum(attended * attended, axis=1)
    sums = head_sum(jnp.stack([feats, squares]))
    mean = sums[0] / D
    var = sums[1] / D - mean * mean
    normed = (attended - mean[:, None]) * lax.rsqrt(var + 1e-05)[:, None]
    out = (normed * norm_gain[None, :] + norm_bias[None, :]).astype(jnp.bfloat16)
    return from_token_major(out)


def solution(mesh):
    placed = (P("head", "seq"),) * 3 + (P(), P("head"), P("head"))
    return jax.shard_map(
        per_device, mesh=mesh, in_specs=placed, out_specs=P("head", "seq"), check_vma=False
    )
```

```python
import math

import jax
import jax.numpy as jnp
from jax import lax
from jax.experimental import pallas as pl
from jax.experimental.pallas import tpu as pltpu
from jax.sharding import PartitionSpec as P

D = 768
HD = 48
SEG = 1024
LOCAL = 1024
MESH = pl.DeviceIdType.MESH
BRANCHES = ((256, 4), (64, 16), (16, 64))
SHIFT = 64


def to_token_major(x):
    f = x.shape[0]
    x = x.reshape(f, 16, 4, 4, 4)
    x = jnp.transpose(x, (4, 3, 2, 1, 0))
    return x.reshape(LOCAL, f)


def from_token_major(x):
    f = x.shape[1]
    x = x.reshape(4, 4, 4, 16, f)
    x = jnp.transpose(x, (4, 3, 2, 1, 0))
    return x.reshape(f, LOCAL)


def pos_of(device, index):
    local = 64 * (index % 16) + 16 * (index // 16 % 4) + 4 * (index // 64 % 4) + index // 256
    return device * LOCAL + local


def slide_of(positions, slide_ends):
    return jnp.sum((positions[..., None] >= slide_ends).astype(jnp.int32), axis=-1)


def attention_kernel(
    q_ref, kv_ref, s1_ref, s2_ref, s3_ref, sq_ref, sk_ref,
    out_ref,
    kv1, kv2, kv3, m_acc, l_acc, send_sem, recv_sem, local_sem, fwd_send, fwd_recv,
):
    heads = 4
    me = lax.axis_index("seq")
    hy = lax.axis_index("head")
    devices = lax.axis_size("seq")
    scale = 1.0 / math.sqrt(HD)
    sends = (s1_ref, s2_ref, s3_ref)
    bufs = (kv1, kv2, kv3)
    width = heads * HD

    barrier = pltpu.get_barrier_semaphore()

    def greet(o, carry):
        pl.semaphore_signal(barrier, inc=1, device_id=(lax.rem(me + o, devices), hy), device_id_type=MESH)
        return carry

    lax.fori_loop(1, devices, greet, 0)
    pl.semaphore_wait(barrier, devices - 1)

    def slot(b, half, pair):
        return bufs[b].at[pair, half]

    sibling = me + 1 - 2 * (me % 2)
    side = me % 2
    locals_ = []
    for b, (count, group) in enumerate(BRANCHES):
        member = lax.rem(me, group)
        cp = pltpu.make_async_copy(sends[b], slot(b, side, member // 2), local_sem.at[b])
        cp.start()
        locals_.append(cp)
    for b, (count, group) in enumerate(BRANCHES):
        member = lax.rem(me, group)
        first = me - member
        pairs = group // 2

        def push(o, carry, b=b, pairs=pairs, member=member, first=first):
            target = first + 2 * lax.rem(member // 2 + o, pairs) + side
            pltpu.make_async_remote_copy(
                src_ref=sends[b],
                dst_ref=slot(b, side, member // 2),
                send_sem=send_sem.at[b],
                recv_sem=recv_sem.at[b],
                device_id=(target, hy),
                device_id_type=MESH,
            ).start()
            return carry

        lax.fori_loop(1, pairs, push, 0)

    q_lane = lax.broadcasted_iota(jnp.int32, (1, 256), 1) // HD
    o_lane = (lax.broadcasted_iota(jnp.int32, (1, 256), 1) - SHIFT) // HD

    def attend(q, j, kv, same):
        qz = jnp.where(q_lane == j, q, jnp.zeros_like(q))
        s = lax.dot_general(qz, kv[:, :256], (((1,), (1,)), ((), ())), preferred_element_type=jnp.float32)
        s = jnp.where(same, s * scale, -1e30)
        m = jnp.max(s, axis=-1, keepdims=True)
        p = jnp.exp(s - m)
        l = jnp.sum(p, axis=-1, keepdims=True)
        o = jnp.dot(p.astype(jnp.bfloat16), kv[:, 128:], preferred_element_type=jnp.float32)
        return m, l, o

    chunk = 256

    def branch0(i, carry):
        rows = pl.ds(pl.multiple_of(i * chunk, chunk), chunk)
        q = q_ref[rows]
        kv = kv_ref[...]
        same = sq_ref[rows] == sk_ref[0]
        mm = ll = oo = None
        for j in range(heads):
            m, l, o = attend(q, j, kv, same)
            if j == 0:
                mm = jnp.broadcast_to(m, (chunk, 256))
                ll = jnp.broadcast_to(l, (chunk, 256))
                oo = o
            else:
                pick = o_lane == j
                mm = jnp.where(pick, m, mm)
                ll = jnp.where(pick, l, ll)
                oo = jnp.where(pick, o, oo)
        m_acc[rows] = mm
        l_acc[rows] = ll
        out_ref[rows] = oo
        return carry

    lax.fori_loop(0, LOCAL // chunk, branch0, 0)

    forwards = []
    for b, (count, group) in enumerate(BRANCHES):
        pairs = group // 2
        locals_[b].wait()
        if pairs > 1:
            got = bufs[b].at[pl.ds(0, pairs - 1), side]
            pltpu.make_async_copy(got, got, recv_sem.at[b]).wait()
        cp = pltpu.make_async_remote_copy(
            src_ref=bufs[b].at[:, side],
            dst_ref=bufs[b].at[:, side],
            send_sem=fwd_send.at[b],
            recv_sem=fwd_recv.at[b],
            device_id=(sibling, hy),
            device_id_type=MESH,
        )
        cp.start()
        forwards.append(cp)

    for b, (count, group) in enumerate(BRANCHES):
        other = bufs[b].at[:, 1 - side]
        pltpu.make_async_copy(other, other, fwd_recv.at[b]).wait()

        def branch(j, carry, b=b, count=count):
            start = j * 256 + (hy * 64 if b >= 1 else 0)
            rows = pl.ds(pl.multiple_of(start, 16), count)
            same = sq_ref[rows] == sk_ref[1 + b * heads + j]
            m_new, l_new, o_new = attend(q_ref[rows], j, bufs[b][...].reshape(LOCAL, 2 * width), same)
            m_old = m_acc[rows]
            mn = jnp.maximum(m_old, m_new)
            keep_old = jnp.exp(m_old - mn)
            keep_new = jnp.exp(m_new - mn)
            pick = o_lane == j
            m_acc[rows] = jnp.where(pick, mn, m_old)
            l_acc[rows] = jnp.where(pick, l_acc[rows] * keep_old + l_new * keep_new, l_acc[rows])
            out_ref[rows] = jnp.where(pick, out_ref[rows] * keep_old + o_new * keep_new, out_ref[rows])
            return carry

        lax.fori_loop(0, heads, branch, 0)

    def finish(i, carry):
        rows = pl.ds(pl.multiple_of(i * chunk, chunk), chunk)
        out_ref[rows] = out_ref[rows] / l_acc[rows]
        return carry

    lax.fori_loop(0, LOCAL // chunk, finish, 0)

    for b, (count, group) in enumerate(BRANCHES):
        pairs = group // 2
        if pairs > 1:
            went = bufs[b].at[pl.ds(0, pairs - 1), side]
            pltpu.make_async_copy(went, went, send_sem.at[b]).wait()
        forwards[b].wait_send()


def head_sum(x):
    for mask in (1, 2):
        x = x + lax.ppermute(x, "head", [(i, i ^ mask) for i in range(4)])
    return x


def per_device(queries, keys, values, slide_lengths, norm_gain, norm_bias):
    heads = queries.shape[0] // HD
    width = heads * HD
    seq = lax.axis_index("seq")
    hy = lax.axis_index("head")
    slide_ends = jnp.cumsum(slide_lengths)
    q = to_token_major(jnp.concatenate([queries, jnp.zeros((256 - width, LOCAL), queries.dtype)]))
    kv = to_token_major(jnp.concatenate([keys, values]))
    kv_lane = jnp.arange(2 * width) % width // HD

    positions = [pos_of(seq, jnp.arange(LOCAL))]
    sends = []
    for b, (count, group) in enumerate(BRANCHES):
        starts = [j * 256 + (hy * 64 if b >= 1 else 0) for j in range(heads)]
        chunk = jnp.zeros((count, 2 * width), kv.dtype)
        for j in range(heads):
            piece = lax.dynamic_slice_in_dim(kv, starts[j], count, 0)
            chunk = jnp.where(kv_lane[None, :] == j, piece, chunk)
        sends.append(chunk)
        first = seq // group * group
        members = first + jnp.arange(group)
        for j in range(heads):
            idx = starts[j] + jnp.arange(count)
            positions.append(pos_of(members[:, None], idx[None, :]).reshape(group * count))
    slides = slide_of(jnp.stack(positions), slide_ends)

    vmem = pl.BlockSpec(memory_space=pltpu.VMEM)
    acc = pl.pallas_call(
        attention_kernel,
        out_shape=jax.ShapeDtypeStruct((LOCAL, 256), jnp.float32),
        in_specs=[vmem] * 7,
        out_specs=vmem,
        scratch_shapes=[
            *[pltpu.VMEM((group // 2, 2, count, 2 * width), jnp.bfloat16) for count, group in BRANCHES],
            pltpu.VMEM((LOCAL, 256), jnp.float32),
            pltpu.VMEM((LOCAL, 256), jnp.float32),
            pltpu.SemaphoreType.DMA((3,)),
            pltpu.SemaphoreType.DMA((3,)),
            pltpu.SemaphoreType.DMA((3,)),
            pltpu.SemaphoreType.DMA((3,)),
            pltpu.SemaphoreType.DMA((3,)),
        ],
        compiler_params=pltpu.CompilerParams(
            collective_id=0, has_side_effects=True, vmem_limit_bytes=60 * 1024 * 1024
        ),
    )(q, kv, *sends, slides[0].reshape(LOCAL, 1), slides.reshape(-1, 1, LOCAL))

    attended = acc[:, SHIFT : SHIFT + width]
    feats = jnp.sum(attended, axis=1)
    squares = jnp.sum(attended * attended, axis=1)
    sums = head_sum(jnp.stack([feats, squares]))
    mean = sums[0] / D
    var = sums[1] / D - mean * mean
    normed = (attended - mean[:, None]) * lax.rsqrt(var + 1e-05)[:, None]
    out = (normed * norm_gain[None, :] + norm_bias[None, :]).astype(jnp.bfloat16)
    return from_token_major(out)


def solution(mesh):
    placed = (P("head", "seq"),) * 3 + (P(), P("head"), P("head"))
    return jax.shard_map(
        per_device, mesh=mesh, in_specs=placed, out_specs=P("head", "seq"), check_vma=False
    )
```

```python
import math

import jax
import jax.numpy as jnp
from jax import lax
from jax.experimental import pallas as pl
from jax.experimental.pallas import tpu as pltpu
from jax.sharding import PartitionSpec as P

D = 768
HD = 48
SEG = 1024
LOCAL = 1024
MESH = pl.DeviceIdType.MESH
BRANCHES = ((256, 4), (64, 16), (16, 64))
SHIFT = 64


def to_token_major(x):
    f = x.shape[0]
    x = x.reshape(f, 16, 4, 4, 4)
    x = jnp.transpose(x, (4, 3, 2, 1, 0))
    return x.reshape(LOCAL, f)


def from_token_major(x):
    f = x.shape[1]
    x = x.reshape(4, 4, 4, 16, f)
    x = jnp.transpose(x, (4, 3, 2, 1, 0))
    return x.reshape(f, LOCAL)


def pos_of(device, index):
    local = 64 * (index % 16) + 16 * (index // 16 % 4) + 4 * (index // 64 % 4) + index // 256
    return device * LOCAL + local


def slide_of(positions, slide_ends):
    return jnp.sum((positions[..., None] >= slide_ends).astype(jnp.int32), axis=-1)


def attention_kernel(
    q_ref, kv_ref, s1_ref, s2_ref, s3_ref, sq_ref, sk_ref, gain_ref, bias_ref,
    out_ref,
    kv1, kv2, kv3, m_acc, l_acc, o_acc, stats, ybuf, cols,
    send_sem, recv_sem, local_sem, fwd_send, fwd_recv, y_send, y_recv,
):
    heads = 4
    me = lax.axis_index("seq")
    hy = lax.axis_index("head")
    devices = lax.axis_size("seq")
    scale = 1.0 / math.sqrt(HD)
    sends = (s1_ref, s2_ref, s3_ref)
    bufs = (kv1, kv2, kv3)
    width = heads * HD

    barrier = pltpu.get_barrier_semaphore()

    def greet(o, carry):
        pl.semaphore_signal(barrier, inc=1, device_id=(lax.rem(me + o, devices), hy), device_id_type=MESH)
        return carry

    lax.fori_loop(1, devices, greet, 0)
    ys = lax.axis_size("head")
    for o in range(1, ys):
        pl.semaphore_signal(barrier, inc=1, device_id=(me, lax.rem(hy + o, ys)), device_id_type=MESH)
    pl.semaphore_wait(barrier, devices - 1 + ys - 1)

    def slot(b, half, pair):
        return bufs[b].at[pair, half]

    sibling = me + 1 - 2 * (me % 2)
    side = me % 2
    locals_ = []
    for b, (count, group) in enumerate(BRANCHES):
        member = lax.rem(me, group)
        cp = pltpu.make_async_copy(sends[b], slot(b, side, member // 2), local_sem.at[b])
        cp.start()
        locals_.append(cp)
    for b, (count, group) in enumerate(BRANCHES):
        member = lax.rem(me, group)
        first = me - member
        pairs = group // 2

        def push(o, carry, b=b, pairs=pairs, member=member, first=first):
            target = first + 2 * lax.rem(member // 2 + o, pairs) + side
            pltpu.make_async_remote_copy(
                src_ref=sends[b],
                dst_ref=slot(b, side, member // 2),
                send_sem=send_sem.at[b],
                recv_sem=recv_sem.at[b],
                device_id=(target, hy),
                device_id_type=MESH,
            ).start()
            return carry

        lax.fori_loop(1, pairs, push, 0)

    q_lane = lax.broadcasted_iota(jnp.int32, (1, 256), 1) // HD
    o_lane = (lax.broadcasted_iota(jnp.int32, (1, 256), 1) - SHIFT) // HD

    def attend(q, j, kv, same):
        qz = jnp.where(q_lane == j, q, jnp.zeros_like(q))
        s = lax.dot_general(qz, kv[:, :256], (((1,), (1,)), ((), ())), preferred_element_type=jnp.float32)
        s = jnp.where(same, s * scale, -1e30)
        m = jnp.max(s, axis=-1, keepdims=True)
        p = jnp.exp(s - m)
        l = jnp.sum(p, axis=-1, keepdims=True)
        o = jnp.dot(p.astype(jnp.bfloat16), kv[:, 128:], preferred_element_type=jnp.float32)
        return m, l, o

    chunk = 256

    def branch0(i, carry):
        rows = pl.ds(pl.multiple_of(i * chunk, chunk), chunk)
        q = q_ref[rows]
        kv = kv_ref[...]
        same = sq_ref[rows] == sk_ref[0]
        mm = ll = oo = None
        for j in range(heads):
            m, l, o = attend(q, j, kv, same)
            if j == 0:
                mm = jnp.broadcast_to(m, (chunk, 256))
                ll = jnp.broadcast_to(l, (chunk, 256))
                oo = o
            else:
                pick = o_lane == j
                mm = jnp.where(pick, m, mm)
                ll = jnp.where(pick, l, ll)
                oo = jnp.where(pick, o, oo)
        m_acc[rows] = mm
        l_acc[rows] = ll
        o_acc[rows] = oo
        return carry

    lax.fori_loop(0, LOCAL // chunk, branch0, 0)

    forwards = []
    for b, (count, group) in enumerate(BRANCHES):
        pairs = group // 2
        locals_[b].wait()
        if pairs > 1:
            got = bufs[b].at[pl.ds(0, pairs - 1), side]
            pltpu.make_async_copy(got, got, recv_sem.at[b]).wait()
        cp = pltpu.make_async_remote_copy(
            src_ref=bufs[b].at[:, side],
            dst_ref=bufs[b].at[:, side],
            send_sem=fwd_send.at[b],
            recv_sem=fwd_recv.at[b],
            device_id=(sibling, hy),
            device_id_type=MESH,
        )
        cp.start()
        forwards.append(cp)

    for b, (count, group) in enumerate(BRANCHES):
        other = bufs[b].at[:, 1 - side]
        pltpu.make_async_copy(other, other, fwd_recv.at[b]).wait()

        def branch(j, carry, b=b, count=count):
            start = j * 256 + (hy * 64 if b >= 1 else 0)
            rows = pl.ds(pl.multiple_of(start, 16), count)
            same = sq_ref[rows] == sk_ref[1 + b * heads + j]
            m_new, l_new, o_new = attend(q_ref[rows], j, bufs[b][...].reshape(LOCAL, 2 * width), same)
            m_old = m_acc[rows]
            mn = jnp.maximum(m_old, m_new)
            keep_old = jnp.exp(m_old - mn)
            keep_new = jnp.exp(m_new - mn)
            pick = o_lane == j
            m_acc[rows] = jnp.where(pick, mn, m_old)
            l_acc[rows] = jnp.where(pick, l_acc[rows] * keep_old + l_new * keep_new, l_acc[rows])
            o_acc[rows] = jnp.where(pick, o_acc[rows] * keep_old + o_new * keep_new, o_acc[rows])
            return carry

        lax.fori_loop(0, heads, branch, 0)

    feature = lax.broadcasted_iota(jnp.int32, (8, 256), 1) >= SHIFT
    ones = jnp.where(feature, 1.0, 0.0).astype(jnp.float32)
    first_row = lax.broadcasted_iota(jnp.int32, (8, chunk), 0) == 0

    def finish(i, carry):
        rows = pl.ds(pl.multiple_of(i * chunk, chunk), chunk)
        att = o_acc[rows] / l_acc[rows]
        o_acc[rows] = att
        dims = (((1,), (1,)), ((), ()))
        total = lax.dot_general(ones, att, dims, precision=lax.Precision.HIGHEST, preferred_element_type=jnp.float32)
        square = lax.dot_general(ones, att * att, dims, precision=lax.Precision.HIGHEST, preferred_element_type=jnp.float32)
        stats[:, rows] = jnp.where(first_row, total, square)
        return carry

    lax.fori_loop(0, LOCAL // chunk, finish, 0)
    ybuf[hy] = stats[...]
    shares = []
    for o in range(1, ys):
        cp = pltpu.make_async_remote_copy(
            src_ref=stats,
            dst_ref=ybuf.at[hy],
            send_sem=y_send.at[o - 1],
            recv_sem=y_recv.at[0],
            device_id=(me, lax.rem(hy + o, ys)),
            device_id_type=MESH,
        )
        cp.start()
        shares.append(cp)
    arrived = ybuf.at[pl.ds(0, ys - 1)]
    pltpu.make_async_copy(arrived, arrived, y_recv.at[0]).wait()
    for cp in shares:
        cp.wait_send()
    summed = ybuf[0]
    for h in range(1, ys):
        summed = summed + ybuf[h]
    mean = summed[0:1] / D
    var = summed[1:2] / D - mean * mean
    rstd = lax.rsqrt(var + 1e-05)
    pair = jnp.where(lax.broadcasted_iota(jnp.int32, (8, LOCAL), 0) == 0, mean, rstd)
    cols[...] = jnp.transpose(pair)

    def normalize(i, carry):
        rows = pl.ds(pl.multiple_of(i * chunk, chunk), chunk)
        col = cols[rows]
        normed = (o_acc[rows] - col[:, 0:1]) * col[:, 1:2]
        out_ref[rows] = (normed * gain_ref[...] + bias_ref[...]).astype(out_ref.dtype)
        return carry

    lax.fori_loop(0, LOCAL // chunk, normalize, 0)

    for b, (count, group) in enumerate(BRANCHES):
        pairs = group // 2
        if pairs > 1:
            went = bufs[b].at[pl.ds(0, pairs - 1), side]
            pltpu.make_async_copy(went, went, send_sem.at[b]).wait()
        forwards[b].wait_send()


def per_device(queries, keys, values, slide_lengths, norm_gain, norm_bias):
    heads = queries.shape[0] // HD
    width = heads * HD
    seq = lax.axis_index("seq")
    hy = lax.axis_index("head")
    slide_ends = jnp.cumsum(slide_lengths)
    q = to_token_major(jnp.concatenate([queries, jnp.zeros((256 - width, LOCAL), queries.dtype)]))
    kv = to_token_major(jnp.concatenate([keys, values]))
    kv_lane = jnp.arange(2 * width) % width // HD

    positions = [pos_of(seq, jnp.arange(LOCAL))]
    sends = []
    for b, (count, group) in enumerate(BRANCHES):
        starts = [j * 256 + (hy * 64 if b >= 1 else 0) for j in range(heads)]
        chunk = jnp.zeros((count, 2 * width), kv.dtype)
        for j in range(heads):
            piece = lax.dynamic_slice_in_dim(kv, starts[j], count, 0)
            chunk = jnp.where(kv_lane[None, :] == j, piece, chunk)
        sends.append(chunk)
        first = seq // group * group
        members = first + jnp.arange(group)
        for j in range(heads):
            idx = starts[j] + jnp.arange(count)
            positions.append(pos_of(members[:, None], idx[None, :]).reshape(group * count))
    slides = slide_of(jnp.stack(positions), slide_ends)

    lead = jnp.zeros((SHIFT,), jnp.float32)
    gain = jnp.concatenate([lead, norm_gain]).reshape(1, 256)
    bias = jnp.concatenate([lead, norm_bias]).reshape(1, 256)
    vmem = pl.BlockSpec(memory_space=pltpu.VMEM)
    out = pl.pallas_call(
        attention_kernel,
        out_shape=jax.ShapeDtypeStruct((LOCAL, 256), jnp.bfloat16),
        in_specs=[vmem] * 9,
        out_specs=vmem,
        scratch_shapes=[
            *[pltpu.VMEM((group // 2, 2, count, 2 * width), jnp.bfloat16) for count, group in BRANCHES],
            pltpu.VMEM((LOCAL, 256), jnp.float32),
            pltpu.VMEM((LOCAL, 256), jnp.float32),
            pltpu.VMEM((LOCAL, 256), jnp.float32),
            pltpu.VMEM((8, LOCAL), jnp.float32),
            pltpu.VMEM((4, 8, LOCAL), jnp.float32),
            pltpu.VMEM((LOCAL, 8), jnp.float32),
            pltpu.SemaphoreType.DMA((3,)),
            pltpu.SemaphoreType.DMA((3,)),
            pltpu.SemaphoreType.DMA((3,)),
            pltpu.SemaphoreType.DMA((3,)),
            pltpu.SemaphoreType.DMA((3,)),
            pltpu.SemaphoreType.DMA((3,)),
            pltpu.SemaphoreType.DMA((1,)),
        ],
        compiler_params=pltpu.CompilerParams(
            collective_id=0, has_side_effects=True, vmem_limit_bytes=60 * 1024 * 1024
        ),
    )(q, kv, *sends, slides[0].reshape(LOCAL, 1), slides.reshape(-1, 1, LOCAL), gain, bias)
    return from_token_major(out[:, SHIFT : SHIFT + width])


def solution(mesh):
    placed = (P("head", "seq"),) * 3 + (P(), P("head"), P("head"))
    return jax.shard_map(
        per_device, mesh=mesh, in_specs=placed, out_specs=P("head", "seq"), check_vma=False
    )
```

```python
import math

import jax
import jax.numpy as jnp
from jax import lax
from jax.experimental import pallas as pl
from jax.experimental.pallas import tpu as pltpu
from jax.sharding import PartitionSpec as P

D = 768
HD = 48
SEG = 1024
LOCAL = 1024
MESH = pl.DeviceIdType.MESH
BRANCHES = ((256, 4), (64, 16), (16, 64))
SHIFT = 64


def to_token_major(x):
    f = x.shape[0]
    x = x.reshape(f, 16, 4, 4, 4)
    x = jnp.transpose(x, (4, 3, 2, 1, 0))
    return x.reshape(LOCAL, f)


def from_token_major(x):
    f = x.shape[1]
    x = x.reshape(4, 4, 4, 16, f)
    x = jnp.transpose(x, (4, 3, 2, 1, 0))
    return x.reshape(f, LOCAL)


def pos_of(device, index):
    local = 64 * (index % 16) + 16 * (index // 16 % 4) + 4 * (index // 64 % 4) + index // 256
    return device * LOCAL + local


def slide_of(positions, slide_ends):
    return jnp.sum((positions[..., None] >= slide_ends).astype(jnp.int32), axis=-1)


def attention_kernel(
    q_ref, kv_ref, s1_ref, s2_ref, s3_ref, sq_ref, sk_ref, gain_ref, bias_ref,
    out_ref,
    kv1, kv2, kv3, m_acc, l_acc, o_acc, stats, ybuf, cols,
    send_sem, recv_sem, local_sem, fwd_send, fwd_recv, y_send, y_recv,
):
    heads = 4
    me = lax.axis_index("seq")
    hy = lax.axis_index("head")
    devices = lax.axis_size("seq")
    scale = 1.0 / math.sqrt(HD)
    sends = (s1_ref, s2_ref, s3_ref)
    bufs = (kv1, kv2, kv3)
    width = heads * HD

    barrier = pltpu.get_barrier_semaphore()

    def greet(o, carry):
        pl.semaphore_signal(barrier, inc=1, device_id=(lax.rem(me + o, devices), hy), device_id_type=MESH)
        return carry

    lax.fori_loop(1, devices, greet, 0)
    ys = lax.axis_size("head")
    for o in range(1, ys):
        pl.semaphore_signal(barrier, inc=1, device_id=(me, lax.rem(hy + o, ys)), device_id_type=MESH)
    pl.semaphore_wait(barrier, devices - 1 + ys - 1)

    def slot(b, half, pair):
        return bufs[b].at[pair, half]

    sibling = me + 1 - 2 * (me % 2)
    side = me % 2
    locals_ = []
    for b, (count, group) in enumerate(BRANCHES):
        member = lax.rem(me, group)
        cp = pltpu.make_async_copy(sends[b], slot(b, side, member // 2), local_sem.at[b])
        cp.start()
        locals_.append(cp)
    for b, (count, group) in enumerate(BRANCHES):
        member = lax.rem(me, group)
        first = me - member
        pairs = group // 2

        def push(o, carry, b=b, pairs=pairs, member=member, first=first):
            target = first + 2 * lax.rem(member // 2 + o, pairs) + side
            pltpu.make_async_remote_copy(
                src_ref=sends[b],
                dst_ref=slot(b, side, member // 2),
                send_sem=send_sem.at[b],
                recv_sem=recv_sem.at[b],
                device_id=(target, hy),
                device_id_type=MESH,
            ).start()
            return carry

        lax.fori_loop(1, pairs, push, 0)

    q_lane = lax.broadcasted_iota(jnp.int32, (1, 256), 1) // HD
    o_lane = (lax.broadcasted_iota(jnp.int32, (1, 256), 1) - SHIFT) // HD

    def attend(q, j, kv, same):
        qz = jnp.where(q_lane == j, q, jnp.zeros_like(q))
        s = lax.dot_general(qz, kv[:, :256], (((1,), (1,)), ((), ())), preferred_element_type=jnp.float32)
        s = jnp.where(same, s, -1e30)
        m = jnp.max(s, axis=-1, keepdims=True)
        p = jnp.exp((s - m) * scale)
        l = jnp.sum(p, axis=-1, keepdims=True)
        o = jnp.dot(p.astype(jnp.bfloat16), kv[:, 128:], preferred_element_type=jnp.float32)
        return m * scale, l, o

    chunk = 256

    def branch0(i, carry):
        rows = pl.ds(pl.multiple_of(i * chunk, chunk), chunk)
        q = q_ref[rows]
        kv = kv_ref[...]
        same = sq_ref[rows] == sk_ref[0]
        mm = ll = oo = None
        for j in range(heads):
            m, l, o = attend(q, j, kv, same)
            if j == 0:
                mm = jnp.broadcast_to(m, (chunk, 256))
                ll = jnp.broadcast_to(l, (chunk, 256))
                oo = o
            else:
                pick = o_lane == j
                mm = jnp.where(pick, m, mm)
                ll = jnp.where(pick, l, ll)
                oo = jnp.where(pick, o, oo)
        m_acc[rows] = mm
        l_acc[rows] = ll
        o_acc[rows] = oo
        return carry

    forwards = []

    def forward(b):
        count, group = BRANCHES[b]
        pairs = group // 2
        locals_[b].wait()
        if pairs > 1:
            got = bufs[b].at[pl.ds(0, pairs - 1), side]
            pltpu.make_async_copy(got, got, recv_sem.at[b]).wait()
        cp = pltpu.make_async_remote_copy(
            src_ref=bufs[b].at[:, side],
            dst_ref=bufs[b].at[:, side],
            send_sem=fwd_send.at[b],
            recv_sem=fwd_recv.at[b],
            device_id=(sibling, hy),
            device_id_type=MESH,
        )
        cp.start()
        forwards.append(cp)

    def later(b):
        count, group = BRANCHES[b]
        other = bufs[b].at[:, 1 - side]
        pltpu.make_async_copy(other, other, fwd_recv.at[b]).wait()

        def branch(j, carry):
            start = j * 256 + (hy * 64 if b >= 1 else 0)
            rows = pl.ds(pl.multiple_of(start, 16), count)
            same = sq_ref[rows] == sk_ref[1 + b * heads + j]
            m_new, l_new, o_new = attend(q_ref[rows], j, bufs[b][...].reshape(LOCAL, 2 * width), same)
            m_old = m_acc[rows]
            mn = jnp.maximum(m_old, m_new)
            keep_old = jnp.exp(m_old - mn)
            keep_new = jnp.exp(m_new - mn)
            pick = o_lane == j
            m_acc[rows] = jnp.where(pick, mn, m_old)
            l_acc[rows] = jnp.where(pick, l_acc[rows] * keep_old + l_new * keep_new, l_acc[rows])
            o_acc[rows] = jnp.where(pick, o_acc[rows] * keep_old + o_new * keep_new, o_acc[rows])
            return carry

        lax.fori_loop(0, heads, branch, 0)

    lax.fori_loop(0, 2, branch0, 0)
    forward(0)
    lax.fori_loop(2, LOCAL // chunk, branch0, 0)
    forward(1)
    later(0)
    forward(2)
    later(1)
    later(2)

    feature = lax.broadcasted_iota(jnp.int32, (8, 256), 1) >= SHIFT
    ones = jnp.where(feature, 1.0, 0.0).astype(jnp.float32)
    first_row = lax.broadcasted_iota(jnp.int32, (8, chunk), 0) == 0

    def finish(i, carry):
        rows = pl.ds(pl.multiple_of(i * chunk, chunk), chunk)
        att = o_acc[rows] / l_acc[rows]
        o_acc[rows] = att
        dims = (((1,), (1,)), ((), ()))
        total = lax.dot_general(ones, att, dims, precision=lax.Precision.HIGHEST, preferred_element_type=jnp.float32)
        square = lax.dot_general(ones, att * att, dims, precision=lax.Precision.HIGHEST, preferred_element_type=jnp.float32)
        stats[:, rows] = jnp.where(first_row, total, square)
        return carry

    lax.fori_loop(0, LOCAL // chunk, finish, 0)
    ybuf[hy] = stats[...]
    shares = []
    for o in range(1, ys):
        cp = pltpu.make_async_remote_copy(
            src_ref=stats,
            dst_ref=ybuf.at[hy],
            send_sem=y_send.at[o - 1],
            recv_sem=y_recv.at[0],
            device_id=(me, lax.rem(hy + o, ys)),
            device_id_type=MESH,
        )
        cp.start()
        shares.append(cp)
    arrived = ybuf.at[pl.ds(0, ys - 1)]
    pltpu.make_async_copy(arrived, arrived, y_recv.at[0]).wait()
    for cp in shares:
        cp.wait_send()
    summed = ybuf[0]
    for h in range(1, ys):
        summed = summed + ybuf[h]
    mean = summed[0:1] / D
    var = summed[1:2] / D - mean * mean
    rstd = lax.rsqrt(var + 1e-05)
    pair = jnp.where(lax.broadcasted_iota(jnp.int32, (8, LOCAL), 0) == 0, mean, rstd)
    cols[...] = jnp.transpose(pair)

    def normalize(i, carry):
        rows = pl.ds(pl.multiple_of(i * chunk, chunk), chunk)
        col = cols[rows]
        normed = (o_acc[rows] - col[:, 0:1]) * col[:, 1:2]
        out_ref[rows] = (normed * gain_ref[...] + bias_ref[...]).astype(out_ref.dtype)
        return carry

    lax.fori_loop(0, LOCAL // chunk, normalize, 0)

    for b, (count, group) in enumerate(BRANCHES):
        pairs = group // 2
        if pairs > 1:
            went = bufs[b].at[pl.ds(0, pairs - 1), side]
            pltpu.make_async_copy(went, went, send_sem.at[b]).wait()
        forwards[b].wait_send()


def per_device(queries, keys, values, slide_lengths, norm_gain, norm_bias):
    heads = queries.shape[0] // HD
    width = heads * HD
    seq = lax.axis_index("seq")
    hy = lax.axis_index("head")
    slide_ends = jnp.cumsum(slide_lengths)
    q = to_token_major(jnp.concatenate([queries, jnp.zeros((256 - width, LOCAL), queries.dtype)]))
    kv = to_token_major(jnp.concatenate([keys, values]))
    kv_lane = jnp.arange(2 * width) % width // HD

    positions = [pos_of(seq, jnp.arange(LOCAL))]
    sends = []
    for b, (count, group) in enumerate(BRANCHES):
        starts = [j * 256 + (hy * 64 if b >= 1 else 0) for j in range(heads)]
        chunk = jnp.zeros((count, 2 * width), kv.dtype)
        for j in range(heads):
            piece = lax.dynamic_slice_in_dim(kv, starts[j], count, 0)
            chunk = jnp.where(kv_lane[None, :] == j, piece, chunk)
        sends.append(chunk)
        first = seq // group * group
        members = first + jnp.arange(group)
        for j in range(heads):
            idx = starts[j] + jnp.arange(count)
            positions.append(pos_of(members[:, None], idx[None, :]).reshape(group * count))
    slides = slide_of(jnp.stack(positions), slide_ends)

    lead = jnp.zeros((SHIFT,), jnp.float32)
    gain = jnp.concatenate([lead, norm_gain]).reshape(1, 256)
    bias = jnp.concatenate([lead, norm_bias]).reshape(1, 256)
    vmem = pl.BlockSpec(memory_space=pltpu.VMEM)
    out = pl.pallas_call(
        attention_kernel,
        out_shape=jax.ShapeDtypeStruct((LOCAL, 256), jnp.bfloat16),
        in_specs=[vmem] * 9,
        out_specs=vmem,
        scratch_shapes=[
            *[pltpu.VMEM((group // 2, 2, count, 2 * width), jnp.bfloat16) for count, group in BRANCHES],
            pltpu.VMEM((LOCAL, 256), jnp.float32),
            pltpu.VMEM((LOCAL, 256), jnp.float32),
            pltpu.VMEM((LOCAL, 256), jnp.float32),
            pltpu.VMEM((8, LOCAL), jnp.float32),
            pltpu.VMEM((4, 8, LOCAL), jnp.float32),
            pltpu.VMEM((LOCAL, 8), jnp.float32),
            pltpu.SemaphoreType.DMA((3,)),
            pltpu.SemaphoreType.DMA((3,)),
            pltpu.SemaphoreType.DMA((3,)),
            pltpu.SemaphoreType.DMA((3,)),
            pltpu.SemaphoreType.DMA((3,)),
            pltpu.SemaphoreType.DMA((3,)),
            pltpu.SemaphoreType.DMA((1,)),
        ],
        compiler_params=pltpu.CompilerParams(
            collective_id=0, has_side_effects=True, vmem_limit_bytes=60 * 1024 * 1024
        ),
    )(q, kv, *sends, slides[0].reshape(LOCAL, 1), slides.reshape(-1, 1, LOCAL), gain, bias)
    return from_token_major(out[:, SHIFT : SHIFT + width])


def solution(mesh):
    placed = (P("head", "seq"),) * 3 + (P(), P("head"), P("head"))
    return jax.shard_map(
        per_device, mesh=mesh, in_specs=placed, out_specs=P("head", "seq"), check_vma=False
    )
```

```python
import math

import jax
import jax.numpy as jnp
from jax import lax
from jax.experimental import pallas as pl
from jax.experimental.pallas import tpu as pltpu
from jax.sharding import PartitionSpec as P

D = 768
HD = 48
SEG = 1024
LOCAL = 1024
MESH = pl.DeviceIdType.MESH
BRANCHES = ((256, 4), (64, 16), (16, 64))
SHIFT = 64


def to_token_major(x):
    f = x.shape[0]
    x = x.reshape(f, 16, 4, 4, 4)
    x = jnp.transpose(x, (4, 3, 2, 1, 0))
    return x.reshape(LOCAL, f)


def from_token_major(x):
    f = x.shape[1]
    x = x.reshape(4, 4, 4, 16, f)
    x = jnp.transpose(x, (4, 3, 2, 1, 0))
    return x.reshape(f, LOCAL)


def pos_of(device, index):
    local = 64 * (index % 16) + 16 * (index // 16 % 4) + 4 * (index // 64 % 4) + index // 256
    return device * LOCAL + local


def slide_of(positions, slide_ends):
    return jnp.sum((positions[..., None] >= slide_ends).astype(jnp.int32), axis=-1)


def attention_kernel(
    q_ref, kv_ref, s1_ref, s2_ref, s3_ref, sq_ref, sk_ref, gain_ref, bias_ref,
    out_ref,
    kv1, kv2, kv3, m_acc, l_acc, o_acc, stats, ybuf, cols,
    send_sem, recv_sem, local_sem, fwd_send, fwd_recv, y_send, y_recv,
):
    heads = 4
    me = lax.axis_index("seq")
    hy = lax.axis_index("head")
    devices = lax.axis_size("seq")
    scale = 1.0 / math.sqrt(HD)
    sends = (s1_ref, s2_ref, s3_ref)
    bufs = (kv1, kv2, kv3)
    width = heads * HD

    ys = lax.axis_size("head")

    def slot(b, half, pair):
        return bufs[b].at[pair, half]

    sibling = me + 1 - 2 * (me % 2)
    side = me % 2
    locals_ = []
    for b, (count, group) in enumerate(BRANCHES):
        member = lax.rem(me, group)
        cp = pltpu.make_async_copy(sends[b], slot(b, side, member // 2), local_sem.at[b])
        cp.start()
        locals_.append(cp)
    for b, (count, group) in enumerate(BRANCHES):
        member = lax.rem(me, group)
        first = me - member
        pairs = group // 2

        def push(o, carry, b=b, pairs=pairs, member=member, first=first):
            target = first + 2 * lax.rem(member // 2 + o, pairs) + side
            pltpu.make_async_remote_copy(
                src_ref=sends[b],
                dst_ref=slot(b, side, member // 2),
                send_sem=send_sem.at[b],
                recv_sem=recv_sem.at[b],
                device_id=(target, hy),
                device_id_type=MESH,
            ).start()
            return carry

        lax.fori_loop(1, pairs, push, 0)

    q_lane = lax.broadcasted_iota(jnp.int32, (1, 256), 1) // HD
    o_lane = (lax.broadcasted_iota(jnp.int32, (1, 256), 1) - SHIFT) // HD

    def attend(q, j, kv, same):
        qz = jnp.where(q_lane == j, q, jnp.zeros_like(q))
        s = lax.dot_general(qz, kv[:, :256], (((1,), (1,)), ((), ())), preferred_element_type=jnp.float32)
        s = jnp.where(same, s, -1e30)
        m = jnp.max(s, axis=-1, keepdims=True)
        p = jnp.exp((s - m) * scale)
        l = jnp.sum(p, axis=-1, keepdims=True)
        o = jnp.dot(p.astype(jnp.bfloat16), kv[:, 128:], preferred_element_type=jnp.float32)
        return m * scale, l, o

    chunk = 256

    def branch0(i, carry):
        rows = pl.ds(pl.multiple_of(i * chunk, chunk), chunk)
        q = q_ref[rows]
        kv = kv_ref[...]
        same = sq_ref[rows] == sk_ref[0]
        mm = ll = oo = None
        for j in range(heads):
            m, l, o = attend(q, j, kv, same)
            if j == 0:
                mm = jnp.broadcast_to(m, (chunk, 256))
                ll = jnp.broadcast_to(l, (chunk, 256))
                oo = o
            else:
                pick = o_lane == j
                mm = jnp.where(pick, m, mm)
                ll = jnp.where(pick, l, ll)
                oo = jnp.where(pick, o, oo)
        m_acc[rows] = mm
        l_acc[rows] = ll
        o_acc[rows] = oo
        return carry

    forwards = []

    def forward(b):
        count, group = BRANCHES[b]
        pairs = group // 2
        locals_[b].wait()
        if pairs > 1:
            got = bufs[b].at[pl.ds(0, pairs - 1), side]
            pltpu.make_async_copy(got, got, recv_sem.at[b]).wait()
        cp = pltpu.make_async_remote_copy(
            src_ref=bufs[b].at[:, side],
            dst_ref=bufs[b].at[:, side],
            send_sem=fwd_send.at[b],
            recv_sem=fwd_recv.at[b],
            device_id=(sibling, hy),
            device_id_type=MESH,
        )
        cp.start()
        forwards.append(cp)

    def later(b):
        count, group = BRANCHES[b]
        other = bufs[b].at[:, 1 - side]
        pltpu.make_async_copy(other, other, fwd_recv.at[b]).wait()

        def branch(j, carry):
            start = j * 256 + (hy * 64 if b >= 1 else 0)
            rows = pl.ds(pl.multiple_of(start, 16), count)
            same = sq_ref[rows] == sk_ref[1 + b * heads + j]
            m_new, l_new, o_new = attend(q_ref[rows], j, bufs[b][...].reshape(LOCAL, 2 * width), same)
            m_old = m_acc[rows]
            mn = jnp.maximum(m_old, m_new)
            keep_old = jnp.exp(m_old - mn)
            keep_new = jnp.exp(m_new - mn)
            pick = o_lane == j
            m_acc[rows] = jnp.where(pick, mn, m_old)
            l_acc[rows] = jnp.where(pick, l_acc[rows] * keep_old + l_new * keep_new, l_acc[rows])
            o_acc[rows] = jnp.where(pick, o_acc[rows] * keep_old + o_new * keep_new, o_acc[rows])
            return carry

        lax.fori_loop(0, heads, branch, 0)

    lax.fori_loop(0, 2, branch0, 0)
    forward(0)
    lax.fori_loop(2, LOCAL // chunk, branch0, 0)
    forward(1)
    later(0)
    forward(2)
    later(1)
    later(2)

    feature = lax.broadcasted_iota(jnp.int32, (8, 256), 1) >= SHIFT
    ones = jnp.where(feature, 1.0, 0.0).astype(jnp.float32)
    first_row = lax.broadcasted_iota(jnp.int32, (8, chunk), 0) == 0

    def finish(i, carry):
        rows = pl.ds(pl.multiple_of(i * chunk, chunk), chunk)
        att = o_acc[rows] / l_acc[rows]
        o_acc[rows] = att
        dims = (((1,), (1,)), ((), ()))
        total = lax.dot_general(ones, att, dims, precision=lax.Precision.HIGHEST, preferred_element_type=jnp.float32)
        square = lax.dot_general(ones, att * att, dims, precision=lax.Precision.HIGHEST, preferred_element_type=jnp.float32)
        stats[:, rows] = jnp.where(first_row, total, square)
        return carry

    lax.fori_loop(0, LOCAL // chunk, finish, 0)
    ybuf[hy] = stats[...]
    shares = []
    for o in range(1, ys):
        cp = pltpu.make_async_remote_copy(
            src_ref=stats,
            dst_ref=ybuf.at[hy],
            send_sem=y_send.at[o - 1],
            recv_sem=y_recv.at[0],
            device_id=(me, lax.rem(hy + o, ys)),
            device_id_type=MESH,
        )
        cp.start()
        shares.append(cp)
    arrived = ybuf.at[pl.ds(0, ys - 1)]
    pltpu.make_async_copy(arrived, arrived, y_recv.at[0]).wait()
    for cp in shares:
        cp.wait_send()
    summed = ybuf[0]
    for h in range(1, ys):
        summed = summed + ybuf[h]
    mean = summed[0:1] / D
    var = summed[1:2] / D - mean * mean
    rstd = lax.rsqrt(var + 1e-05)
    pair = jnp.where(lax.broadcasted_iota(jnp.int32, (8, LOCAL), 0) == 0, mean, rstd)
    cols[...] = jnp.transpose(pair)

    def normalize(i, carry):
        rows = pl.ds(pl.multiple_of(i * chunk, chunk), chunk)
        col = cols[rows]
        normed = (o_acc[rows] - col[:, 0:1]) * col[:, 1:2]
        out_ref[rows] = (normed * gain_ref[...] + bias_ref[...]).astype(out_ref.dtype)
        return carry

    lax.fori_loop(0, LOCAL // chunk, normalize, 0)

    for b, (count, group) in enumerate(BRANCHES):
        pairs = group // 2
        if pairs > 1:
            went = bufs[b].at[pl.ds(0, pairs - 1), side]
            pltpu.make_async_copy(went, went, send_sem.at[b]).wait()
        forwards[b].wait_send()


def per_device(queries, keys, values, slide_lengths, norm_gain, norm_bias):
    heads = queries.shape[0] // HD
    width = heads * HD
    seq = lax.axis_index("seq")
    hy = lax.axis_index("head")
    slide_ends = jnp.cumsum(slide_lengths)
    q = to_token_major(jnp.concatenate([queries, jnp.zeros((256 - width, LOCAL), queries.dtype)]))
    kv = to_token_major(jnp.concatenate([keys, values]))
    kv_lane = jnp.arange(2 * width) % width // HD

    positions = [pos_of(seq, jnp.arange(LOCAL))]
    sends = []
    for b, (count, group) in enumerate(BRANCHES):
        starts = [j * 256 + (hy * 64 if b >= 1 else 0) for j in range(heads)]
        chunk = jnp.zeros((count, 2 * width), kv.dtype)
        for j in range(heads):
            piece = lax.dynamic_slice_in_dim(kv, starts[j], count, 0)
            chunk = jnp.where(kv_lane[None, :] == j, piece, chunk)
        sends.append(chunk)
        first = seq // group * group
        members = first + jnp.arange(group)
        for j in range(heads):
            idx = starts[j] + jnp.arange(count)
            positions.append(pos_of(members[:, None], idx[None, :]).reshape(group * count))
    slides = slide_of(jnp.stack(positions), slide_ends)

    lead = jnp.zeros((SHIFT,), jnp.float32)
    gain = jnp.concatenate([lead, norm_gain]).reshape(1, 256)
    bias = jnp.concatenate([lead, norm_bias]).reshape(1, 256)
    vmem = pl.BlockSpec(memory_space=pltpu.VMEM)
    out = pl.pallas_call(
        attention_kernel,
        out_shape=jax.ShapeDtypeStruct((LOCAL, 256), jnp.bfloat16),
        in_specs=[vmem] * 9,
        out_specs=vmem,
        scratch_shapes=[
            *[pltpu.VMEM((group // 2, 2, count, 2 * width), jnp.bfloat16) for count, group in BRANCHES],
            pltpu.VMEM((LOCAL, 256), jnp.float32),
            pltpu.VMEM((LOCAL, 256), jnp.float32),
            pltpu.VMEM((LOCAL, 256), jnp.float32),
            pltpu.VMEM((8, LOCAL), jnp.float32),
            pltpu.VMEM((4, 8, LOCAL), jnp.float32),
            pltpu.VMEM((LOCAL, 8), jnp.float32),
            pltpu.SemaphoreType.DMA((3,)),
            pltpu.SemaphoreType.DMA((3,)),
            pltpu.SemaphoreType.DMA((3,)),
            pltpu.SemaphoreType.DMA((3,)),
            pltpu.SemaphoreType.DMA((3,)),
            pltpu.SemaphoreType.DMA((3,)),
            pltpu.SemaphoreType.DMA((1,)),
        ],
        compiler_params=pltpu.CompilerParams(
            has_side_effects=True, vmem_limit_bytes=60 * 1024 * 1024
        ),
    )(q, kv, *sends, slides[0].reshape(LOCAL, 1), slides.reshape(-1, 1, LOCAL), gain, bias)
    return from_token_major(out[:, SHIFT : SHIFT + width])


def solution(mesh):
    placed = (P("head", "seq"),) * 3 + (P(), P("head"), P("head"))
    return jax.shard_map(
        per_device, mesh=mesh, in_specs=placed, out_specs=P("head", "seq"), check_vma=False
    )
```

```python
import math

import jax
import jax.numpy as jnp
from jax import lax
from jax.experimental import pallas as pl
from jax.experimental.pallas import tpu as pltpu
from jax.sharding import PartitionSpec as P

D = 768
HD = 48
SEG = 1024
LOCAL = 1024
MESH = pl.DeviceIdType.MESH
BRANCHES = ((256, 4), (64, 16), (16, 64))
SHIFT = 64


def to_token_major(x):
    f = x.shape[0]
    x = x.reshape(f, 16, 4, 4, 4)
    x = jnp.transpose(x, (4, 3, 2, 1, 0))
    return x.reshape(LOCAL, f)


def from_token_major(x):
    f = x.shape[1]
    x = x.reshape(4, 4, 4, 16, f)
    x = jnp.transpose(x, (4, 3, 2, 1, 0))
    return x.reshape(f, LOCAL)


def pos_of(device, index):
    local = 64 * (index % 16) + 16 * (index // 16 % 4) + 4 * (index // 64 % 4) + index // 256
    return device * LOCAL + local


def slide_of(positions, slide_ends):
    return jnp.sum((positions[..., None] >= slide_ends).astype(jnp.int32), axis=-1)


def attention_kernel(
    q_ref, kv_ref, s1_ref, s2_ref, s3_ref, sq_ref, sk_ref, gain_ref, bias_ref,
    out_ref,
    kv1, kv2, kv3, m_acc, l_acc, o_acc, stats, ybuf, cols,
    send_sem, recv_sem, local_sem, fwd_send, fwd_recv, y_send, y_recv,
):
    heads = 4
    me = lax.axis_index("seq")
    hy = lax.axis_index("head")
    devices = lax.axis_size("seq")
    scale = 1.0 / math.sqrt(HD)
    sends = (s1_ref, s2_ref, s3_ref)
    bufs = (kv1, kv2, kv3)
    width = heads * HD

    barrier = pltpu.get_barrier_semaphore()

    side = me % 2
    halves = devices // 2

    def greet(o, carry):
        peer = 2 * lax.rem(me // 2 + o, halves) + side
        pl.semaphore_signal(barrier, inc=1, device_id=(peer, hy), device_id_type=MESH)
        return carry

    lax.fori_loop(1, halves, greet, 0)
    pl.semaphore_signal(barrier, inc=1, device_id=(me + 1 - 2 * side, hy), device_id_type=MESH)
    ys = lax.axis_size("head")
    for o in range(1, ys):
        pl.semaphore_signal(barrier, inc=1, device_id=(me, lax.rem(hy + o, ys)), device_id_type=MESH)

    def slot(b, half, pair):
        return bufs[b].at[pair, half]

    sibling = me + 1 - 2 * (me % 2)
    locals_ = []
    for b, (count, group) in enumerate(BRANCHES):
        member = lax.rem(me, group)
        cp = pltpu.make_async_copy(sends[b], slot(b, side, member // 2), local_sem.at[b])
        cp.start()
        locals_.append(cp)
    def start_pushes():
        for b, (count, group) in enumerate(BRANCHES):
            member = lax.rem(me, group)
            first = me - member
            pairs = group // 2

            def push(o, carry, b=b, pairs=pairs, member=member, first=first):
                target = first + 2 * lax.rem(member // 2 + o, pairs) + side
                pltpu.make_async_remote_copy(
                    src_ref=sends[b],
                    dst_ref=slot(b, side, member // 2),
                    send_sem=send_sem.at[b],
                    recv_sem=recv_sem.at[b],
                    device_id=(target, hy),
                    device_id_type=MESH,
                ).start()
                return carry

            lax.fori_loop(1, pairs, push, 0)


    q_lane = lax.broadcasted_iota(jnp.int32, (1, 256), 1) // HD
    o_lane = (lax.broadcasted_iota(jnp.int32, (1, 256), 1) - SHIFT) // HD

    def attend(q, j, kv, same):
        qz = jnp.where(q_lane == j, q, jnp.zeros_like(q))
        s = lax.dot_general(qz, kv[:, :256], (((1,), (1,)), ((), ())), preferred_element_type=jnp.float32)
        s = jnp.where(same, s, -1e30)
        m = jnp.max(s, axis=-1, keepdims=True)
        p = jnp.exp((s - m) * scale)
        l = jnp.sum(p, axis=-1, keepdims=True)
        o = jnp.dot(p.astype(jnp.bfloat16), kv[:, 128:], preferred_element_type=jnp.float32)
        return m * scale, l, o

    chunk = 256

    def branch0(i, carry):
        rows = pl.ds(pl.multiple_of(i * chunk, chunk), chunk)
        q = q_ref[rows]
        kv = kv_ref[...]
        same = sq_ref[rows] == sk_ref[0]
        mm = ll = oo = None
        for j in range(heads):
            m, l, o = attend(q, j, kv, same)
            if j == 0:
                mm = jnp.broadcast_to(m, (chunk, 256))
                ll = jnp.broadcast_to(l, (chunk, 256))
                oo = o
            else:
                pick = o_lane == j
                mm = jnp.where(pick, m, mm)
                ll = jnp.where(pick, l, ll)
                oo = jnp.where(pick, o, oo)
        m_acc[rows] = mm
        l_acc[rows] = ll
        o_acc[rows] = oo
        return carry

    forwards = []

    def forward(b):
        count, group = BRANCHES[b]
        pairs = group // 2
        locals_[b].wait()
        if pairs > 1:
            got = bufs[b].at[pl.ds(0, pairs - 1), side]
            pltpu.make_async_copy(got, got, recv_sem.at[b]).wait()
        cp = pltpu.make_async_remote_copy(
            src_ref=bufs[b].at[:, side],
            dst_ref=bufs[b].at[:, side],
            send_sem=fwd_send.at[b],
            recv_sem=fwd_recv.at[b],
            device_id=(sibling, hy),
            device_id_type=MESH,
        )
        cp.start()
        forwards.append(cp)

    def later(b):
        count, group = BRANCHES[b]
        other = bufs[b].at[:, 1 - side]
        pltpu.make_async_copy(other, other, fwd_recv.at[b]).wait()

        def branch(j, carry):
            start = j * 256 + (hy * 64 if b >= 1 else 0)
            rows = pl.ds(pl.multiple_of(start, 16), count)
            same = sq_ref[rows] == sk_ref[1 + b * heads + j]
            m_new, l_new, o_new = attend(q_ref[rows], j, bufs[b][...].reshape(LOCAL, 2 * width), same)
            m_old = m_acc[rows]
            mn = jnp.maximum(m_old, m_new)
            keep_old = jnp.exp(m_old - mn)
            keep_new = jnp.exp(m_new - mn)
            pick = o_lane == j
            m_acc[rows] = jnp.where(pick, mn, m_old)
            l_acc[rows] = jnp.where(pick, l_acc[rows] * keep_old + l_new * keep_new, l_acc[rows])
            o_acc[rows] = jnp.where(pick, o_acc[rows] * keep_old + o_new * keep_new, o_acc[rows])
            return carry

        lax.fori_loop(0, heads, branch, 0)

    lax.fori_loop(0, 1, branch0, 0)
    pl.semaphore_wait(barrier, halves + ys - 1)
    start_pushes()
    lax.fori_loop(1, 3, branch0, 0)
    forward(0)
    lax.fori_loop(3, LOCAL // chunk, branch0, 0)
    forward(1)
    later(0)
    forward(2)
    later(1)
    later(2)

    feature = lax.broadcasted_iota(jnp.int32, (8, 256), 1) >= SHIFT
    ones = jnp.where(feature, 1.0, 0.0).astype(jnp.float32)
    first_row = lax.broadcasted_iota(jnp.int32, (8, chunk), 0) == 0

    def finish(i, carry):
        rows = pl.ds(pl.multiple_of(i * chunk, chunk), chunk)
        att = o_acc[rows] / l_acc[rows]
        o_acc[rows] = att
        dims = (((1,), (1,)), ((), ()))
        total = lax.dot_general(ones, att, dims, precision=lax.Precision.HIGHEST, preferred_element_type=jnp.float32)
        square = lax.dot_general(ones, att * att, dims, precision=lax.Precision.HIGHEST, preferred_element_type=jnp.float32)
        stats[:, rows] = jnp.where(first_row, total, square)
        return carry

    lax.fori_loop(0, LOCAL // chunk, finish, 0)
    ybuf[hy] = stats[...]
    shares = []
    for o in range(1, ys):
        cp = pltpu.make_async_remote_copy(
            src_ref=stats,
            dst_ref=ybuf.at[hy],
            send_sem=y_send.at[o - 1],
            recv_sem=y_recv.at[0],
            device_id=(me, lax.rem(hy + o, ys)),
            device_id_type=MESH,
        )
        cp.start()
        shares.append(cp)
    arrived = ybuf.at[pl.ds(0, ys - 1)]
    pltpu.make_async_copy(arrived, arrived, y_recv.at[0]).wait()
    for cp in shares:
        cp.wait_send()
    summed = ybuf[0]
    for h in range(1, ys):
        summed = summed + ybuf[h]
    mean = summed[0:1] / D
    var = summed[1:2] / D - mean * mean
    rstd = lax.rsqrt(var + 1e-05)
    pair = jnp.where(lax.broadcasted_iota(jnp.int32, (8, LOCAL), 0) == 0, mean, rstd)
    cols[...] = jnp.transpose(pair)

    def normalize(i, carry):
        rows = pl.ds(pl.multiple_of(i * chunk, chunk), chunk)
        col = cols[rows]
        normed = (o_acc[rows] - col[:, 0:1]) * col[:, 1:2]
        out_ref[rows] = (normed * gain_ref[...] + bias_ref[...]).astype(out_ref.dtype)
        return carry

    lax.fori_loop(0, LOCAL // chunk, normalize, 0)

    for b, (count, group) in enumerate(BRANCHES):
        pairs = group // 2
        if pairs > 1:
            went = bufs[b].at[pl.ds(0, pairs - 1), side]
            pltpu.make_async_copy(went, went, send_sem.at[b]).wait()
        forwards[b].wait_send()


def per_device(queries, keys, values, slide_lengths, norm_gain, norm_bias):
    heads = queries.shape[0] // HD
    width = heads * HD
    seq = lax.axis_index("seq")
    hy = lax.axis_index("head")
    slide_ends = jnp.cumsum(slide_lengths)
    q = to_token_major(jnp.concatenate([queries, jnp.zeros((256 - width, LOCAL), queries.dtype)]))
    kv = to_token_major(jnp.concatenate([keys, values]))
    kv_lane = jnp.arange(2 * width) % width // HD

    positions = [pos_of(seq, jnp.arange(LOCAL))]
    sends = []
    for b, (count, group) in enumerate(BRANCHES):
        starts = [j * 256 + (hy * 64 if b >= 1 else 0) for j in range(heads)]
        chunk = jnp.zeros((count, 2 * width), kv.dtype)
        for j in range(heads):
            piece = lax.dynamic_slice_in_dim(kv, starts[j], count, 0)
            chunk = jnp.where(kv_lane[None, :] == j, piece, chunk)
        sends.append(chunk)
        first = seq // group * group
        members = first + jnp.arange(group)
        for j in range(heads):
            idx = starts[j] + jnp.arange(count)
            positions.append(pos_of(members[:, None], idx[None, :]).reshape(group * count))
    slides = slide_of(jnp.stack(positions), slide_ends)

    lead = jnp.zeros((SHIFT,), jnp.float32)
    gain = jnp.concatenate([lead, norm_gain]).reshape(1, 256)
    bias = jnp.concatenate([lead, norm_bias]).reshape(1, 256)
    vmem = pl.BlockSpec(memory_space=pltpu.VMEM)
    out = pl.pallas_call(
        attention_kernel,
        out_shape=jax.ShapeDtypeStruct((LOCAL, 256), jnp.bfloat16),
        in_specs=[vmem] * 9,
        out_specs=vmem,
        scratch_shapes=[
            *[pltpu.VMEM((group // 2, 2, count, 2 * width), jnp.bfloat16) for count, group in BRANCHES],
            pltpu.VMEM((LOCAL, 256), jnp.float32),
            pltpu.VMEM((LOCAL, 256), jnp.float32),
            pltpu.VMEM((LOCAL, 256), jnp.float32),
            pltpu.VMEM((8, LOCAL), jnp.float32),
            pltpu.VMEM((4, 8, LOCAL), jnp.float32),
            pltpu.VMEM((LOCAL, 8), jnp.float32),
            pltpu.SemaphoreType.DMA((3,)),
            pltpu.SemaphoreType.DMA((3,)),
            pltpu.SemaphoreType.DMA((3,)),
            pltpu.SemaphoreType.DMA((3,)),
            pltpu.SemaphoreType.DMA((3,)),
            pltpu.SemaphoreType.DMA((3,)),
            pltpu.SemaphoreType.DMA((1,)),
        ],
        compiler_params=pltpu.CompilerParams(
            collective_id=0, has_side_effects=True, vmem_limit_bytes=60 * 1024 * 1024
        ),
    )(q, kv, *sends, slides[0].reshape(LOCAL, 1), slides.reshape(-1, 1, LOCAL), gain, bias)
    return from_token_major(out[:, SHIFT : SHIFT + width])


def solution(mesh):
    placed = (P("head", "seq"),) * 3 + (P(), P("head"), P("head"))
    return jax.shard_map(
        per_device, mesh=mesh, in_specs=placed, out_specs=P("head", "seq"), check_vma=False
    )
```

```python
import math

import jax
import jax.numpy as jnp
from jax import lax
from jax.experimental import pallas as pl
from jax.experimental.pallas import tpu as pltpu
from jax.sharding import PartitionSpec as P

D = 768
HD = 48
SEG = 1024
LOCAL = 1024
MESH = pl.DeviceIdType.MESH
BRANCHES = ((256, 4), (64, 16), (16, 64))
SHIFT = 64


def to_token_major(x):
    f = x.shape[0]
    x = x.reshape(f, 16, 4, 4, 4)
    x = jnp.transpose(x, (4, 3, 2, 1, 0))
    return x.reshape(LOCAL, f)


def from_token_major(x):
    f = x.shape[1]
    x = x.reshape(4, 4, 4, 16, f)
    x = jnp.transpose(x, (4, 3, 2, 1, 0))
    return x.reshape(f, LOCAL)


def pos_of(device, index):
    local = 64 * (index % 16) + 16 * (index // 16 % 4) + 4 * (index // 64 % 4) + index // 256
    return device * LOCAL + local


def slide_of(positions, slide_ends):
    return jnp.sum((positions[..., None] >= slide_ends).astype(jnp.int32), axis=-1)


def attention_kernel(
    q_ref, kv_ref, s1_ref, s2_ref, s3_ref, sk_ref, gain_ref, bias_ref,
    out_ref,
    kv1, kv2, kv3, m_acc, l_acc, o_acc, stats, ybuf, cols, sqcol,
    send_sem, recv_sem, local_sem, fwd_send, fwd_recv, y_send, y_recv,
):
    heads = 4
    me = lax.axis_index("seq")
    hy = lax.axis_index("head")
    devices = lax.axis_size("seq")
    scale = 1.0 / math.sqrt(HD)
    sends = (s1_ref, s2_ref, s3_ref)
    sqcol[...] = jnp.transpose(sk_ref[pl.ds(0, 8), :])
    bufs = (kv1, kv2, kv3)
    width = heads * HD

    barrier = pltpu.get_barrier_semaphore()

    side = me % 2
    halves = devices // 2

    def greet(o, carry):
        peer = 2 * lax.rem(me // 2 + o, halves) + side
        pl.semaphore_signal(barrier, inc=1, device_id=(peer, hy), device_id_type=MESH)
        return carry

    lax.fori_loop(1, halves, greet, 0)
    pl.semaphore_signal(barrier, inc=1, device_id=(me + 1 - 2 * side, hy), device_id_type=MESH)
    ys = lax.axis_size("head")
    for o in range(1, ys):
        pl.semaphore_signal(barrier, inc=1, device_id=(me, lax.rem(hy + o, ys)), device_id_type=MESH)

    def slot(b, half, pair):
        return bufs[b].at[pair, half]

    sibling = me + 1 - 2 * (me % 2)
    locals_ = []
    for b, (count, group) in enumerate(BRANCHES):
        member = lax.rem(me, group)
        cp = pltpu.make_async_copy(sends[b], slot(b, side, member // 2), local_sem.at[b])
        cp.start()
        locals_.append(cp)
    def start_pushes():
        for b, (count, group) in enumerate(BRANCHES):
            member = lax.rem(me, group)
            first = me - member
            pairs = group // 2

            def push(o, carry, b=b, pairs=pairs, member=member, first=first):
                target = first + 2 * lax.rem(member // 2 + o, pairs) + side
                pltpu.make_async_remote_copy(
                    src_ref=sends[b],
                    dst_ref=slot(b, side, member // 2),
                    send_sem=send_sem.at[b],
                    recv_sem=recv_sem.at[b],
                    device_id=(target, hy),
                    device_id_type=MESH,
                ).start()
                return carry

            lax.fori_loop(1, pairs, push, 0)


    q_lane = (lax.broadcasted_iota(jnp.int32, (1, 256), 1) - SHIFT) // HD
    o_lane = lax.broadcasted_iota(jnp.int32, (1, 256), 1) // HD

    def attend(q, j, kv, same):
        qz = jnp.where(q_lane == j, q, jnp.zeros_like(q))
        s = lax.dot_general(qz, kv[:, 128:], (((1,), (1,)), ((), ())), preferred_element_type=jnp.float32)
        s = jnp.where(same, s, -1e30)
        m = jnp.max(s, axis=-1, keepdims=True)
        p = jnp.exp((s - m) * scale)
        l = jnp.sum(p, axis=-1, keepdims=True)
        o = jnp.dot(p.astype(jnp.bfloat16), kv[:, :256], preferred_element_type=jnp.float32)
        return m * scale, l, o

    chunk = 256

    def branch0(i, carry):
        rows = pl.ds(pl.multiple_of(i * chunk, chunk), chunk)
        q = q_ref[rows]
        kv = kv_ref[...]
        same = sqcol[rows, 0:1] == sk_ref[pl.ds(0, 1), :]
        mm = ll = oo = None
        for j in range(heads):
            m, l, o = attend(q, j, kv, same)
            if j == 0:
                mm = jnp.broadcast_to(m, (chunk, 256))
                ll = jnp.broadcast_to(l, (chunk, 256))
                oo = o
            else:
                pick = o_lane == j
                mm = jnp.where(pick, m, mm)
                ll = jnp.where(pick, l, ll)
                oo = jnp.where(pick, o, oo)
        m_acc[rows] = mm
        l_acc[rows] = ll
        o_acc[rows] = oo
        return carry

    forwards = []

    def forward(b):
        count, group = BRANCHES[b]
        pairs = group // 2
        locals_[b].wait()
        if pairs > 1:
            got = bufs[b].at[pl.ds(0, pairs - 1), side]
            pltpu.make_async_copy(got, got, recv_sem.at[b]).wait()
        cp = pltpu.make_async_remote_copy(
            src_ref=bufs[b].at[:, side],
            dst_ref=bufs[b].at[:, side],
            send_sem=fwd_send.at[b],
            recv_sem=fwd_recv.at[b],
            device_id=(sibling, hy),
            device_id_type=MESH,
        )
        cp.start()
        forwards.append(cp)

    def later(b):
        count, group = BRANCHES[b]
        other = bufs[b].at[:, 1 - side]
        pltpu.make_async_copy(other, other, fwd_recv.at[b]).wait()

        def branch(j, carry):
            start = j * 256 + (hy * 64 if b >= 1 else 0)
            rows = pl.ds(pl.multiple_of(start, 16), count)
            same = sqcol[rows, 0:1] == sk_ref[pl.ds(1 + b * heads + j, 1), :]
            m_new, l_new, o_new = attend(q_ref[rows], j, bufs[b][...].reshape(LOCAL, 2 * width), same)
            m_old = m_acc[rows]
            mn = jnp.maximum(m_old, m_new)
            keep_old = jnp.exp(m_old - mn)
            keep_new = jnp.exp(m_new - mn)
            pick = o_lane == j
            m_acc[rows] = jnp.where(pick, mn, m_old)
            l_acc[rows] = jnp.where(pick, l_acc[rows] * keep_old + l_new * keep_new, l_acc[rows])
            o_acc[rows] = jnp.where(pick, o_acc[rows] * keep_old + o_new * keep_new, o_acc[rows])
            return carry

        lax.fori_loop(0, heads, branch, 0)

    lax.fori_loop(0, 1, branch0, 0)
    pl.semaphore_wait(barrier, halves + ys - 1)
    start_pushes()
    lax.fori_loop(1, 3, branch0, 0)
    forward(0)
    lax.fori_loop(3, LOCAL // chunk, branch0, 0)
    forward(1)
    later(0)
    forward(2)
    later(1)
    later(2)

    feature = lax.broadcasted_iota(jnp.int32, (8, 256), 1) < heads * HD
    ones = jnp.where(feature, 1.0, 0.0).astype(jnp.float32)
    first_row = lax.broadcasted_iota(jnp.int32, (8, chunk), 0) == 0

    def finish(i, carry):
        rows = pl.ds(pl.multiple_of(i * chunk, chunk), chunk)
        att = o_acc[rows] / l_acc[rows]
        o_acc[rows] = att
        dims = (((1,), (1,)), ((), ()))
        total = lax.dot_general(ones, att, dims, precision=lax.Precision.HIGHEST, preferred_element_type=jnp.float32)
        square = lax.dot_general(ones, att * att, dims, precision=lax.Precision.HIGHEST, preferred_element_type=jnp.float32)
        stats[:, rows] = jnp.where(first_row, total, square)
        return carry

    lax.fori_loop(0, LOCAL // chunk, finish, 0)
    ybuf[hy] = stats[...]
    shares = []
    for o in range(1, ys):
        cp = pltpu.make_async_remote_copy(
            src_ref=stats,
            dst_ref=ybuf.at[hy],
            send_sem=y_send.at[o - 1],
            recv_sem=y_recv.at[0],
            device_id=(me, lax.rem(hy + o, ys)),
            device_id_type=MESH,
        )
        cp.start()
        shares.append(cp)
    arrived = ybuf.at[pl.ds(0, ys - 1)]
    pltpu.make_async_copy(arrived, arrived, y_recv.at[0]).wait()
    for cp in shares:
        cp.wait_send()
    summed = ybuf[0]
    for h in range(1, ys):
        summed = summed + ybuf[h]
    mean = summed[0:1] / D
    var = summed[1:2] / D - mean * mean
    rstd = lax.rsqrt(var + 1e-05)
    pair = jnp.where(lax.broadcasted_iota(jnp.int32, (8, LOCAL), 0) == 0, mean, rstd)
    cols[...] = jnp.transpose(pair)

    def normalize(i, carry):
        rows = pl.ds(pl.multiple_of(i * chunk, chunk), chunk)
        col = cols[rows]
        normed = (o_acc[rows] - col[:, 0:1]) * col[:, 1:2]
        out_ref[rows] = (normed[:, : heads * HD] * gain_ref[...] + bias_ref[...]).astype(out_ref.dtype)
        return carry

    lax.fori_loop(0, LOCAL // chunk, normalize, 0)

    for b, (count, group) in enumerate(BRANCHES):
        pairs = group // 2
        if pairs > 1:
            went = bufs[b].at[pl.ds(0, pairs - 1), side]
            pltpu.make_async_copy(went, went, send_sem.at[b]).wait()
        forwards[b].wait_send()


def per_device(queries, keys, values, slide_lengths, norm_gain, norm_bias):
    heads = queries.shape[0] // HD
    width = heads * HD
    seq = lax.axis_index("seq")
    hy = lax.axis_index("head")
    slide_ends = jnp.cumsum(slide_lengths)
    q = to_token_major(jnp.concatenate([jnp.zeros((SHIFT, LOCAL), queries.dtype), queries]))
    kv = to_token_major(jnp.concatenate([values, keys]))
    kv_lane = jnp.arange(2 * width) % width // HD

    counts, groups, offsets = [LOCAL], [1], [0]
    for b, (count, group) in enumerate(BRANCHES):
        for j in range(heads):
            counts.append(count)
            groups.append(group)
            offsets.append(j * 256 + (hy * 64 if b >= 1 else 0))
    counts = jnp.array(counts, jnp.int32)[:, None]
    groups = jnp.array(groups, jnp.int32)[:, None]
    offsets = jnp.stack([jnp.asarray(o, jnp.int32) for o in offsets])[:, None]
    column = jnp.arange(LOCAL, dtype=jnp.int32)[None, :]
    devices = seq - seq % groups + column // counts
    slides = slide_of(pos_of(devices, offsets + column % counts), slide_ends)
    sends = []
    for b, (count, group) in enumerate(BRANCHES):
        starts = [j * 256 + (hy * 64 if b >= 1 else 0) for j in range(heads)]
        chunk = jnp.zeros((count, 2 * width), kv.dtype)
        for j in range(heads):
            piece = lax.dynamic_slice_in_dim(kv, starts[j], count, 0)
            chunk = jnp.where(kv_lane[None, :] == j, piece, chunk)
        sends.append(chunk)

    gain = norm_gain.reshape(1, width)
    bias = norm_bias.reshape(1, width)
    vmem = pl.BlockSpec(memory_space=pltpu.VMEM)
    out = pl.pallas_call(
        attention_kernel,
        out_shape=jax.ShapeDtypeStruct((LOCAL, width), jnp.bfloat16),
        in_specs=[vmem] * 8,
        out_specs=vmem,
        scratch_shapes=[
            *[pltpu.VMEM((group // 2, 2, count, 2 * width), jnp.bfloat16) for count, group in BRANCHES],
            pltpu.VMEM((LOCAL, 256), jnp.float32),
            pltpu.VMEM((LOCAL, 256), jnp.float32),
            pltpu.VMEM((LOCAL, 256), jnp.float32),
            pltpu.VMEM((8, LOCAL), jnp.float32),
            pltpu.VMEM((4, 8, LOCAL), jnp.float32),
            pltpu.VMEM((LOCAL, 8), jnp.float32),
            pltpu.VMEM((LOCAL, 8), jnp.int32),
            pltpu.SemaphoreType.DMA((3,)),
            pltpu.SemaphoreType.DMA((3,)),
            pltpu.SemaphoreType.DMA((3,)),
            pltpu.SemaphoreType.DMA((3,)),
            pltpu.SemaphoreType.DMA((3,)),
            pltpu.SemaphoreType.DMA((3,)),
            pltpu.SemaphoreType.DMA((1,)),
        ],
        compiler_params=pltpu.CompilerParams(
            collective_id=0, has_side_effects=True, vmem_limit_bytes=60 * 1024 * 1024
        ),
    )(q, kv, *sends, slides, gain, bias)
    return from_token_major(out)


def solution(mesh):
    placed = (P("head", "seq"),) * 3 + (P(), P("head"), P("head"))
    return jax.shard_map(
        per_device, mesh=mesh, in_specs=placed, out_specs=P("head", "seq"), check_vma=False
    )
```

```python
import math

import jax
import jax.numpy as jnp
from jax import lax
from jax.experimental import pallas as pl
from jax.experimental.pallas import tpu as pltpu
from jax.sharding import PartitionSpec as P

D = 768
HD = 48
SEG = 1024
LOCAL = 1024
MESH = pl.DeviceIdType.MESH
BRANCHES = ((256, 4), (64, 16), (16, 64))
SHIFT = 64


def to_token_major(x):
    f = x.shape[0]
    x = x.reshape(f, 16, 4, 4, 4)
    x = jnp.transpose(x, (4, 3, 2, 1, 0))
    return x.reshape(LOCAL, f)


def from_token_major(x):
    f = x.shape[1]
    x = x.reshape(4, 4, 4, 16, f)
    x = jnp.transpose(x, (4, 3, 2, 1, 0))
    return x.reshape(f, LOCAL)


def pos_of(device, index):
    local = 64 * (index % 16) + 16 * (index // 16 % 4) + 4 * (index // 64 % 4) + index // 256
    return device * LOCAL + local


def slide_of(positions, slide_ends):
    return jnp.sum((positions[..., None] >= slide_ends).astype(jnp.int32), axis=-1)


def attention_kernel(
    q_ref, kv_ref, send_ref, sk_ref, gain_ref, bias_ref,
    out_ref,
    kv1, kv2, kv3, m_acc, l_acc, o_acc, stats, ybuf, cols, sqcol,
    send_sem, recv_sem, local_sem, fwd_send, fwd_recv, y_send, y_recv,
):
    heads = 4
    me = lax.axis_index("seq")
    hy = lax.axis_index("head")
    devices = lax.axis_size("seq")
    scale = 1.0 / math.sqrt(HD)
    sends = (send_ref.at[pl.ds(0, 256)], send_ref.at[pl.ds(256, 64)], send_ref.at[pl.ds(320, 16)])
    sqcol[...] = jnp.transpose(sk_ref[pl.ds(0, 8), :])
    bufs = (kv1, kv2, kv3)
    width = heads * HD

    barrier = pltpu.get_barrier_semaphore()

    side = me % 2
    halves = devices // 2

    def greet(o, carry):
        peer = 2 * lax.rem(me // 2 + o, halves) + side
        pl.semaphore_signal(barrier, inc=1, device_id=(peer, hy), device_id_type=MESH)
        return carry

    lax.fori_loop(1, halves, greet, 0)
    pl.semaphore_signal(barrier, inc=1, device_id=(me + 1 - 2 * side, hy), device_id_type=MESH)
    ys = lax.axis_size("head")
    for o in range(1, ys):
        pl.semaphore_signal(barrier, inc=1, device_id=(me, lax.rem(hy + o, ys)), device_id_type=MESH)

    def slot(b, half, pair):
        return bufs[b].at[pair, half]

    sibling = me + 1 - 2 * (me % 2)
    locals_ = []
    for b, (count, group) in enumerate(BRANCHES):
        member = lax.rem(me, group)
        cp = pltpu.make_async_copy(sends[b], slot(b, side, member // 2), local_sem.at[b])
        cp.start()
        locals_.append(cp)
    def start_pushes():
        for b, (count, group) in enumerate(BRANCHES):
            member = lax.rem(me, group)
            first = me - member
            pairs = group // 2

            def push(o, carry, b=b, pairs=pairs, member=member, first=first):
                target = first + 2 * lax.rem(member // 2 + o, pairs) + side
                pltpu.make_async_remote_copy(
                    src_ref=sends[b],
                    dst_ref=slot(b, side, member // 2),
                    send_sem=send_sem.at[b],
                    recv_sem=recv_sem.at[b],
                    device_id=(target, hy),
                    device_id_type=MESH,
                ).start()
                return carry

            lax.fori_loop(1, pairs, push, 0)


    q_lane = (lax.broadcasted_iota(jnp.int32, (1, 256), 1) - SHIFT) // HD
    o_lane = lax.broadcasted_iota(jnp.int32, (1, 256), 1) // HD

    def attend(q, j, kv, same):
        qz = jnp.where(q_lane == j, q, jnp.zeros_like(q))
        s = lax.dot_general(qz, kv[:, 128:], (((1,), (1,)), ((), ())), preferred_element_type=jnp.float32)
        s = jnp.where(same, s, -1e30)
        m = jnp.max(s, axis=-1, keepdims=True)
        p = jnp.exp((s - m) * scale)
        l = jnp.sum(p, axis=-1, keepdims=True)
        o = jnp.dot(p.astype(jnp.bfloat16), kv[:, :256], preferred_element_type=jnp.float32)
        return m * scale, l, o

    chunk = 256

    def branch0(i, carry):
        rows = pl.ds(pl.multiple_of(i * chunk, chunk), chunk)
        q = q_ref[rows]
        kv = kv_ref[...]
        same = sqcol[rows, 0:1] == sk_ref[pl.ds(0, 1), :]
        mm = ll = oo = None
        for j in range(heads):
            m, l, o = attend(q, j, kv, same)
            if j == 0:
                mm = jnp.broadcast_to(m, (chunk, 256))
                ll = jnp.broadcast_to(l, (chunk, 256))
                oo = o
            else:
                pick = o_lane == j
                mm = jnp.where(pick, m, mm)
                ll = jnp.where(pick, l, ll)
                oo = jnp.where(pick, o, oo)
        m_acc[rows] = mm
        l_acc[rows] = ll
        o_acc[rows] = oo
        return carry

    forwards = []

    def forward(b):
        count, group = BRANCHES[b]
        pairs = group // 2
        locals_[b].wait()
        if pairs > 1:
            got = bufs[b].at[pl.ds(0, pairs - 1), side]
            pltpu.make_async_copy(got, got, recv_sem.at[b]).wait()
        cp = pltpu.make_async_remote_copy(
            src_ref=bufs[b].at[:, side],
            dst_ref=bufs[b].at[:, side],
            send_sem=fwd_send.at[b],
            recv_sem=fwd_recv.at[b],
            device_id=(sibling, hy),
            device_id_type=MESH,
        )
        cp.start()
        forwards.append(cp)

    def later(b):
        count, group = BRANCHES[b]
        other = bufs[b].at[:, 1 - side]
        pltpu.make_async_copy(other, other, fwd_recv.at[b]).wait()

        def branch(j, carry):
            start = j * 256 + (hy * 64 if b >= 1 else 0)
            rows = pl.ds(pl.multiple_of(start, 16), count)
            same = sqcol[rows, 0:1] == sk_ref[pl.ds(1 + b * heads + j, 1), :]
            m_new, l_new, o_new = attend(q_ref[rows], j, bufs[b][...].reshape(LOCAL, 2 * width), same)
            m_old = m_acc[rows]
            mn = jnp.maximum(m_old, m_new)
            keep_old = jnp.exp(m_old - mn)
            keep_new = jnp.exp(m_new - mn)
            pick = o_lane == j
            m_acc[rows] = jnp.where(pick, mn, m_old)
            l_acc[rows] = jnp.where(pick, l_acc[rows] * keep_old + l_new * keep_new, l_acc[rows])
            o_acc[rows] = jnp.where(pick, o_acc[rows] * keep_old + o_new * keep_new, o_acc[rows])
            return carry

        lax.fori_loop(0, heads, branch, 0)

    lax.fori_loop(0, 1, branch0, 0)
    pl.semaphore_wait(barrier, halves + ys - 1)
    start_pushes()
    lax.fori_loop(1, 3, branch0, 0)
    forward(0)
    lax.fori_loop(3, LOCAL // chunk, branch0, 0)
    forward(1)
    later(0)
    forward(2)
    later(1)
    later(2)

    feature = lax.broadcasted_iota(jnp.int32, (8, 256), 1) < heads * HD
    ones = jnp.where(feature, 1.0, 0.0).astype(jnp.float32)
    first_row = lax.broadcasted_iota(jnp.int32, (8, chunk), 0) == 0

    def finish(i, carry):
        rows = pl.ds(pl.multiple_of(i * chunk, chunk), chunk)
        att = o_acc[rows] / l_acc[rows]
        o_acc[rows] = att
        dims = (((1,), (1,)), ((), ()))
        total = lax.dot_general(ones, att, dims, precision=lax.Precision.HIGHEST, preferred_element_type=jnp.float32)
        square = lax.dot_general(ones, att * att, dims, precision=lax.Precision.HIGHEST, preferred_element_type=jnp.float32)
        stats[:, rows] = jnp.where(first_row, total, square)
        return carry

    lax.fori_loop(0, LOCAL // chunk, finish, 0)
    ybuf[hy] = stats[...]
    shares = []
    for o in range(1, ys):
        cp = pltpu.make_async_remote_copy(
            src_ref=stats,
            dst_ref=ybuf.at[hy],
            send_sem=y_send.at[o - 1],
            recv_sem=y_recv.at[0],
            device_id=(me, lax.rem(hy + o, ys)),
            device_id_type=MESH,
        )
        cp.start()
        shares.append(cp)
    arrived = ybuf.at[pl.ds(0, ys - 1)]
    pltpu.make_async_copy(arrived, arrived, y_recv.at[0]).wait()
    for cp in shares:
        cp.wait_send()
    summed = ybuf[0]
    for h in range(1, ys):
        summed = summed + ybuf[h]
    mean = summed[0:1] / D
    var = summed[1:2] / D - mean * mean
    rstd = lax.rsqrt(var + 1e-05)
    pair = jnp.where(lax.broadcasted_iota(jnp.int32, (8, LOCAL), 0) == 0, mean, rstd)
    cols[...] = jnp.transpose(pair)

    def normalize(i, carry):
        rows = pl.ds(pl.multiple_of(i * chunk, chunk), chunk)
        col = cols[rows]
        normed = (o_acc[rows] - col[:, 0:1]) * col[:, 1:2]
        out_ref[rows] = (normed[:, : heads * HD] * gain_ref[...] + bias_ref[...]).astype(out_ref.dtype)
        return carry

    lax.fori_loop(0, LOCAL // chunk, normalize, 0)

    for b, (count, group) in enumerate(BRANCHES):
        pairs = group // 2
        if pairs > 1:
            went = bufs[b].at[pl.ds(0, pairs - 1), side]
            pltpu.make_async_copy(went, went, send_sem.at[b]).wait()
        forwards[b].wait_send()


def per_device(queries, keys, values, slide_lengths, norm_gain, norm_bias):
    heads = queries.shape[0] // HD
    width = heads * HD
    seq = lax.axis_index("seq")
    hy = lax.axis_index("head")
    slide_ends = jnp.cumsum(slide_lengths)
    q = to_token_major(jnp.concatenate([jnp.zeros((SHIFT, LOCAL), queries.dtype), queries]))
    kv = to_token_major(jnp.concatenate([values, keys]))
    kv_lane = jnp.arange(2 * width) % width // HD

    counts, groups, offsets = [LOCAL], [1], [0]
    for b, (count, group) in enumerate(BRANCHES):
        for j in range(heads):
            counts.append(count)
            groups.append(group)
            offsets.append(j * 256 + (hy * 64 if b >= 1 else 0))
    counts = jnp.array(counts, jnp.int32)[:, None]
    groups = jnp.array(groups, jnp.int32)[:, None]
    offsets = jnp.stack([jnp.asarray(o, jnp.int32) for o in offsets])[:, None]
    column = jnp.arange(LOCAL, dtype=jnp.int32)[None, :]
    devices = seq - seq % groups + column // counts
    slides = slide_of(pos_of(devices, offsets + column % counts), slide_ends)
    sends = []
    for b, (count, group) in enumerate(BRANCHES):
        starts = [j * 256 + (hy * 64 if b >= 1 else 0) for j in range(heads)]
        chunk = jnp.zeros((count, 2 * width), kv.dtype)
        for j in range(heads):
            piece = lax.dynamic_slice_in_dim(kv, starts[j], count, 0)
            chunk = jnp.where(kv_lane[None, :] == j, piece, chunk)
        sends.append(chunk)

    gain = norm_gain.reshape(1, width)
    bias = norm_bias.reshape(1, width)
    vmem = pl.BlockSpec(memory_space=pltpu.VMEM)
    out = pl.pallas_call(
        attention_kernel,
        out_shape=jax.ShapeDtypeStruct((LOCAL, width), jnp.bfloat16),
        in_specs=[vmem] * 6,
        out_specs=vmem,
        scratch_shapes=[
            *[pltpu.VMEM((group // 2, 2, count, 2 * width), jnp.bfloat16) for count, group in BRANCHES],
            pltpu.VMEM((LOCAL, 256), jnp.float32),
            pltpu.VMEM((LOCAL, 256), jnp.float32),
            pltpu.VMEM((LOCAL, 256), jnp.float32),
            pltpu.VMEM((8, LOCAL), jnp.float32),
            pltpu.VMEM((4, 8, LOCAL), jnp.float32),
            pltpu.VMEM((LOCAL, 8), jnp.float32),
            pltpu.VMEM((LOCAL, 8), jnp.int32),
            pltpu.SemaphoreType.DMA((3,)),
            pltpu.SemaphoreType.DMA((3,)),
            pltpu.SemaphoreType.DMA((3,)),
            pltpu.SemaphoreType.DMA((3,)),
            pltpu.SemaphoreType.DMA((3,)),
            pltpu.SemaphoreType.DMA((3,)),
            pltpu.SemaphoreType.DMA((1,)),
        ],
        compiler_params=pltpu.CompilerParams(
            collective_id=0, has_side_effects=True, vmem_limit_bytes=60 * 1024 * 1024
        ),
    )(q, kv, jnp.concatenate(sends), slides, gain, bias)
    return from_token_major(out)


def solution(mesh):
    placed = (P("head", "seq"),) * 3 + (P(), P("head"), P("head"))
    return jax.shard_map(
        per_device, mesh=mesh, in_specs=placed, out_specs=P("head", "seq"), check_vma=False
    )
```

```python
import math

import jax
import jax.numpy as jnp
from jax import lax
from jax.experimental import pallas as pl
from jax.experimental.pallas import tpu as pltpu
from jax.sharding import PartitionSpec as P

D = 768
HD = 48
SEG = 1024
LOCAL = 1024
MESH = pl.DeviceIdType.MESH
BRANCHES = ((256, 4), (64, 16), (16, 64))
SHIFT = 64


def to_token_major(x):
    f = x.shape[0]
    x = x.reshape(f, 16, 4, 4, 4)
    x = jnp.transpose(x, (4, 3, 2, 1, 0))
    return x.reshape(LOCAL, f)


def from_token_major(x):
    f = x.shape[1]
    x = x.reshape(4, 4, 4, 16, f)
    x = jnp.transpose(x, (4, 3, 2, 1, 0))
    return x.reshape(f, LOCAL)


def pos_of(device, index):
    local = 64 * (index % 16) + 16 * (index // 16 % 4) + 4 * (index // 64 % 4) + index // 256
    return device * LOCAL + local


def slide_of(positions, slide_ends):
    return jnp.sum((positions[..., None] >= slide_ends).astype(jnp.int32), axis=-1)


def attention_kernel(
    q_ref, kv_ref, send_ref, sk_ref, gain_ref, bias_ref,
    out_ref,
    kv1, kv2, kv3, m_acc, l_acc, o_acc, stats, ybuf, cols, sqcol,
    send_sem, recv_sem, local_sem, fwd_send, fwd_recv, y_send, y_recv,
):
    heads = 4
    me = lax.axis_index("seq")
    hy = lax.axis_index("head")
    devices = lax.axis_size("seq")
    scale = 1.0 / math.sqrt(HD)
    sends = (send_ref.at[pl.ds(0, 256)], send_ref.at[pl.ds(256, 64)], send_ref.at[pl.ds(320, 16)])
    sqcol[...] = jnp.transpose(sk_ref[pl.ds(0, 8), :])
    bufs = (kv1, kv2, kv3)
    width = heads * HD

    barrier = pltpu.get_barrier_semaphore()

    side = me % 2
    halves = devices // 2

    def greet(o, carry):
        peer = 2 * lax.rem(me // 2 + o, halves) + side
        pl.semaphore_signal(barrier, inc=1, device_id=(peer, hy), device_id_type=MESH)
        return carry

    lax.fori_loop(1, halves, greet, 0)
    pl.semaphore_signal(barrier, inc=1, device_id=(me + 1 - 2 * side, hy), device_id_type=MESH)
    ys = lax.axis_size("head")
    for o in range(1, ys):
        pl.semaphore_signal(barrier, inc=1, device_id=(me, lax.rem(hy + o, ys)), device_id_type=MESH)

    def slot(b, half, pair):
        return bufs[b].at[pair, half]

    sibling = me + 1 - 2 * (me % 2)
    locals_ = []
    for b, (count, group) in enumerate(BRANCHES):
        member = lax.rem(me, group)
        cp = pltpu.make_async_copy(sends[b], slot(b, side, member // 2), local_sem.at[b])
        cp.start()
        locals_.append(cp)
    def start_pushes():
        for b, (count, group) in enumerate(BRANCHES):
            member = lax.rem(me, group)
            first = me - member
            pairs = group // 2

            def push(o, carry, b=b, pairs=pairs, member=member, first=first):
                target = first + 2 * lax.rem(member // 2 + o, pairs) + side
                pltpu.make_async_remote_copy(
                    src_ref=sends[b],
                    dst_ref=slot(b, side, member // 2),
                    send_sem=send_sem.at[b],
                    recv_sem=recv_sem.at[b],
                    device_id=(target, hy),
                    device_id_type=MESH,
                ).start()
                return carry

            lax.fori_loop(1, pairs, push, 0)


    q_lane = (lax.broadcasted_iota(jnp.int32, (1, 256), 1) - SHIFT) // HD
    o_lane = lax.broadcasted_iota(jnp.int32, (1, 256), 1) // HD

    def attend(q, j, kv, same):
        qz = jnp.where(q_lane == j, q, jnp.zeros_like(q))
        s = lax.dot_general(qz, kv[:, 128:], (((1,), (1,)), ((), ())), preferred_element_type=jnp.float32)
        s = jnp.where(same, s, -1e30)
        m = jnp.max(s, axis=-1, keepdims=True)
        p = jnp.exp((s - m) * scale)
        l = jnp.sum(p, axis=-1, keepdims=True)
        o = jnp.dot(p.astype(jnp.bfloat16), kv[:, :256], preferred_element_type=jnp.float32)
        return m * scale, l, o

    chunk = 256

    def branch0(i, carry):
        rows = pl.ds(pl.multiple_of(i * chunk, chunk), chunk)
        q = q_ref[rows]
        kv = kv_ref[...]
        same = sqcol[rows, 0:1] == sk_ref[pl.ds(0, 1), :]
        mm = ll = oo = None
        for j in range(heads):
            m, l, o = attend(q, j, kv, same)
            if j == 0:
                mm = jnp.broadcast_to(m, (chunk, 256))
                ll = jnp.broadcast_to(l, (chunk, 256))
                oo = o
            else:
                pick = o_lane == j
                mm = jnp.where(pick, m, mm)
                ll = jnp.where(pick, l, ll)
                oo = jnp.where(pick, o, oo)
        m_acc[rows] = mm
        l_acc[rows] = ll
        o_acc[rows] = oo
        return carry

    forwards = []

    def forward(b):
        count, group = BRANCHES[b]
        pairs = group // 2
        locals_[b].wait()
        if pairs > 1:
            got = bufs[b].at[pl.ds(0, pairs - 1), side]
            pltpu.make_async_copy(got, got, recv_sem.at[b]).wait()
        cp = pltpu.make_async_remote_copy(
            src_ref=bufs[b].at[:, side],
            dst_ref=bufs[b].at[:, side],
            send_sem=fwd_send.at[b],
            recv_sem=fwd_recv.at[b],
            device_id=(sibling, hy),
            device_id_type=MESH,
        )
        cp.start()
        forwards.append(cp)

    def later(b):
        count, group = BRANCHES[b]
        other = bufs[b].at[:, 1 - side]
        pltpu.make_async_copy(other, other, fwd_recv.at[b]).wait()

        def branch(j, carry):
            start = j * 256 + (hy * 64 if b >= 1 else 0)
            rows = pl.ds(pl.multiple_of(start, 16), count)
            same = sqcol[rows, 0:1] == sk_ref[pl.ds(1 + b * heads + j, 1), :]
            m_new, l_new, o_new = attend(q_ref[rows], j, bufs[b][...].reshape(LOCAL, 2 * width), same)
            m_old = m_acc[rows]
            mn = jnp.maximum(m_old, m_new)
            keep_old = jnp.exp(m_old - mn)
            keep_new = jnp.exp(m_new - mn)
            pick = o_lane == j
            m_acc[rows] = jnp.where(pick, mn, m_old)
            l_acc[rows] = jnp.where(pick, l_acc[rows] * keep_old + l_new * keep_new, l_acc[rows])
            o_acc[rows] = jnp.where(pick, o_acc[rows] * keep_old + o_new * keep_new, o_acc[rows])
            return carry

        lax.fori_loop(0, heads, branch, 0)

    pl.semaphore_wait(barrier, halves + ys - 1)
    start_pushes()
    lax.fori_loop(0, 3, branch0, 0)
    forward(0)
    lax.fori_loop(3, LOCAL // chunk, branch0, 0)
    forward(1)
    later(0)
    forward(2)
    later(1)
    later(2)

    feature = lax.broadcasted_iota(jnp.int32, (8, 256), 1) < heads * HD
    ones = jnp.where(feature, 1.0, 0.0).astype(jnp.float32)
    first_row = lax.broadcasted_iota(jnp.int32, (8, chunk), 0) == 0

    def finish(i, carry):
        rows = pl.ds(pl.multiple_of(i * chunk, chunk), chunk)
        att = o_acc[rows] / l_acc[rows]
        o_acc[rows] = att
        dims = (((1,), (1,)), ((), ()))
        total = lax.dot_general(ones, att, dims, precision=lax.Precision.HIGHEST, preferred_element_type=jnp.float32)
        square = lax.dot_general(ones, att * att, dims, precision=lax.Precision.HIGHEST, preferred_element_type=jnp.float32)
        stats[:, rows] = jnp.where(first_row, total, square)
        return carry

    lax.fori_loop(0, LOCAL // chunk, finish, 0)
    ybuf[hy] = stats[...]
    shares = []
    for o in range(1, ys):
        cp = pltpu.make_async_remote_copy(
            src_ref=stats,
            dst_ref=ybuf.at[hy],
            send_sem=y_send.at[o - 1],
            recv_sem=y_recv.at[0],
            device_id=(me, lax.rem(hy + o, ys)),
            device_id_type=MESH,
        )
        cp.start()
        shares.append(cp)
    arrived = ybuf.at[pl.ds(0, ys - 1)]
    pltpu.make_async_copy(arrived, arrived, y_recv.at[0]).wait()
    for cp in shares:
        cp.wait_send()
    summed = ybuf[0]
    for h in range(1, ys):
        summed = summed + ybuf[h]
    mean = summed[0:1] / D
    var = summed[1:2] / D - mean * mean
    rstd = lax.rsqrt(var + 1e-05)
    pair = jnp.where(lax.broadcasted_iota(jnp.int32, (8, LOCAL), 0) == 0, mean, rstd)
    cols[...] = jnp.transpose(pair)

    def normalize(i, carry):
        rows = pl.ds(pl.multiple_of(i * chunk, chunk), chunk)
        col = cols[rows]
        normed = (o_acc[rows] - col[:, 0:1]) * col[:, 1:2]
        out_ref[rows] = (normed[:, : heads * HD] * gain_ref[...] + bias_ref[...]).astype(out_ref.dtype)
        return carry

    lax.fori_loop(0, LOCAL // chunk, normalize, 0)

    for b, (count, group) in enumerate(BRANCHES):
        pairs = group // 2
        if pairs > 1:
            went = bufs[b].at[pl.ds(0, pairs - 1), side]
            pltpu.make_async_copy(went, went, send_sem.at[b]).wait()
        forwards[b].wait_send()


def per_device(queries, keys, values, slide_lengths, norm_gain, norm_bias):
    heads = queries.shape[0] // HD
    width = heads * HD
    seq = lax.axis_index("seq")
    hy = lax.axis_index("head")
    slide_ends = jnp.cumsum(slide_lengths)
    q = to_token_major(jnp.concatenate([jnp.zeros((SHIFT, LOCAL), queries.dtype), queries]))
    kv = to_token_major(jnp.concatenate([values, keys]))
    kv_lane = jnp.arange(2 * width) % width // HD

    counts, groups, offsets = [LOCAL], [1], [0]
    for b, (count, group) in enumerate(BRANCHES):
        for j in range(heads):
            counts.append(count)
            groups.append(group)
            offsets.append(j * 256 + (hy * 64 if b >= 1 else 0))
    counts = jnp.array(counts, jnp.int32)[:, None]
    groups = jnp.array(groups, jnp.int32)[:, None]
    offsets = jnp.stack([jnp.asarray(o, jnp.int32) for o in offsets])[:, None]
    column = jnp.arange(LOCAL, dtype=jnp.int32)[None, :]
    devices = seq - seq % groups + column // counts
    slides = slide_of(pos_of(devices, offsets + column % counts), slide_ends)
    sends = []
    for b, (count, group) in enumerate(BRANCHES):
        starts = [j * 256 + (hy * 64 if b >= 1 else 0) for j in range(heads)]
        chunk = jnp.zeros((count, 2 * width), kv.dtype)
        for j in range(heads):
            piece = lax.dynamic_slice_in_dim(kv, starts[j], count, 0)
            chunk = jnp.where(kv_lane[None, :] == j, piece, chunk)
        sends.append(chunk)

    gain = norm_gain.reshape(1, width)
    bias = norm_bias.reshape(1, width)
    vmem = pl.BlockSpec(memory_space=pltpu.VMEM)
    out = pl.pallas_call(
        attention_kernel,
        out_shape=jax.ShapeDtypeStruct((LOCAL, width), jnp.bfloat16),
        in_specs=[vmem] * 6,
        out_specs=vmem,
        scratch_shapes=[
            *[pltpu.VMEM((group // 2, 2, count, 2 * width), jnp.bfloat16) for count, group in BRANCHES],
            pltpu.VMEM((LOCAL, 256), jnp.float32),
            pltpu.VMEM((LOCAL, 256), jnp.float32),
            pltpu.VMEM((LOCAL, 256), jnp.float32),
            pltpu.VMEM((8, LOCAL), jnp.float32),
            pltpu.VMEM((4, 8, LOCAL), jnp.float32),
            pltpu.VMEM((LOCAL, 8), jnp.float32),
            pltpu.VMEM((LOCAL, 8), jnp.int32),
            pltpu.SemaphoreType.DMA((3,)),
            pltpu.SemaphoreType.DMA((3,)),
            pltpu.SemaphoreType.DMA((3,)),
            pltpu.SemaphoreType.DMA((3,)),
            pltpu.SemaphoreType.DMA((3,)),
            pltpu.SemaphoreType.DMA((3,)),
            pltpu.SemaphoreType.DMA((1,)),
        ],
        compiler_params=pltpu.CompilerParams(
            collective_id=0, has_side_effects=True, vmem_limit_bytes=60 * 1024 * 1024
        ),
    )(q, kv, jnp.concatenate(sends), slides, gain, bias)
    return from_token_major(out)


def solution(mesh):
    placed = (P("head", "seq"),) * 3 + (P(), P("head"), P("head"))
    return jax.shard_map(
        per_device, mesh=mesh, in_specs=placed, out_specs=P("head", "seq"), check_vma=False
    )
```

```python
import math

import jax
import jax.numpy as jnp
from jax import lax
from jax.experimental import pallas as pl
from jax.experimental.pallas import tpu as pltpu
from jax.sharding import PartitionSpec as P

D = 768
HD = 48
SEG = 1024
LOCAL = 1024
MESH = pl.DeviceIdType.MESH
BRANCHES = ((256, 4), (64, 16), (16, 64))
SHIFT = 64


def to_token_major(x):
    f = x.shape[0]
    x = x.reshape(f, 16, 4, 4, 4)
    x = jnp.transpose(x, (4, 3, 2, 1, 0))
    return x.reshape(LOCAL, f)


def from_token_major(x):
    f = x.shape[1]
    x = x.reshape(4, 4, 4, 16, f)
    x = jnp.transpose(x, (4, 3, 2, 1, 0))
    return x.reshape(f, LOCAL)


def pos_of(device, index):
    local = 64 * (index % 16) + 16 * (index // 16 % 4) + 4 * (index // 64 % 4) + index // 256
    return device * LOCAL + local


def slide_of(positions, slide_ends):
    return jnp.sum((positions[..., None] >= slide_ends).astype(jnp.int32), axis=-1)


def attention_kernel(
    q_ref, kv_ref, send_ref, len_ref, gain_ref, bias_ref,
    out_ref,
    kv1, kv2, kv3, m_acc, l_acc, o_acc, stats, ybuf, cols, sqcol, sk_ref,
    send_sem, recv_sem, local_sem, fwd_send, fwd_recv, y_send, y_recv,
):
    heads = 4
    me = lax.axis_index("seq")
    hy = lax.axis_index("head")
    devices = lax.axis_size("seq")
    scale = 1.0 / math.sqrt(HD)
    sends = (send_ref.at[pl.ds(0, 256)], send_ref.at[pl.ds(256, 64)], send_ref.at[pl.ds(320, 16)])
    bufs = (kv1, kv2, kv3)
    width = heads * HD

    barrier = pltpu.get_barrier_semaphore()

    side = me % 2
    halves = devices // 2

    def greet(o, carry):
        peer = 2 * lax.rem(me // 2 + o, halves) + side
        pl.semaphore_signal(barrier, inc=1, device_id=(peer, hy), device_id_type=MESH)
        return carry

    lax.fori_loop(1, halves, greet, 0)
    pl.semaphore_signal(barrier, inc=1, device_id=(me + 1 - 2 * side, hy), device_id_type=MESH)
    ys = lax.axis_size("head")
    for o in range(1, ys):
        pl.semaphore_signal(barrier, inc=1, device_id=(me, lax.rem(hy + o, ys)), device_id_type=MESH)

    row = lax.broadcasted_iota(jnp.int32, (16, LOCAL), 0)
    column = lax.broadcasted_iota(jnp.int32, (16, LOCAL), 1)
    shift = jnp.where(row == 0, 10, jnp.where(row <= 4, 8, jnp.where(row <= 8, 6, 4)))
    group = jnp.where(row == 0, 1, jnp.where(row <= 4, 4, jnp.where(row <= 8, 16, 64)))
    offset = jnp.where(row == 0, 0, ((row - 1) & 3) * 256 + jnp.where(row >= 5, hy * 64, 0))
    device = me - (me & (group - 1)) + (column >> shift)
    index = offset + (column & ((1 << shift) - 1))
    local = ((index & 15) << 6) + (((index >> 4) & 3) << 4) + (((index >> 6) & 3) << 2) + (index >> 8)
    position = device * LOCAL + local

    def count_ends(k, carry):
        end, acc = carry
        end = end + len_ref[k]
        return end, acc + jnp.where(position >= end, 1, 0)

    _, slide = lax.fori_loop(0, len_ref.shape[0], count_ends, (jnp.int32(0), jnp.zeros((16, LOCAL), jnp.int32)))
    sk_ref[...] = slide
    sqcol[...] = jnp.transpose(slide[0:8])

    def slot(b, half, pair):
        return bufs[b].at[pair, half]

    sibling = me + 1 - 2 * (me % 2)
    locals_ = []
    for b, (count, group) in enumerate(BRANCHES):
        member = lax.rem(me, group)
        cp = pltpu.make_async_copy(sends[b], slot(b, side, member // 2), local_sem.at[b])
        cp.start()
        locals_.append(cp)
    def start_pushes():
        for b, (count, group) in enumerate(BRANCHES):
            member = lax.rem(me, group)
            first = me - member
            pairs = group // 2

            def push(o, carry, b=b, pairs=pairs, member=member, first=first):
                target = first + 2 * lax.rem(member // 2 + o, pairs) + side
                pltpu.make_async_remote_copy(
                    src_ref=sends[b],
                    dst_ref=slot(b, side, member // 2),
                    send_sem=send_sem.at[b],
                    recv_sem=recv_sem.at[b],
                    device_id=(target, hy),
                    device_id_type=MESH,
                ).start()
                return carry

            lax.fori_loop(1, pairs, push, 0)


    q_lane = (lax.broadcasted_iota(jnp.int32, (1, 256), 1) - SHIFT) // HD
    o_lane = lax.broadcasted_iota(jnp.int32, (1, 256), 1) // HD

    def attend(q, j, kv, same):
        qz = jnp.where(q_lane == j, q, jnp.zeros_like(q))
        s = lax.dot_general(qz, kv[:, 128:], (((1,), (1,)), ((), ())), preferred_element_type=jnp.float32)
        s = jnp.where(same, s, -1e30)
        m = jnp.max(s, axis=-1, keepdims=True)
        p = jnp.exp((s - m) * scale)
        l = jnp.sum(p, axis=-1, keepdims=True)
        o = jnp.dot(p.astype(jnp.bfloat16), kv[:, :256], preferred_element_type=jnp.float32)
        return m * scale, l, o

    chunk = 256

    def branch0(i, carry):
        rows = pl.ds(pl.multiple_of(i * chunk, chunk), chunk)
        q = q_ref[rows]
        kv = kv_ref[...]
        same = sqcol[rows, 0:1] == sk_ref[pl.ds(0, 1), :]
        mm = ll = oo = None
        for j in range(heads):
            m, l, o = attend(q, j, kv, same)
            if j == 0:
                mm = jnp.broadcast_to(m, (chunk, 256))
                ll = jnp.broadcast_to(l, (chunk, 256))
                oo = o
            else:
                pick = o_lane == j
                mm = jnp.where(pick, m, mm)
                ll = jnp.where(pick, l, ll)
                oo = jnp.where(pick, o, oo)
        m_acc[rows] = mm
        l_acc[rows] = ll
        o_acc[rows] = oo
        return carry

    forwards = []

    def forward(b):
        count, group = BRANCHES[b]
        pairs = group // 2
        locals_[b].wait()
        if pairs > 1:
            got = bufs[b].at[pl.ds(0, pairs - 1), side]
            pltpu.make_async_copy(got, got, recv_sem.at[b]).wait()
        cp = pltpu.make_async_remote_copy(
            src_ref=bufs[b].at[:, side],
            dst_ref=bufs[b].at[:, side],
            send_sem=fwd_send.at[b],
            recv_sem=fwd_recv.at[b],
            device_id=(sibling, hy),
            device_id_type=MESH,
        )
        cp.start()
        forwards.append(cp)

    def later(b):
        count, group = BRANCHES[b]
        other = bufs[b].at[:, 1 - side]
        pltpu.make_async_copy(other, other, fwd_recv.at[b]).wait()

        def branch(j, carry):
            start = j * 256 + (hy * 64 if b >= 1 else 0)
            rows = pl.ds(pl.multiple_of(start, 16), count)
            same = sqcol[rows, 0:1] == sk_ref[pl.ds(1 + b * heads + j, 1), :]
            m_new, l_new, o_new = attend(q_ref[rows], j, bufs[b][...].reshape(LOCAL, 2 * width), same)
            m_old = m_acc[rows]
            mn = jnp.maximum(m_old, m_new)
            keep_old = jnp.exp(m_old - mn)
            keep_new = jnp.exp(m_new - mn)
            pick = o_lane == j
            m_acc[rows] = jnp.where(pick, mn, m_old)
            l_acc[rows] = jnp.where(pick, l_acc[rows] * keep_old + l_new * keep_new, l_acc[rows])
            o_acc[rows] = jnp.where(pick, o_acc[rows] * keep_old + o_new * keep_new, o_acc[rows])
            return carry

        lax.fori_loop(0, heads, branch, 0)

    lax.fori_loop(0, 1, branch0, 0)
    pl.semaphore_wait(barrier, halves + ys - 1)
    start_pushes()
    lax.fori_loop(1, 3, branch0, 0)
    forward(0)
    lax.fori_loop(3, LOCAL // chunk, branch0, 0)
    forward(1)
    later(0)
    forward(2)
    later(1)
    later(2)

    feature = lax.broadcasted_iota(jnp.int32, (8, 256), 1) < heads * HD
    ones = jnp.where(feature, 1.0, 0.0).astype(jnp.float32)
    first_row = lax.broadcasted_iota(jnp.int32, (8, chunk), 0) == 0

    def finish(i, carry):
        rows = pl.ds(pl.multiple_of(i * chunk, chunk), chunk)
        att = o_acc[rows] / l_acc[rows]
        o_acc[rows] = att
        dims = (((1,), (1,)), ((), ()))
        total = lax.dot_general(ones, att, dims, precision=lax.Precision.HIGHEST, preferred_element_type=jnp.float32)
        square = lax.dot_general(ones, att * att, dims, precision=lax.Precision.HIGHEST, preferred_element_type=jnp.float32)
        stats[:, rows] = jnp.where(first_row, total, square)
        return carry

    lax.fori_loop(0, LOCAL // chunk, finish, 0)
    ybuf[hy] = stats[...]
    shares = []
    for o in range(1, ys):
        cp = pltpu.make_async_remote_copy(
            src_ref=stats,
            dst_ref=ybuf.at[hy],
            send_sem=y_send.at[o - 1],
            recv_sem=y_recv.at[0],
            device_id=(me, lax.rem(hy + o, ys)),
            device_id_type=MESH,
        )
        cp.start()
        shares.append(cp)
    arrived = ybuf.at[pl.ds(0, ys - 1)]
    pltpu.make_async_copy(arrived, arrived, y_recv.at[0]).wait()
    for cp in shares:
        cp.wait_send()
    summed = ybuf[0]
    for h in range(1, ys):
        summed = summed + ybuf[h]
    mean = summed[0:1] / D
    var = summed[1:2] / D - mean * mean
    rstd = lax.rsqrt(var + 1e-05)
    pair = jnp.where(lax.broadcasted_iota(jnp.int32, (8, LOCAL), 0) == 0, mean, rstd)
    cols[...] = jnp.transpose(pair)

    def normalize(i, carry):
        rows = pl.ds(pl.multiple_of(i * chunk, chunk), chunk)
        col = cols[rows]
        normed = (o_acc[rows] - col[:, 0:1]) * col[:, 1:2]
        out_ref[rows] = (normed[:, : heads * HD] * gain_ref[...] + bias_ref[...]).astype(out_ref.dtype)
        return carry

    lax.fori_loop(0, LOCAL // chunk, normalize, 0)

    for b, (count, group) in enumerate(BRANCHES):
        pairs = group // 2
        if pairs > 1:
            went = bufs[b].at[pl.ds(0, pairs - 1), side]
            pltpu.make_async_copy(went, went, send_sem.at[b]).wait()
        forwards[b].wait_send()


def per_device(queries, keys, values, slide_lengths, norm_gain, norm_bias):
    heads = queries.shape[0] // HD
    width = heads * HD
    seq = lax.axis_index("seq")
    hy = lax.axis_index("head")
    q = to_token_major(jnp.concatenate([jnp.zeros((SHIFT, LOCAL), queries.dtype), queries]))
    kv = to_token_major(jnp.concatenate([values, keys]))
    kv_lane = jnp.arange(2 * width) % width // HD

    sends = []
    for b, (count, group) in enumerate(BRANCHES):
        starts = [j * 256 + (hy * 64 if b >= 1 else 0) for j in range(heads)]
        chunk = jnp.zeros((count, 2 * width), kv.dtype)
        for j in range(heads):
            piece = lax.dynamic_slice_in_dim(kv, starts[j], count, 0)
            chunk = jnp.where(kv_lane[None, :] == j, piece, chunk)
        sends.append(chunk)

    gain = norm_gain.reshape(1, width)
    bias = norm_bias.reshape(1, width)
    vmem = pl.BlockSpec(memory_space=pltpu.VMEM)
    out = pl.pallas_call(
        attention_kernel,
        out_shape=jax.ShapeDtypeStruct((LOCAL, width), jnp.bfloat16),
        in_specs=[vmem] * 3 + [pl.BlockSpec(memory_space=pltpu.SMEM)] + [vmem] * 2,
        out_specs=vmem,
        scratch_shapes=[
            *[pltpu.VMEM((group // 2, 2, count, 2 * width), jnp.bfloat16) for count, group in BRANCHES],
            pltpu.VMEM((LOCAL, 256), jnp.float32),
            pltpu.VMEM((LOCAL, 256), jnp.float32),
            pltpu.VMEM((LOCAL, 256), jnp.float32),
            pltpu.VMEM((8, LOCAL), jnp.float32),
            pltpu.VMEM((4, 8, LOCAL), jnp.float32),
            pltpu.VMEM((LOCAL, 8), jnp.float32),
            pltpu.VMEM((LOCAL, 8), jnp.int32),
            pltpu.VMEM((16, LOCAL), jnp.int32),
            pltpu.SemaphoreType.DMA((3,)),
            pltpu.SemaphoreType.DMA((3,)),
            pltpu.SemaphoreType.DMA((3,)),
            pltpu.SemaphoreType.DMA((3,)),
            pltpu.SemaphoreType.DMA((3,)),
            pltpu.SemaphoreType.DMA((3,)),
            pltpu.SemaphoreType.DMA((1,)),
        ],
        compiler_params=pltpu.CompilerParams(
            collective_id=0, has_side_effects=True, vmem_limit_bytes=60 * 1024 * 1024
        ),
    )(q, kv, jnp.concatenate(sends), slide_lengths, gain, bias)
    return from_token_major(out)


def solution(mesh):
    placed = (P("head", "seq"),) * 3 + (P(), P("head"), P("head"))
    return jax.shard_map(
        per_device, mesh=mesh, in_specs=placed, out_specs=P("head", "seq"), check_vma=False
    )
```

```python
import math

import jax
import jax.numpy as jnp
from jax import lax
from jax.experimental import pallas as pl
from jax.experimental.pallas import tpu as pltpu
from jax.sharding import PartitionSpec as P

D = 768
HD = 48
SEG = 1024
LOCAL = 1024
MESH = pl.DeviceIdType.MESH
BRANCHES = ((256, 4), (64, 16), (16, 64))
SHIFT = 64


def to_token_major(x):
    f = x.shape[0]
    x = x.reshape(f, 16, 4, 4, 4)
    x = jnp.transpose(x, (4, 3, 2, 1, 0))
    return x.reshape(LOCAL, f)


def from_token_major(x):
    f = x.shape[1]
    x = x.reshape(4, 4, 4, 16, f)
    x = jnp.transpose(x, (4, 3, 2, 1, 0))
    return x.reshape(f, LOCAL)


def pos_of(device, index):
    local = 64 * (index % 16) + 16 * (index // 16 % 4) + 4 * (index // 64 % 4) + index // 256
    return device * LOCAL + local


def slide_of(positions, slide_ends):
    return jnp.sum((positions[..., None] >= slide_ends).astype(jnp.int32), axis=-1)


def attention_kernel(
    x_ref, send_ref, len_ref, gain_ref, bias_ref,
    out_ref,
    kv1, kv2, kv3, m_acc, l_acc, o_acc, stats, ybuf, cols, sqcol, sk_ref,
    send_sem, recv_sem, local_sem, fwd_send, fwd_recv, y_send, y_recv,
):
    heads = 4
    me = lax.axis_index("seq")
    hy = lax.axis_index("head")
    devices = lax.axis_size("seq")
    scale = 1.0 / math.sqrt(HD)
    sends = (send_ref.at[pl.ds(0, 256)], send_ref.at[pl.ds(256, 64)], send_ref.at[pl.ds(320, 16)])
    bufs = (kv1, kv2, kv3)
    width = heads * HD

    barrier = pltpu.get_barrier_semaphore()

    side = me % 2
    halves = devices // 2

    def greet(o, carry):
        peer = 2 * lax.rem(me // 2 + o, halves) + side
        pl.semaphore_signal(barrier, inc=1, device_id=(peer, hy), device_id_type=MESH)
        return carry

    lax.fori_loop(1, halves, greet, 0)
    pl.semaphore_signal(barrier, inc=1, device_id=(me + 1 - 2 * side, hy), device_id_type=MESH)
    ys = lax.axis_size("head")
    for o in range(1, ys):
        pl.semaphore_signal(barrier, inc=1, device_id=(me, lax.rem(hy + o, ys)), device_id_type=MESH)

    row = lax.broadcasted_iota(jnp.int32, (16, LOCAL), 0)
    column = lax.broadcasted_iota(jnp.int32, (16, LOCAL), 1)
    shift = jnp.where(row == 0, 10, jnp.where(row <= 4, 8, jnp.where(row <= 8, 6, 4)))
    group = jnp.where(row == 0, 1, jnp.where(row <= 4, 4, jnp.where(row <= 8, 16, 64)))
    offset = jnp.where(row == 0, 0, ((row - 1) & 3) * 256 + jnp.where(row >= 5, hy * 64, 0))
    device = me - (me & (group - 1)) + (column >> shift)
    index = offset + (column & ((1 << shift) - 1))
    local = ((index & 15) << 6) + (((index >> 4) & 3) << 4) + (((index >> 6) & 3) << 2) + (index >> 8)
    position = device * LOCAL + local

    def count_ends(k, carry):
        end, acc = carry
        end = end + len_ref[k]
        return end, acc + jnp.where(position >= end, 1, 0)

    _, slide = lax.fori_loop(0, len_ref.shape[0], count_ends, (jnp.int32(0), jnp.zeros((16, LOCAL), jnp.int32)))
    sk_ref[...] = slide
    sqcol[...] = jnp.transpose(slide[0:8])

    def slot(b, half, pair):
        return bufs[b].at[pair, half]

    sibling = me + 1 - 2 * (me % 2)
    locals_ = []
    for b, (count, group) in enumerate(BRANCHES):
        member = lax.rem(me, group)
        cp = pltpu.make_async_copy(sends[b], slot(b, side, member // 2), local_sem.at[b])
        cp.start()
        locals_.append(cp)
    def start_pushes():
        for b, (count, group) in enumerate(BRANCHES):
            member = lax.rem(me, group)
            first = me - member
            pairs = group // 2

            def push(o, carry, b=b, pairs=pairs, member=member, first=first):
                target = first + 2 * lax.rem(member // 2 + o, pairs) + side
                pltpu.make_async_remote_copy(
                    src_ref=sends[b],
                    dst_ref=slot(b, side, member // 2),
                    send_sem=send_sem.at[b],
                    recv_sem=recv_sem.at[b],
                    device_id=(target, hy),
                    device_id_type=MESH,
                ).start()
                return carry

            lax.fori_loop(1, pairs, push, 0)


    q_lane = (lax.broadcasted_iota(jnp.int32, (1, 256), 1) - SHIFT) // HD
    o_lane = lax.broadcasted_iota(jnp.int32, (1, 256), 1) // HD

    def attend(q, j, kv, same):
        qz = jnp.where(q_lane == j, q, jnp.zeros_like(q))
        s = lax.dot_general(qz, kv[:, 128:], (((1,), (1,)), ((), ())), preferred_element_type=jnp.float32)
        s = jnp.where(same, s, -1e30)
        m = jnp.max(s, axis=-1, keepdims=True)
        p = jnp.exp((s - m) * scale)
        l = jnp.sum(p, axis=-1, keepdims=True)
        o = jnp.dot(p.astype(jnp.bfloat16), kv[:, :256], preferred_element_type=jnp.float32)
        return m * scale, l, o

    chunk = 256

    def branch0(i, carry):
        rows = pl.ds(pl.multiple_of(i * chunk, chunk), chunk)
        q = x_ref[rows, pl.ds(0, 256)]
        kv = x_ref[:, pl.ds(256, 384)]
        same = sqcol[rows, 0:1] == sk_ref[pl.ds(0, 1), :]
        mm = ll = oo = None
        for j in range(heads):
            m, l, o = attend(q, j, kv, same)
            if j == 0:
                mm = jnp.broadcast_to(m, (chunk, 256))
                ll = jnp.broadcast_to(l, (chunk, 256))
                oo = o
            else:
                pick = o_lane == j
                mm = jnp.where(pick, m, mm)
                ll = jnp.where(pick, l, ll)
                oo = jnp.where(pick, o, oo)
        m_acc[rows] = mm
        l_acc[rows] = ll
        o_acc[rows] = oo
        return carry

    forwards = []

    def forward(b):
        count, group = BRANCHES[b]
        pairs = group // 2
        locals_[b].wait()
        if pairs > 1:
            got = bufs[b].at[pl.ds(0, pairs - 1), side]
            pltpu.make_async_copy(got, got, recv_sem.at[b]).wait()
        cp = pltpu.make_async_remote_copy(
            src_ref=bufs[b].at[:, side],
            dst_ref=bufs[b].at[:, side],
            send_sem=fwd_send.at[b],
            recv_sem=fwd_recv.at[b],
            device_id=(sibling, hy),
            device_id_type=MESH,
        )
        cp.start()
        forwards.append(cp)

    def later(b):
        count, group = BRANCHES[b]
        other = bufs[b].at[:, 1 - side]
        pltpu.make_async_copy(other, other, fwd_recv.at[b]).wait()

        def branch(j, carry):
            start = j * 256 + (hy * 64 if b >= 1 else 0)
            rows = pl.ds(pl.multiple_of(start, 16), count)
            same = sqcol[rows, 0:1] == sk_ref[pl.ds(1 + b * heads + j, 1), :]
            m_new, l_new, o_new = attend(x_ref[rows, pl.ds(0, 256)], j, bufs[b][...].reshape(LOCAL, 2 * width), same)
            m_old = m_acc[rows]
            mn = jnp.maximum(m_old, m_new)
            keep_old = jnp.exp(m_old - mn)
            keep_new = jnp.exp(m_new - mn)
            pick = o_lane == j
            m_acc[rows] = jnp.where(pick, mn, m_old)
            l_acc[rows] = jnp.where(pick, l_acc[rows] * keep_old + l_new * keep_new, l_acc[rows])
            o_acc[rows] = jnp.where(pick, o_acc[rows] * keep_old + o_new * keep_new, o_acc[rows])
            return carry

        lax.fori_loop(0, heads, branch, 0)

    lax.fori_loop(0, 1, branch0, 0)
    pl.semaphore_wait(barrier, halves + ys - 1)
    start_pushes()
    lax.fori_loop(1, 3, branch0, 0)
    forward(0)
    lax.fori_loop(3, LOCAL // chunk, branch0, 0)
    forward(1)
    later(0)
    forward(2)
    later(1)
    later(2)

    feature = lax.broadcasted_iota(jnp.int32, (8, 256), 1) < heads * HD
    ones = jnp.where(feature, 1.0, 0.0).astype(jnp.float32)
    first_row = lax.broadcasted_iota(jnp.int32, (8, chunk), 0) == 0

    def finish(i, carry):
        rows = pl.ds(pl.multiple_of(i * chunk, chunk), chunk)
        att = o_acc[rows] / l_acc[rows]
        o_acc[rows] = att
        dims = (((1,), (1,)), ((), ()))
        total = lax.dot_general(ones, att, dims, precision=lax.Precision.HIGHEST, preferred_element_type=jnp.float32)
        square = lax.dot_general(ones, att * att, dims, precision=lax.Precision.HIGHEST, preferred_element_type=jnp.float32)
        stats[:, rows] = jnp.where(first_row, total, square)
        return carry

    lax.fori_loop(0, LOCAL // chunk, finish, 0)
    ybuf[hy] = stats[...]
    shares = []
    for o in range(1, ys):
        cp = pltpu.make_async_remote_copy(
            src_ref=stats,
            dst_ref=ybuf.at[hy],
            send_sem=y_send.at[o - 1],
            recv_sem=y_recv.at[0],
            device_id=(me, lax.rem(hy + o, ys)),
            device_id_type=MESH,
        )
        cp.start()
        shares.append(cp)
    arrived = ybuf.at[pl.ds(0, ys - 1)]
    pltpu.make_async_copy(arrived, arrived, y_recv.at[0]).wait()
    for cp in shares:
        cp.wait_send()
    summed = ybuf[0]
    for h in range(1, ys):
        summed = summed + ybuf[h]
    mean = summed[0:1] / D
    var = summed[1:2] / D - mean * mean
    rstd = lax.rsqrt(var + 1e-05)
    pair = jnp.where(lax.broadcasted_iota(jnp.int32, (8, LOCAL), 0) == 0, mean, rstd)
    cols[...] = jnp.transpose(pair)

    def normalize(i, carry):
        rows = pl.ds(pl.multiple_of(i * chunk, chunk), chunk)
        col = cols[rows]
        normed = (o_acc[rows] - col[:, 0:1]) * col[:, 1:2]
        out_ref[rows] = (normed[:, : heads * HD] * gain_ref[...] + bias_ref[...]).astype(out_ref.dtype)
        return carry

    lax.fori_loop(0, LOCAL // chunk, normalize, 0)

    for b, (count, group) in enumerate(BRANCHES):
        pairs = group // 2
        if pairs > 1:
            went = bufs[b].at[pl.ds(0, pairs - 1), side]
            pltpu.make_async_copy(went, went, send_sem.at[b]).wait()
        forwards[b].wait_send()


def per_device(queries, keys, values, slide_lengths, norm_gain, norm_bias):
    heads = queries.shape[0] // HD
    width = heads * HD
    seq = lax.axis_index("seq")
    hy = lax.axis_index("head")
    x = to_token_major(jnp.concatenate([jnp.zeros((SHIFT, LOCAL), queries.dtype), queries, values, keys]))
    kv = x[:, 256:]
    kv_lane = jnp.arange(2 * width) % width // HD

    sends = []
    for b, (count, group) in enumerate(BRANCHES):
        starts = [j * 256 + (hy * 64 if b >= 1 else 0) for j in range(heads)]
        chunk = jnp.zeros((count, 2 * width), kv.dtype)
        for j in range(heads):
            piece = lax.dynamic_slice_in_dim(kv, starts[j], count, 0)
            chunk = jnp.where(kv_lane[None, :] == j, piece, chunk)
        sends.append(chunk)

    gain = norm_gain.reshape(1, width)
    bias = norm_bias.reshape(1, width)
    vmem = pl.BlockSpec(memory_space=pltpu.VMEM)
    out = pl.pallas_call(
        attention_kernel,
        out_shape=jax.ShapeDtypeStruct((LOCAL, width), jnp.bfloat16),
        in_specs=[vmem] * 2 + [pl.BlockSpec(memory_space=pltpu.SMEM)] + [vmem] * 2,
        out_specs=vmem,
        scratch_shapes=[
            *[pltpu.VMEM((group // 2, 2, count, 2 * width), jnp.bfloat16) for count, group in BRANCHES],
            pltpu.VMEM((LOCAL, 256), jnp.float32),
            pltpu.VMEM((LOCAL, 256), jnp.float32),
            pltpu.VMEM((LOCAL, 256), jnp.float32),
            pltpu.VMEM((8, LOCAL), jnp.float32),
            pltpu.VMEM((4, 8, LOCAL), jnp.float32),
            pltpu.VMEM((LOCAL, 8), jnp.float32),
            pltpu.VMEM((LOCAL, 8), jnp.int32),
            pltpu.VMEM((16, LOCAL), jnp.int32),
            pltpu.SemaphoreType.DMA((3,)),
            pltpu.SemaphoreType.DMA((3,)),
            pltpu.SemaphoreType.DMA((3,)),
            pltpu.SemaphoreType.DMA((3,)),
            pltpu.SemaphoreType.DMA((3,)),
            pltpu.SemaphoreType.DMA((3,)),
            pltpu.SemaphoreType.DMA((1,)),
        ],
        compiler_params=pltpu.CompilerParams(
            collective_id=0, has_side_effects=True, vmem_limit_bytes=60 * 1024 * 1024
        ),
    )(x, jnp.concatenate(sends), slide_lengths, gain, bias)
    return from_token_major(out)


def solution(mesh):
    placed = (P("head", "seq"),) * 3 + (P(), P("head"), P("head"))
    return jax.shard_map(
        per_device, mesh=mesh, in_specs=placed, out_specs=P("head", "seq"), check_vma=False
    )
```

```python
import math

import jax
import jax.numpy as jnp
from jax import lax
from jax.experimental import pallas as pl
from jax.experimental.pallas import tpu as pltpu
from jax.sharding import PartitionSpec as P

D = 768
HD = 48
SEG = 1024
LOCAL = 1024
MESH = pl.DeviceIdType.MESH
BRANCHES = ((256, 4), (64, 16), (16, 64))
SHIFT = 64


def to_token_major(x):
    f = x.shape[0]
    x = x.reshape(f, 16, 4, 4, 4)
    x = jnp.transpose(x, (4, 3, 2, 1, 0))
    return x.reshape(LOCAL, f)


def from_digit_order(x):
    f = x.shape[0]
    x = x.reshape(f, 4, 4, 4, 16)
    x = jnp.transpose(x, (0, 4, 3, 2, 1))
    return x.reshape(f, LOCAL)


def from_token_major(x):
    f = x.shape[1]
    x = x.reshape(4, 4, 4, 16, f)
    x = jnp.transpose(x, (4, 3, 2, 1, 0))
    return x.reshape(f, LOCAL)


def pos_of(device, index):
    local = 64 * (index % 16) + 16 * (index // 16 % 4) + 4 * (index // 64 % 4) + index // 256
    return device * LOCAL + local


def slide_of(positions, slide_ends):
    return jnp.sum((positions[..., None] >= slide_ends).astype(jnp.int32), axis=-1)


def attention_kernel(
    q_ref, kv_ref, send_ref, len_ref, gain_ref, bias_ref,
    out_ref,
    kv1, kv2, kv3, m_acc, l_acc, o_acc, stats, ybuf, cols, sqcol, sk_ref, zbuf,
    send_sem, recv_sem, local_sem, fwd_send, fwd_recv, y_send, y_recv,
):
    heads = 4
    me = lax.axis_index("seq")
    hy = lax.axis_index("head")
    devices = lax.axis_size("seq")
    scale = 1.0 / math.sqrt(HD)
    sends = (send_ref.at[pl.ds(0, 256)], send_ref.at[pl.ds(256, 64)], send_ref.at[pl.ds(320, 16)])
    bufs = (kv1, kv2, kv3)
    width = heads * HD

    barrier = pltpu.get_barrier_semaphore()

    side = me % 2
    halves = devices // 2

    def greet(o, carry):
        peer = 2 * lax.rem(me // 2 + o, halves) + side
        pl.semaphore_signal(barrier, inc=1, device_id=(peer, hy), device_id_type=MESH)
        return carry

    lax.fori_loop(1, halves, greet, 0)
    pl.semaphore_signal(barrier, inc=1, device_id=(me + 1 - 2 * side, hy), device_id_type=MESH)
    ys = lax.axis_size("head")
    for o in range(1, ys):
        pl.semaphore_signal(barrier, inc=1, device_id=(me, lax.rem(hy + o, ys)), device_id_type=MESH)

    row = lax.broadcasted_iota(jnp.int32, (16, LOCAL), 0)
    column = lax.broadcasted_iota(jnp.int32, (16, LOCAL), 1)
    shift = jnp.where(row == 0, 10, jnp.where(row <= 4, 8, jnp.where(row <= 8, 6, 4)))
    group = jnp.where(row == 0, 1, jnp.where(row <= 4, 4, jnp.where(row <= 8, 16, 64)))
    offset = jnp.where(row == 0, 0, ((row - 1) & 3) * 256 + jnp.where(row >= 5, hy * 64, 0))
    device = me - (me & (group - 1)) + (column >> shift)
    index = offset + (column & ((1 << shift) - 1))
    local = ((index & 15) << 6) + (((index >> 4) & 3) << 4) + (((index >> 6) & 3) << 2) + (index >> 8)
    position = device * LOCAL + local

    def count_ends(k, carry):
        end, acc = carry
        end = end + len_ref[k]
        return end, acc + jnp.where(position >= end, 1, 0)

    _, slide = lax.fori_loop(0, len_ref.shape[0], count_ends, (jnp.int32(0), jnp.zeros((16, LOCAL), jnp.int32)))
    sk_ref[...] = slide
    sqcol[...] = jnp.transpose(slide[0:8])

    def slot(b, half, pair):
        return bufs[b].at[pair, half]

    sibling = me + 1 - 2 * (me % 2)
    locals_ = []
    for b, (count, group) in enumerate(BRANCHES):
        member = lax.rem(me, group)
        cp = pltpu.make_async_copy(sends[b], slot(b, side, member // 2), local_sem.at[b])
        cp.start()
        locals_.append(cp)
    def start_pushes():
        for b, (count, group) in enumerate(BRANCHES):
            member = lax.rem(me, group)
            first = me - member
            pairs = group // 2

            def push(o, carry, b=b, pairs=pairs, member=member, first=first):
                target = first + 2 * lax.rem(member // 2 + o, pairs) + side
                pltpu.make_async_remote_copy(
                    src_ref=sends[b],
                    dst_ref=slot(b, side, member // 2),
                    send_sem=send_sem.at[b],
                    recv_sem=recv_sem.at[b],
                    device_id=(target, hy),
                    device_id_type=MESH,
                ).start()
                return carry

            lax.fori_loop(1, pairs, push, 0)


    q_lane = (lax.broadcasted_iota(jnp.int32, (1, 256), 1) - SHIFT) // HD
    o_lane = lax.broadcasted_iota(jnp.int32, (1, 256), 1) // HD

    def attend(q, j, kv, same):
        qz = jnp.where(q_lane == j, q, jnp.zeros_like(q))
        s = lax.dot_general(qz, kv[:, 128:], (((1,), (1,)), ((), ())), preferred_element_type=jnp.float32)
        s = jnp.where(same, s, -1e30)
        m = jnp.max(s, axis=-1, keepdims=True)
        p = jnp.exp((s - m) * scale)
        l = jnp.sum(p, axis=-1, keepdims=True)
        o = jnp.dot(p.astype(jnp.bfloat16), kv[:, :256], preferred_element_type=jnp.float32)
        return m * scale, l, o

    chunk = 256

    def branch0(i, carry):
        rows = pl.ds(pl.multiple_of(i * chunk, chunk), chunk)
        q = q_ref[rows]
        kv = kv_ref[...]
        same = sqcol[rows, 0:1] == sk_ref[pl.ds(0, 1), :]
        mm = ll = oo = None
        for j in range(heads):
            m, l, o = attend(q, j, kv, same)
            if j == 0:
                mm = jnp.broadcast_to(m, (chunk, 256))
                ll = jnp.broadcast_to(l, (chunk, 256))
                oo = o
            else:
                pick = o_lane == j
                mm = jnp.where(pick, m, mm)
                ll = jnp.where(pick, l, ll)
                oo = jnp.where(pick, o, oo)
        m_acc[rows] = mm
        l_acc[rows] = ll
        o_acc[rows] = oo
        return carry

    forwards = []

    def forward(b):
        count, group = BRANCHES[b]
        pairs = group // 2
        locals_[b].wait()
        if pairs > 1:
            got = bufs[b].at[pl.ds(0, pairs - 1), side]
            pltpu.make_async_copy(got, got, recv_sem.at[b]).wait()
        cp = pltpu.make_async_remote_copy(
            src_ref=bufs[b].at[:, side],
            dst_ref=bufs[b].at[:, side],
            send_sem=fwd_send.at[b],
            recv_sem=fwd_recv.at[b],
            device_id=(sibling, hy),
            device_id_type=MESH,
        )
        cp.start()
        forwards.append(cp)

    def later(b):
        count, group = BRANCHES[b]
        other = bufs[b].at[:, 1 - side]
        pltpu.make_async_copy(other, other, fwd_recv.at[b]).wait()

        def branch(j, carry):
            start = j * 256 + (hy * 64 if b >= 1 else 0)
            rows = pl.ds(pl.multiple_of(start, 16), count)
            same = sqcol[rows, 0:1] == sk_ref[pl.ds(1 + b * heads + j, 1), :]
            m_new, l_new, o_new = attend(q_ref[rows], j, bufs[b][...].reshape(LOCAL, 2 * width), same)
            m_old = m_acc[rows]
            mn = jnp.maximum(m_old, m_new)
            keep_old = jnp.exp(m_old - mn)
            keep_new = jnp.exp(m_new - mn)
            pick = o_lane == j
            m_acc[rows] = jnp.where(pick, mn, m_old)
            l_acc[rows] = jnp.where(pick, l_acc[rows] * keep_old + l_new * keep_new, l_acc[rows])
            o_acc[rows] = jnp.where(pick, o_acc[rows] * keep_old + o_new * keep_new, o_acc[rows])
            return carry

        lax.fori_loop(0, heads, branch, 0)

    lax.fori_loop(0, 1, branch0, 0)
    pl.semaphore_wait(barrier, halves + ys - 1)
    start_pushes()
    lax.fori_loop(1, 3, branch0, 0)
    forward(0)
    lax.fori_loop(3, LOCAL // chunk, branch0, 0)
    forward(1)
    later(0)
    forward(2)
    later(1)
    later(2)

    feature = lax.broadcasted_iota(jnp.int32, (8, 256), 1) < heads * HD
    ones = jnp.where(feature, 1.0, 0.0).astype(jnp.float32)
    first_row = lax.broadcasted_iota(jnp.int32, (8, chunk), 0) == 0

    def finish(i, carry):
        rows = pl.ds(pl.multiple_of(i * chunk, chunk), chunk)
        att = o_acc[rows] / l_acc[rows]
        o_acc[rows] = att
        dims = (((1,), (1,)), ((), ()))
        total = lax.dot_general(ones, att, dims, precision=lax.Precision.HIGHEST, preferred_element_type=jnp.float32)
        square = lax.dot_general(ones, att * att, dims, precision=lax.Precision.HIGHEST, preferred_element_type=jnp.float32)
        stats[:, rows] = jnp.where(first_row, total, square)
        return carry

    lax.fori_loop(0, LOCAL // chunk, finish, 0)
    ybuf[hy] = stats[...]
    shares = []
    for o in range(1, ys):
        cp = pltpu.make_async_remote_copy(
            src_ref=stats,
            dst_ref=ybuf.at[hy],
            send_sem=y_send.at[o - 1],
            recv_sem=y_recv.at[0],
            device_id=(me, lax.rem(hy + o, ys)),
            device_id_type=MESH,
        )
        cp.start()
        shares.append(cp)
    arrived = ybuf.at[pl.ds(0, ys - 1)]
    pltpu.make_async_copy(arrived, arrived, y_recv.at[0]).wait()
    for cp in shares:
        cp.wait_send()
    summed = ybuf[0]
    for h in range(1, ys):
        summed = summed + ybuf[h]
    mean = summed[0:1] / D
    var = summed[1:2] / D - mean * mean
    rstd = lax.rsqrt(var + 1e-05)
    pair = jnp.where(lax.broadcasted_iota(jnp.int32, (8, LOCAL), 0) == 0, mean, rstd)
    cols[...] = jnp.transpose(pair)

    def normalize(i, carry):
        rows = pl.ds(pl.multiple_of(i * chunk, chunk), chunk)
        col = cols[rows]
        normed = (o_acc[rows] - col[:, 0:1]) * col[:, 1:2]
        zbuf[:, 0 : heads * HD] = normed[:, : heads * HD] * gain_ref[...] + bias_ref[...]
        out_ref[:, rows] = jnp.transpose(zbuf[...])[0 : heads * HD].astype(out_ref.dtype)
        return carry

    lax.fori_loop(0, LOCAL // chunk, normalize, 0)

    for b, (count, group) in enumerate(BRANCHES):
        pairs = group // 2
        if pairs > 1:
            went = bufs[b].at[pl.ds(0, pairs - 1), side]
            pltpu.make_async_copy(went, went, send_sem.at[b]).wait()
        forwards[b].wait_send()


def per_device(queries, keys, values, slide_lengths, norm_gain, norm_bias):
    heads = queries.shape[0] // HD
    width = heads * HD
    seq = lax.axis_index("seq")
    hy = lax.axis_index("head")
    q = to_token_major(jnp.concatenate([jnp.zeros((SHIFT, LOCAL), queries.dtype), queries]))
    kv = to_token_major(jnp.concatenate([values, keys]))
    kv_lane = jnp.arange(2 * width) % width // HD

    sends = []
    for b, (count, group) in enumerate(BRANCHES):
        starts = [j * 256 + (hy * 64 if b >= 1 else 0) for j in range(heads)]
        chunk = jnp.zeros((count, 2 * width), kv.dtype)
        for j in range(heads):
            piece = lax.dynamic_slice_in_dim(kv, starts[j], count, 0)
            chunk = jnp.where(kv_lane[None, :] == j, piece, chunk)
        sends.append(chunk)

    gain = norm_gain.reshape(1, width)
    bias = norm_bias.reshape(1, width)
    vmem = pl.BlockSpec(memory_space=pltpu.VMEM)
    out = pl.pallas_call(
        attention_kernel,
        out_shape=jax.ShapeDtypeStruct((width, LOCAL), jnp.bfloat16),
        in_specs=[vmem] * 3 + [pl.BlockSpec(memory_space=pltpu.SMEM)] + [vmem] * 2,
        out_specs=vmem,
        scratch_shapes=[
            *[pltpu.VMEM((group // 2, 2, count, 2 * width), jnp.bfloat16) for count, group in BRANCHES],
            pltpu.VMEM((LOCAL, 256), jnp.float32),
            pltpu.VMEM((LOCAL, 256), jnp.float32),
            pltpu.VMEM((LOCAL, 256), jnp.float32),
            pltpu.VMEM((8, LOCAL), jnp.float32),
            pltpu.VMEM((4, 8, LOCAL), jnp.float32),
            pltpu.VMEM((LOCAL, 8), jnp.float32),
            pltpu.VMEM((LOCAL, 8), jnp.int32),
            pltpu.VMEM((16, LOCAL), jnp.int32),
            pltpu.VMEM((256, 256), jnp.float32),
            pltpu.SemaphoreType.DMA((3,)),
            pltpu.SemaphoreType.DMA((3,)),
            pltpu.SemaphoreType.DMA((3,)),
            pltpu.SemaphoreType.DMA((3,)),
            pltpu.SemaphoreType.DMA((3,)),
            pltpu.SemaphoreType.DMA((3,)),
            pltpu.SemaphoreType.DMA((1,)),
        ],
        compiler_params=pltpu.CompilerParams(
            collective_id=0, has_side_effects=True, vmem_limit_bytes=60 * 1024 * 1024
        ),
    )(q, kv, jnp.concatenate(sends), slide_lengths, gain, bias)
    return from_digit_order(out)


def solution(mesh):
    placed = (P("head", "seq"),) * 3 + (P(), P("head"), P("head"))
    return jax.shard_map(
        per_device, mesh=mesh, in_specs=placed, out_specs=P("head", "seq"), check_vma=False
    )
```

```python
import math

import jax
import jax.numpy as jnp
from jax import lax
from jax.experimental import pallas as pl
from jax.experimental.pallas import tpu as pltpu
from jax.sharding import PartitionSpec as P

D = 768
HD = 48
SEG = 1024
LOCAL = 1024
MESH = pl.DeviceIdType.MESH
BRANCHES = ((256, 4), (64, 16), (16, 64))
SHIFT = 64


def to_token_major(x):
    f = x.shape[0]
    x = x.reshape(f, 16, 4, 4, 4)
    x = jnp.transpose(x, (4, 3, 2, 1, 0))
    return x.reshape(LOCAL, f)


def from_token_major(x):
    f = x.shape[1]
    x = x.reshape(4, 4, 4, 16, f)
    x = jnp.transpose(x, (4, 3, 2, 1, 0))
    return x.reshape(f, LOCAL)


def pos_of(device, index):
    local = 64 * (index % 16) + 16 * (index // 16 % 4) + 4 * (index // 64 % 4) + index // 256
    return device * LOCAL + local


def slide_of(positions, slide_ends):
    return jnp.sum((positions[..., None] >= slide_ends).astype(jnp.int32), axis=-1)


def attention_kernel(
    q_ref, kv_ref, send_ref, len_ref, gain_ref, bias_ref,
    out_ref,
    kv1, kv2, kv3, m_acc, l_acc, o_acc, stats, ybuf, cols, sqcol, sk_ref,
    send_sem, recv_sem, local_sem, fwd_send, fwd_recv, y_send, y_recv,
):
    heads = 4
    me = lax.axis_index("seq")
    hy = lax.axis_index("head")
    devices = lax.axis_size("seq")
    scale = 1.0 / math.sqrt(HD)
    sends = (send_ref.at[pl.ds(0, 256)], send_ref.at[pl.ds(256, 64)], send_ref.at[pl.ds(320, 16)])
    bufs = (kv1, kv2, kv3)
    width = heads * HD

    barrier = pltpu.get_barrier_semaphore()

    side = me % 2
    halves = devices // 2

    def greet(o, carry):
        peer = 2 * lax.rem(me // 2 + o, halves) + side
        pl.semaphore_signal(barrier, inc=1, device_id=(peer, hy), device_id_type=MESH)
        return carry

    lax.fori_loop(1, halves, greet, 0)
    pl.semaphore_signal(barrier, inc=1, device_id=(me + 1 - 2 * side, hy), device_id_type=MESH)
    ys = lax.axis_size("head")
    for o in range(1, ys):
        pl.semaphore_signal(barrier, inc=1, device_id=(me, lax.rem(hy + o, ys)), device_id_type=MESH)

    row = lax.broadcasted_iota(jnp.int32, (16, LOCAL), 0)
    column = lax.broadcasted_iota(jnp.int32, (16, LOCAL), 1)
    shift = jnp.where(row == 0, 10, jnp.where(row <= 4, 8, jnp.where(row <= 8, 6, 4)))
    group = jnp.where(row == 0, 1, jnp.where(row <= 4, 4, jnp.where(row <= 8, 16, 64)))
    offset = jnp.where(row == 0, 0, ((row - 1) & 3) * 256 + jnp.where(row >= 5, hy * 64, 0))
    device = me - (me & (group - 1)) + (column >> shift)
    index = offset + (column & ((1 << shift) - 1))
    local = ((index & 15) << 6) + (((index >> 4) & 3) << 4) + (((index >> 6) & 3) << 2) + (index >> 8)
    position = device * LOCAL + local

    def count_ends(k, carry):
        end, acc = carry
        end = end + len_ref[k]
        return end, acc + jnp.where(position >= end, 1, 0)

    _, slide = lax.fori_loop(0, len_ref.shape[0], count_ends, (jnp.int32(0), jnp.zeros((16, LOCAL), jnp.int32)))
    sk_ref[...] = slide
    sqcol[...] = jnp.transpose(slide[0:8])

    def slot(b, half, pair):
        return bufs[b].at[pair, half]

    sibling = me + 1 - 2 * (me % 2)
    locals_ = []
    for b, (count, group) in enumerate(BRANCHES):
        member = lax.rem(me, group)
        cp = pltpu.make_async_copy(sends[b], slot(b, side, member // 2), local_sem.at[b])
        cp.start()
        locals_.append(cp)
    def start_pushes():
        for b, (count, group) in reversed(list(enumerate(BRANCHES))):
            member = lax.rem(me, group)
            first = me - member
            pairs = group // 2

            def push(o, carry, b=b, pairs=pairs, member=member, first=first):
                target = first + 2 * lax.rem(member // 2 + o, pairs) + side
                pltpu.make_async_remote_copy(
                    src_ref=sends[b],
                    dst_ref=slot(b, side, member // 2),
                    send_sem=send_sem.at[b],
                    recv_sem=recv_sem.at[b],
                    device_id=(target, hy),
                    device_id_type=MESH,
                ).start()
                return carry

            lax.fori_loop(1, pairs, push, 0)


    q_lane = (lax.broadcasted_iota(jnp.int32, (1, 256), 1) - SHIFT) // HD
    o_lane = lax.broadcasted_iota(jnp.int32, (1, 256), 1) // HD

    def attend(q, j, kv, same):
        qz = jnp.where(q_lane == j, q, jnp.zeros_like(q))
        s = lax.dot_general(qz, kv[:, 128:], (((1,), (1,)), ((), ())), preferred_element_type=jnp.float32)
        s = jnp.where(same, s, -1e30)
        m = jnp.max(s, axis=-1, keepdims=True)
        p = jnp.exp((s - m) * scale)
        l = jnp.sum(p, axis=-1, keepdims=True)
        o = jnp.dot(p.astype(jnp.bfloat16), kv[:, :256], preferred_element_type=jnp.float32)
        return m * scale, l, o

    chunk = 256

    def branch0(i, carry):
        rows = pl.ds(pl.multiple_of(i * chunk, chunk), chunk)
        q = q_ref[rows]
        kv = kv_ref[...]
        same = sqcol[rows, 0:1] == sk_ref[pl.ds(0, 1), :]
        mm = ll = oo = None
        for j in range(heads):
            m, l, o = attend(q, j, kv, same)
            if j == 0:
                mm = jnp.broadcast_to(m, (chunk, 256))
                ll = jnp.broadcast_to(l, (chunk, 256))
                oo = o
            else:
                pick = o_lane == j
                mm = jnp.where(pick, m, mm)
                ll = jnp.where(pick, l, ll)
                oo = jnp.where(pick, o, oo)
        m_acc[rows] = mm
        l_acc[rows] = ll
        o_acc[rows] = oo
        return carry

    forwards = []

    def forward(b):
        count, group = BRANCHES[b]
        pairs = group // 2
        locals_[b].wait()
        if pairs > 1:
            got = bufs[b].at[pl.ds(0, pairs - 1), side]
            pltpu.make_async_copy(got, got, recv_sem.at[b]).wait()
        cp = pltpu.make_async_remote_copy(
            src_ref=bufs[b].at[:, side],
            dst_ref=bufs[b].at[:, side],
            send_sem=fwd_send.at[b],
            recv_sem=fwd_recv.at[b],
            device_id=(sibling, hy),
            device_id_type=MESH,
        )
        cp.start()
        forwards.append(cp)

    def later(b):
        count, group = BRANCHES[b]
        other = bufs[b].at[:, 1 - side]
        pltpu.make_async_copy(other, other, fwd_recv.at[b]).wait()

        def branch(j, carry):
            start = j * 256 + (hy * 64 if b >= 1 else 0)
            rows = pl.ds(pl.multiple_of(start, 16), count)
            same = sqcol[rows, 0:1] == sk_ref[pl.ds(1 + b * heads + j, 1), :]
            m_new, l_new, o_new = attend(q_ref[rows], j, bufs[b][...].reshape(LOCAL, 2 * width), same)
            m_old = m_acc[rows]
            mn = jnp.maximum(m_old, m_new)
            keep_old = jnp.exp(m_old - mn)
            keep_new = jnp.exp(m_new - mn)
            pick = o_lane == j
            m_acc[rows] = jnp.where(pick, mn, m_old)
            l_acc[rows] = jnp.where(pick, l_acc[rows] * keep_old + l_new * keep_new, l_acc[rows])
            o_acc[rows] = jnp.where(pick, o_acc[rows] * keep_old + o_new * keep_new, o_acc[rows])
            return carry

        lax.fori_loop(0, heads, branch, 0)

    lax.fori_loop(0, 1, branch0, 0)
    pl.semaphore_wait(barrier, halves + ys - 1)
    start_pushes()
    lax.fori_loop(1, 3, branch0, 0)
    forward(0)
    lax.fori_loop(3, LOCAL // chunk, branch0, 0)
    forward(1)
    later(0)
    forward(2)
    later(1)
    later(2)

    feature = lax.broadcasted_iota(jnp.int32, (8, 256), 1) < heads * HD
    ones = jnp.where(feature, 1.0, 0.0).astype(jnp.float32)
    first_row = lax.broadcasted_iota(jnp.int32, (8, chunk), 0) == 0

    def finish(i, carry):
        rows = pl.ds(pl.multiple_of(i * chunk, chunk), chunk)
        att = o_acc[rows] / l_acc[rows]
        o_acc[rows] = att
        dims = (((1,), (1,)), ((), ()))
        total = lax.dot_general(ones, att, dims, precision=lax.Precision.HIGHEST, preferred_element_type=jnp.float32)
        square = lax.dot_general(ones, att * att, dims, precision=lax.Precision.HIGHEST, preferred_element_type=jnp.float32)
        stats[:, rows] = jnp.where(first_row, total, square)
        return carry

    lax.fori_loop(0, LOCAL // chunk, finish, 0)
    ybuf[hy] = stats[...]
    shares = []
    for o in range(1, ys):
        cp = pltpu.make_async_remote_copy(
            src_ref=stats,
            dst_ref=ybuf.at[hy],
            send_sem=y_send.at[o - 1],
            recv_sem=y_recv.at[0],
            device_id=(me, lax.rem(hy + o, ys)),
            device_id_type=MESH,
        )
        cp.start()
        shares.append(cp)
    arrived = ybuf.at[pl.ds(0, ys - 1)]
    pltpu.make_async_copy(arrived, arrived, y_recv.at[0]).wait()
    for cp in shares:
        cp.wait_send()
    summed = ybuf[0]
    for h in range(1, ys):
        summed = summed + ybuf[h]
    mean = summed[0:1] / D
    var = summed[1:2] / D - mean * mean
    rstd = lax.rsqrt(var + 1e-05)
    pair = jnp.where(lax.broadcasted_iota(jnp.int32, (8, LOCAL), 0) == 0, mean, rstd)
    cols[...] = jnp.transpose(pair)

    def normalize(i, carry):
        rows = pl.ds(pl.multiple_of(i * chunk, chunk), chunk)
        col = cols[rows]
        normed = (o_acc[rows] - col[:, 0:1]) * col[:, 1:2]
        out_ref[rows] = (normed[:, : heads * HD] * gain_ref[...] + bias_ref[...]).astype(out_ref.dtype)
        return carry

    lax.fori_loop(0, LOCAL // chunk, normalize, 0)

    for b, (count, group) in enumerate(BRANCHES):
        pairs = group // 2
        if pairs > 1:
            went = bufs[b].at[pl.ds(0, pairs - 1), side]
            pltpu.make_async_copy(went, went, send_sem.at[b]).wait()
        forwards[b].wait_send()


def per_device(queries, keys, values, slide_lengths, norm_gain, norm_bias):
    heads = queries.shape[0] // HD
    width = heads * HD
    seq = lax.axis_index("seq")
    hy = lax.axis_index("head")
    q = to_token_major(jnp.concatenate([jnp.zeros((SHIFT, LOCAL), queries.dtype), queries]))
    kv = to_token_major(jnp.concatenate([values, keys]))
    kv_lane = jnp.arange(2 * width) % width // HD

    sends = []
    for b, (count, group) in enumerate(BRANCHES):
        starts = [j * 256 + (hy * 64 if b >= 1 else 0) for j in range(heads)]
        chunk = jnp.zeros((count, 2 * width), kv.dtype)
        for j in range(heads):
            piece = lax.dynamic_slice_in_dim(kv, starts[j], count, 0)
            chunk = jnp.where(kv_lane[None, :] == j, piece, chunk)
        sends.append(chunk)

    gain = norm_gain.reshape(1, width)
    bias = norm_bias.reshape(1, width)
    vmem = pl.BlockSpec(memory_space=pltpu.VMEM)
    out = pl.pallas_call(
        attention_kernel,
        out_shape=jax.ShapeDtypeStruct((LOCAL, width), jnp.bfloat16),
        in_specs=[vmem] * 3 + [pl.BlockSpec(memory_space=pltpu.SMEM)] + [vmem] * 2,
        out_specs=vmem,
        scratch_shapes=[
            *[pltpu.VMEM((group // 2, 2, count, 2 * width), jnp.bfloat16) for count, group in BRANCHES],
            pltpu.VMEM((LOCAL, 256), jnp.float32),
            pltpu.VMEM((LOCAL, 256), jnp.float32),
            pltpu.VMEM((LOCAL, 256), jnp.float32),
            pltpu.VMEM((8, LOCAL), jnp.float32),
            pltpu.VMEM((4, 8, LOCAL), jnp.float32),
            pltpu.VMEM((LOCAL, 8), jnp.float32),
            pltpu.VMEM((LOCAL, 8), jnp.int32),
            pltpu.VMEM((16, LOCAL), jnp.int32),
            pltpu.SemaphoreType.DMA((3,)),
            pltpu.SemaphoreType.DMA((3,)),
            pltpu.SemaphoreType.DMA((3,)),
            pltpu.SemaphoreType.DMA((3,)),
            pltpu.SemaphoreType.DMA((3,)),
            pltpu.SemaphoreType.DMA((3,)),
            pltpu.SemaphoreType.DMA((1,)),
        ],
        compiler_params=pltpu.CompilerParams(
            collective_id=0, has_side_effects=True, vmem_limit_bytes=60 * 1024 * 1024
        ),
    )(q, kv, jnp.concatenate(sends), slide_lengths, gain, bias)
    return from_token_major(out)


def solution(mesh):
    placed = (P("head", "seq"),) * 3 + (P(), P("head"), P("head"))
    return jax.shard_map(
        per_device, mesh=mesh, in_specs=placed, out_specs=P("head", "seq"), check_vma=False
    )
```

```python
import math

import jax
import jax.numpy as jnp
from jax import lax
from jax.experimental import pallas as pl
from jax.experimental.pallas import tpu as pltpu
from jax.sharding import PartitionSpec as P

D = 768
HD = 48
SEG = 1024
LOCAL = 1024
MESH = pl.DeviceIdType.MESH
BRANCHES = ((256, 4), (64, 16), (16, 64))
SHIFT = 64


def to_token_major(x):
    f = x.shape[0]
    x = x.reshape(f, 16, 4, 4, 4)
    x = jnp.transpose(x, (4, 3, 2, 1, 0))
    return x.reshape(LOCAL, f)


def from_token_major(x):
    f = x.shape[1]
    x = x.reshape(4, 4, 4, 16, f)
    x = jnp.transpose(x, (4, 3, 2, 1, 0))
    return x.reshape(f, LOCAL)


def pos_of(device, index):
    local = 64 * (index % 16) + 16 * (index // 16 % 4) + 4 * (index // 64 % 4) + index // 256
    return device * LOCAL + local


def slide_of(positions, slide_ends):
    return jnp.sum((positions[..., None] >= slide_ends).astype(jnp.int32), axis=-1)


def attention_kernel(
    q_ref, kv_ref, send_ref, len_ref, gain_ref, bias_ref,
    out_ref,
    kv1, kv2, kv3, m_acc, l_acc, o_acc, stats, ybuf, cols, sqcol, sk_ref,
    send_sem, recv_sem, local_sem, fwd_send, fwd_recv, y_send, y_recv,
):
    heads = 4
    me = lax.axis_index("seq")
    hy = lax.axis_index("head")
    devices = lax.axis_size("seq")
    scale = 1.0 / math.sqrt(HD)
    sends = (send_ref.at[pl.ds(0, 256)], send_ref.at[pl.ds(256, 64)], send_ref.at[pl.ds(320, 16)])
    bufs = (kv1, kv2, kv3)
    width = heads * HD

    barrier = pltpu.get_barrier_semaphore()

    side = me % 2
    halves = devices // 2

    def greet(o, carry):
        peer = 2 * lax.rem(me // 2 + o, halves) + side
        pl.semaphore_signal(barrier, inc=1, device_id=(peer, hy), device_id_type=MESH)
        return carry

    lax.fori_loop(1, halves, greet, 0)
    pl.semaphore_signal(barrier, inc=1, device_id=(me + 1 - 2 * side, hy), device_id_type=MESH)
    ys = lax.axis_size("head")
    for o in range(1, ys):
        pl.semaphore_signal(barrier, inc=1, device_id=(me, lax.rem(hy + o, ys)), device_id_type=MESH)

    row = lax.broadcasted_iota(jnp.int32, (16, LOCAL), 0)
    column = lax.broadcasted_iota(jnp.int32, (16, LOCAL), 1)
    shift = jnp.where(row == 0, 10, jnp.where(row <= 4, 8, jnp.where(row <= 8, 6, 4)))
    group = jnp.where(row == 0, 1, jnp.where(row <= 4, 4, jnp.where(row <= 8, 16, 64)))
    offset = jnp.where(row == 0, 0, ((row - 1) & 3) * 256 + jnp.where(row >= 5, hy * 64, 0))
    device = me - (me & (group - 1)) + (column >> shift)
    index = offset + (column & ((1 << shift) - 1))
    local = ((index & 15) << 6) + (((index >> 4) & 3) << 4) + (((index >> 6) & 3) << 2) + (index >> 8)
    position = device * LOCAL + local

    def count_ends(k, carry):
        end, acc = carry
        end = end + len_ref[k]
        return end, acc + jnp.where(position >= end, 1, 0)

    _, slide = lax.fori_loop(0, len_ref.shape[0], count_ends, (jnp.int32(0), jnp.zeros((16, LOCAL), jnp.int32)))
    sk_ref[...] = slide
    sqcol[...] = jnp.transpose(slide[0:8])

    def slot(b, half, pair):
        return bufs[b].at[pair, half]

    sibling = me + 1 - 2 * (me % 2)
    locals_ = []
    for b, (count, group) in enumerate(BRANCHES):
        member = lax.rem(me, group)
        cp = pltpu.make_async_copy(sends[b], slot(b, side, member // 2), local_sem.at[b])
        cp.start()
        locals_.append(cp)
    def start_pushes():
        for b, (count, group) in enumerate(BRANCHES):
            member = lax.rem(me, group)
            first = me - member
            pairs = group // 2

            def push(o, carry, b=b, pairs=pairs, member=member, first=first):
                target = first + 2 * lax.rem(member // 2 + o, pairs) + side
                pltpu.make_async_remote_copy(
                    src_ref=sends[b],
                    dst_ref=slot(b, side, member // 2),
                    send_sem=send_sem.at[b],
                    recv_sem=recv_sem.at[b],
                    device_id=(target, hy),
                    device_id_type=MESH,
                ).start()
                return carry

            lax.fori_loop(1, pairs, push, 0)


    q_lane = (lax.broadcasted_iota(jnp.int32, (1, 256), 1) - SHIFT) // HD
    o_lane = lax.broadcasted_iota(jnp.int32, (1, 256), 1) // HD

    def attend(q, j, kv, same):
        qz = jnp.where(q_lane == j, q, jnp.zeros_like(q))
        s = lax.dot_general(qz, kv[:, 128:], (((1,), (1,)), ((), ())), preferred_element_type=jnp.float32)
        s = jnp.where(same, s, -1e30)
        m = jnp.max(s, axis=-1, keepdims=True)
        p = jnp.exp((s - m) * scale)
        l = jnp.sum(p, axis=-1, keepdims=True)
        o = jnp.dot(p.astype(jnp.bfloat16), kv[:, :256], preferred_element_type=jnp.float32)
        return m * scale, l, o

    chunk = 256

    def branch0(i, carry):
        rows = pl.ds(pl.multiple_of(i * chunk, chunk), chunk)
        q = q_ref[rows]
        kv = kv_ref[...]
        same = sqcol[rows, 0:1] == sk_ref[pl.ds(0, 1), :]
        mm = ll = oo = None
        for j in range(heads):
            m, l, o = attend(q, j, kv, same)
            if j == 0:
                mm = jnp.broadcast_to(m, (chunk, 256))
                ll = jnp.broadcast_to(l, (chunk, 256))
                oo = o
            else:
                pick = o_lane == j
                mm = jnp.where(pick, m, mm)
                ll = jnp.where(pick, l, ll)
                oo = jnp.where(pick, o, oo)
        m_acc[rows] = mm
        l_acc[rows] = ll
        o_acc[rows] = oo
        return carry

    forwards = []

    def forward(b):
        count, group = BRANCHES[b]
        pairs = group // 2
        locals_[b].wait()
        if pairs > 1:
            got = bufs[b].at[pl.ds(0, pairs - 1), side]
            pltpu.make_async_copy(got, got, recv_sem.at[b]).wait()
        cp = pltpu.make_async_remote_copy(
            src_ref=bufs[b].at[:, side],
            dst_ref=bufs[b].at[:, side],
            send_sem=fwd_send.at[b],
            recv_sem=fwd_recv.at[b],
            device_id=(sibling, hy),
            device_id_type=MESH,
        )
        cp.start()
        forwards.append(cp)

    def later(b):
        count, group = BRANCHES[b]
        other = bufs[b].at[:, 1 - side]
        pltpu.make_async_copy(other, other, fwd_recv.at[b]).wait()

        def branch(j, carry):
            start = j * 256 + (hy * 64 if b >= 1 else 0)
            rows = pl.ds(pl.multiple_of(start, 16), count)
            same = sqcol[rows, 0:1] == sk_ref[pl.ds(1 + b * heads + j, 1), :]
            m_new, l_new, o_new = attend(q_ref[rows], j, bufs[b][...].reshape(LOCAL, 2 * width), same)
            m_old = m_acc[rows]
            mn = jnp.maximum(m_old, m_new)
            keep_old = jnp.exp(m_old - mn)
            keep_new = jnp.exp(m_new - mn)
            pick = o_lane == j
            m_acc[rows] = jnp.where(pick, mn, m_old)
            l_acc[rows] = jnp.where(pick, l_acc[rows] * keep_old + l_new * keep_new, l_acc[rows])
            o_acc[rows] = jnp.where(pick, o_acc[rows] * keep_old + o_new * keep_new, o_acc[rows])
            return carry

        lax.fori_loop(0, heads, branch, 0)

    lax.fori_loop(0, 1, branch0, 0)
    pl.semaphore_wait(barrier, halves + ys - 1)
    start_pushes()
    lax.fori_loop(1, LOCAL // chunk, branch0, 0)
    forward(0)
    forward(1)
    later(0)
    forward(2)
    later(1)
    later(2)

    feature = lax.broadcasted_iota(jnp.int32, (8, 256), 1) < heads * HD
    ones = jnp.where(feature, 1.0, 0.0).astype(jnp.float32)
    first_row = lax.broadcasted_iota(jnp.int32, (8, chunk), 0) == 0

    def finish(i, carry):
        rows = pl.ds(pl.multiple_of(i * chunk, chunk), chunk)
        att = o_acc[rows] / l_acc[rows]
        o_acc[rows] = att
        dims = (((1,), (1,)), ((), ()))
        total = lax.dot_general(ones, att, dims, precision=lax.Precision.HIGHEST, preferred_element_type=jnp.float32)
        square = lax.dot_general(ones, att * att, dims, precision=lax.Precision.HIGHEST, preferred_element_type=jnp.float32)
        stats[:, rows] = jnp.where(first_row, total, square)
        return carry

    lax.fori_loop(0, LOCAL // chunk, finish, 0)
    ybuf[hy] = stats[...]
    shares = []
    for o in range(1, ys):
        cp = pltpu.make_async_remote_copy(
            src_ref=stats,
            dst_ref=ybuf.at[hy],
            send_sem=y_send.at[o - 1],
            recv_sem=y_recv.at[0],
            device_id=(me, lax.rem(hy + o, ys)),
            device_id_type=MESH,
        )
        cp.start()
        shares.append(cp)
    arrived = ybuf.at[pl.ds(0, ys - 1)]
    pltpu.make_async_copy(arrived, arrived, y_recv.at[0]).wait()
    for cp in shares:
        cp.wait_send()
    summed = ybuf[0]
    for h in range(1, ys):
        summed = summed + ybuf[h]
    mean = summed[0:1] / D
    var = summed[1:2] / D - mean * mean
    rstd = lax.rsqrt(var + 1e-05)
    pair = jnp.where(lax.broadcasted_iota(jnp.int32, (8, LOCAL), 0) == 0, mean, rstd)
    cols[...] = jnp.transpose(pair)

    def normalize(i, carry):
        rows = pl.ds(pl.multiple_of(i * chunk, chunk), chunk)
        col = cols[rows]
        normed = (o_acc[rows] - col[:, 0:1]) * col[:, 1:2]
        out_ref[rows] = (normed[:, : heads * HD] * gain_ref[...] + bias_ref[...]).astype(out_ref.dtype)
        return carry

    lax.fori_loop(0, LOCAL // chunk, normalize, 0)

    for b, (count, group) in enumerate(BRANCHES):
        pairs = group // 2
        if pairs > 1:
            went = bufs[b].at[pl.ds(0, pairs - 1), side]
            pltpu.make_async_copy(went, went, send_sem.at[b]).wait()
        forwards[b].wait_send()


def per_device(queries, keys, values, slide_lengths, norm_gain, norm_bias):
    heads = queries.shape[0] // HD
    width = heads * HD
    seq = lax.axis_index("seq")
    hy = lax.axis_index("head")
    q = to_token_major(jnp.concatenate([jnp.zeros((SHIFT, LOCAL), queries.dtype), queries]))
    kv = to_token_major(jnp.concatenate([values, keys]))
    kv_lane = jnp.arange(2 * width) % width // HD

    sends = []
    for b, (count, group) in enumerate(BRANCHES):
        starts = [j * 256 + (hy * 64 if b >= 1 else 0) for j in range(heads)]
        chunk = jnp.zeros((count, 2 * width), kv.dtype)
        for j in range(heads):
            piece = lax.dynamic_slice_in_dim(kv, starts[j], count, 0)
            chunk = jnp.where(kv_lane[None, :] == j, piece, chunk)
        sends.append(chunk)

    gain = norm_gain.reshape(1, width)
    bias = norm_bias.reshape(1, width)
    vmem = pl.BlockSpec(memory_space=pltpu.VMEM)
    out = pl.pallas_call(
        attention_kernel,
        out_shape=jax.ShapeDtypeStruct((LOCAL, width), jnp.bfloat16),
        in_specs=[vmem] * 3 + [pl.BlockSpec(memory_space=pltpu.SMEM)] + [vmem] * 2,
        out_specs=vmem,
        scratch_shapes=[
            *[pltpu.VMEM((group // 2, 2, count, 2 * width), jnp.bfloat16) for count, group in BRANCHES],
            pltpu.VMEM((LOCAL, 256), jnp.float32),
            pltpu.VMEM((LOCAL, 256), jnp.float32),
            pltpu.VMEM((LOCAL, 256), jnp.float32),
            pltpu.VMEM((8, LOCAL), jnp.float32),
            pltpu.VMEM((4, 8, LOCAL), jnp.float32),
            pltpu.VMEM((LOCAL, 8), jnp.float32),
            pltpu.VMEM((LOCAL, 8), jnp.int32),
            pltpu.VMEM((16, LOCAL), jnp.int32),
            pltpu.SemaphoreType.DMA((3,)),
            pltpu.SemaphoreType.DMA((3,)),
            pltpu.SemaphoreType.DMA((3,)),
            pltpu.SemaphoreType.DMA((3,)),
            pltpu.SemaphoreType.DMA((3,)),
            pltpu.SemaphoreType.DMA((3,)),
            pltpu.SemaphoreType.DMA((1,)),
        ],
        compiler_params=pltpu.CompilerParams(
            collective_id=0, has_side_effects=True, vmem_limit_bytes=60 * 1024 * 1024
        ),
    )(q, kv, jnp.concatenate(sends), slide_lengths, gain, bias)
    return from_token_major(out)


def solution(mesh):
    placed = (P("head", "seq"),) * 3 + (P(), P("head"), P("head"))
    return jax.shard_map(
        per_device, mesh=mesh, in_specs=placed, out_specs=P("head", "seq"), check_vma=False
    )
```

```python
import math

import jax
import jax.numpy as jnp
from jax import lax
from jax.experimental import pallas as pl
from jax.experimental.pallas import tpu as pltpu
from jax.sharding import PartitionSpec as P

D = 768
HD = 48
SEG = 1024
LOCAL = 1024
MESH = pl.DeviceIdType.MESH
BRANCHES = ((256, 4), (64, 16), (16, 64))
SHIFT = 64


def to_token_major(x):
    f = x.shape[0]
    x = x.reshape(f, 16, 4, 4, 4)
    x = jnp.transpose(x, (4, 3, 2, 1, 0))
    return x.reshape(LOCAL, f)


def from_token_major(x):
    f = x.shape[1]
    x = x.reshape(4, 4, 4, 16, f)
    x = jnp.transpose(x, (4, 3, 2, 1, 0))
    return x.reshape(f, LOCAL)


def pos_of(device, index):
    local = 64 * (index % 16) + 16 * (index // 16 % 4) + 4 * (index // 64 % 4) + index // 256
    return device * LOCAL + local


def slide_of(positions, slide_ends):
    return jnp.sum((positions[..., None] >= slide_ends).astype(jnp.int32), axis=-1)


def attention_kernel(
    q_ref, kv_ref, send_ref, len_ref, gain_ref, bias_ref,
    out_ref,
    kv1, kv2, kv3, m_acc, l_acc, o_acc, stats, ybuf, cols, sqcol, sk_ref,
    send_sem, recv_sem, local_sem, fwd_send, fwd_recv, y_send, y_recv,
):
    heads = 4
    me = lax.axis_index("seq")
    hy = lax.axis_index("head")
    devices = lax.axis_size("seq")
    scale = 1.0 / math.sqrt(HD)
    sends = (send_ref.at[pl.ds(0, 256)], send_ref.at[pl.ds(256, 64)], send_ref.at[pl.ds(320, 16)])
    bufs = (kv1, kv2, kv3)
    width = heads * HD

    barrier = pltpu.get_barrier_semaphore()

    side = me % 2
    halves = devices // 2

    def greet(o, carry):
        peer = 2 * lax.rem(me // 2 + o, halves) + side
        pl.semaphore_signal(barrier, inc=1, device_id=(peer, hy), device_id_type=MESH)
        return carry

    lax.fori_loop(1, halves, greet, 0)
    pl.semaphore_signal(barrier, inc=1, device_id=(me + 1 - 2 * side, hy), device_id_type=MESH)
    ys = lax.axis_size("head")
    for o in range(1, ys):
        pl.semaphore_signal(barrier, inc=1, device_id=(me, lax.rem(hy + o, ys)), device_id_type=MESH)

    row = lax.broadcasted_iota(jnp.int32, (16, LOCAL), 0)
    column = lax.broadcasted_iota(jnp.int32, (16, LOCAL), 1)
    shift = jnp.where(row == 0, 10, jnp.where(row <= 4, 8, jnp.where(row <= 8, 6, 4)))
    group = jnp.where(row == 0, 1, jnp.where(row <= 4, 4, jnp.where(row <= 8, 16, 64)))
    offset = jnp.where(row == 0, 0, ((row - 1) & 3) * 256 + jnp.where(row >= 5, hy * 64, 0))
    device = me - (me & (group - 1)) + (column >> shift)
    index = offset + (column & ((1 << shift) - 1))
    local = ((index & 15) << 6) + (((index >> 4) & 3) << 4) + (((index >> 6) & 3) << 2) + (index >> 8)
    position = device * LOCAL + local

    def count_ends(k, carry):
        end, acc = carry
        end = end + len_ref[k]
        return end, acc + jnp.where(position >= end, 1, 0)

    _, slide = lax.fori_loop(0, len_ref.shape[0], count_ends, (jnp.int32(0), jnp.zeros((16, LOCAL), jnp.int32)))
    sk_ref[...] = slide
    sqcol[...] = jnp.transpose(slide[0:8])

    def slot(b, half, pair):
        return bufs[b].at[pair, half]

    sibling = me + 1 - 2 * (me % 2)
    locals_ = []
    for b, (count, group) in enumerate(BRANCHES):
        member = lax.rem(me, group)
        cp = pltpu.make_async_copy(sends[b], slot(b, side, member // 2), local_sem.at[b])
        cp.start()
        locals_.append(cp)
    def start_pushes():
        for b, (count, group) in enumerate(BRANCHES):
            member = lax.rem(me, group)
            first = me - member
            pairs = group // 2

            def push(o, carry, b=b, pairs=pairs, member=member, first=first):
                target = first + 2 * lax.rem(member // 2 + o, pairs) + side
                pltpu.make_async_remote_copy(
                    src_ref=sends[b],
                    dst_ref=slot(b, side, member // 2),
                    send_sem=send_sem.at[b],
                    recv_sem=recv_sem.at[b],
                    device_id=(target, hy),
                    device_id_type=MESH,
                ).start()
                return carry

            lax.fori_loop(1, pairs, push, 0)


    q_lane = (lax.broadcasted_iota(jnp.int32, (1, 256), 1) - SHIFT) // HD
    o_lane = lax.broadcasted_iota(jnp.int32, (1, 256), 1) // HD

    def attend(q, j, kv, same):
        qz = jnp.where(q_lane == j, q, jnp.zeros_like(q))
        s = lax.dot_general(qz, kv[:, 128:], (((1,), (1,)), ((), ())), preferred_element_type=jnp.float32)
        s = jnp.where(same, s, -1e30)
        m = jnp.max(s, axis=-1, keepdims=True)
        p = jnp.exp((s - m) * scale)
        l = jnp.sum(p, axis=-1, keepdims=True)
        o = jnp.dot(p.astype(jnp.bfloat16), kv[:, :256], preferred_element_type=jnp.float32)
        return m * scale, l, o

    chunk = 256

    def branch0(i, carry):
        rows = pl.ds(pl.multiple_of(i * chunk, chunk), chunk)
        q = q_ref[rows]
        kv = kv_ref[...]
        same = sqcol[rows, 0:1] == sk_ref[pl.ds(0, 1), :]
        mm = ll = oo = None
        for j in range(heads):
            m, l, o = attend(q, j, kv, same)
            if j == 0:
                mm = jnp.broadcast_to(m, (chunk, 256))
                ll = jnp.broadcast_to(l, (chunk, 256))
                oo = o
            else:
                pick = o_lane == j
                mm = jnp.where(pick, m, mm)
                ll = jnp.where(pick, l, ll)
                oo = jnp.where(pick, o, oo)
        m_acc[rows] = mm
        l_acc[rows] = ll
        o_acc[rows] = oo
        return carry

    forwards = []

    def forward(b):
        count, group = BRANCHES[b]
        pairs = group // 2
        locals_[b].wait()
        if pairs > 1:
            got = bufs[b].at[pl.ds(0, pairs - 1), side]
            pltpu.make_async_copy(got, got, recv_sem.at[b]).wait()
        cp = pltpu.make_async_remote_copy(
            src_ref=bufs[b].at[:, side],
            dst_ref=bufs[b].at[:, side],
            send_sem=fwd_send.at[b],
            recv_sem=fwd_recv.at[b],
            device_id=(sibling, hy),
            device_id_type=MESH,
        )
        cp.start()
        forwards.append(cp)

    def later(b):
        count, group = BRANCHES[b]
        other = bufs[b].at[:, 1 - side]
        pltpu.make_async_copy(other, other, fwd_recv.at[b]).wait()

        def branch(j, carry):
            start = j * 256 + (hy * 64 if b >= 1 else 0)
            rows = pl.ds(pl.multiple_of(start, 16), count)
            same = sqcol[rows, 0:1] == sk_ref[pl.ds(1 + b * heads + j, 1), :]
            m_new, l_new, o_new = attend(q_ref[rows], j, bufs[b][...].reshape(LOCAL, 2 * width), same)
            m_old = m_acc[rows]
            mn = jnp.maximum(m_old, m_new)
            keep_old = jnp.exp(m_old - mn)
            keep_new = jnp.exp(m_new - mn)
            pick = o_lane == j
            m_acc[rows] = jnp.where(pick, mn, m_old)
            l_acc[rows] = jnp.where(pick, l_acc[rows] * keep_old + l_new * keep_new, l_acc[rows])
            o_acc[rows] = jnp.where(pick, o_acc[rows] * keep_old + o_new * keep_new, o_acc[rows])
            return carry

        lax.fori_loop(0, heads, branch, 0)

    lax.fori_loop(0, 1, branch0, 0)
    pl.semaphore_wait(barrier, halves + ys - 1)
    start_pushes()
    lax.fori_loop(1, LOCAL // chunk, branch0, 0)
    forward(0)
    later(0)
    forward(1)
    forward(2)
    later(1)
    later(2)

    feature = lax.broadcasted_iota(jnp.int32, (8, 256), 1) < heads * HD
    ones = jnp.where(feature, 1.0, 0.0).astype(jnp.float32)
    first_row = lax.broadcasted_iota(jnp.int32, (8, chunk), 0) == 0

    def finish(i, carry):
        rows = pl.ds(pl.multiple_of(i * chunk, chunk), chunk)
        att = o_acc[rows] / l_acc[rows]
        o_acc[rows] = att
        dims = (((1,), (1,)), ((), ()))
        total = lax.dot_general(ones, att, dims, precision=lax.Precision.HIGHEST, preferred_element_type=jnp.float32)
        square = lax.dot_general(ones, att * att, dims, precision=lax.Precision.HIGHEST, preferred_element_type=jnp.float32)
        stats[:, rows] = jnp.where(first_row, total, square)
        return carry

    lax.fori_loop(0, LOCAL // chunk, finish, 0)
    ybuf[hy] = stats[...]
    shares = []
    for o in range(1, ys):
        cp = pltpu.make_async_remote_copy(
            src_ref=stats,
            dst_ref=ybuf.at[hy],
            send_sem=y_send.at[o - 1],
            recv_sem=y_recv.at[0],
            device_id=(me, lax.rem(hy + o, ys)),
            device_id_type=MESH,
        )
        cp.start()
        shares.append(cp)
    arrived = ybuf.at[pl.ds(0, ys - 1)]
    pltpu.make_async_copy(arrived, arrived, y_recv.at[0]).wait()
    for cp in shares:
        cp.wait_send()
    summed = ybuf[0]
    for h in range(1, ys):
        summed = summed + ybuf[h]
    mean = summed[0:1] / D
    var = summed[1:2] / D - mean * mean
    rstd = lax.rsqrt(var + 1e-05)
    pair = jnp.where(lax.broadcasted_iota(jnp.int32, (8, LOCAL), 0) == 0, mean, rstd)
    cols[...] = jnp.transpose(pair)

    def normalize(i, carry):
        rows = pl.ds(pl.multiple_of(i * chunk, chunk), chunk)
        col = cols[rows]
        normed = (o_acc[rows] - col[:, 0:1]) * col[:, 1:2]
        out_ref[rows] = (normed[:, : heads * HD] * gain_ref[...] + bias_ref[...]).astype(out_ref.dtype)
        return carry

    lax.fori_loop(0, LOCAL // chunk, normalize, 0)

    for b, (count, group) in enumerate(BRANCHES):
        pairs = group // 2
        if pairs > 1:
            went = bufs[b].at[pl.ds(0, pairs - 1), side]
            pltpu.make_async_copy(went, went, send_sem.at[b]).wait()
        forwards[b].wait_send()


def per_device(queries, keys, values, slide_lengths, norm_gain, norm_bias):
    heads = queries.shape[0] // HD
    width = heads * HD
    seq = lax.axis_index("seq")
    hy = lax.axis_index("head")
    q = to_token_major(jnp.concatenate([jnp.zeros((SHIFT, LOCAL), queries.dtype), queries]))
    kv = to_token_major(jnp.concatenate([values, keys]))
    kv_lane = jnp.arange(2 * width) % width // HD

    sends = []
    for b, (count, group) in enumerate(BRANCHES):
        starts = [j * 256 + (hy * 64 if b >= 1 else 0) for j in range(heads)]
        chunk = jnp.zeros((count, 2 * width), kv.dtype)
        for j in range(heads):
            piece = lax.dynamic_slice_in_dim(kv, starts[j], count, 0)
            chunk = jnp.where(kv_lane[None, :] == j, piece, chunk)
        sends.append(chunk)

    gain = norm_gain.reshape(1, width)
    bias = norm_bias.reshape(1, width)
    vmem = pl.BlockSpec(memory_space=pltpu.VMEM)
    out = pl.pallas_call(
        attention_kernel,
        out_shape=jax.ShapeDtypeStruct((LOCAL, width), jnp.bfloat16),
        in_specs=[vmem] * 3 + [pl.BlockSpec(memory_space=pltpu.SMEM)] + [vmem] * 2,
        out_specs=vmem,
        scratch_shapes=[
            *[pltpu.VMEM((group // 2, 2, count, 2 * width), jnp.bfloat16) for count, group in BRANCHES],
            pltpu.VMEM((LOCAL, 256), jnp.float32),
            pltpu.VMEM((LOCAL, 256), jnp.float32),
            pltpu.VMEM((LOCAL, 256), jnp.float32),
            pltpu.VMEM((8, LOCAL), jnp.float32),
            pltpu.VMEM((4, 8, LOCAL), jnp.float32),
            pltpu.VMEM((LOCAL, 8), jnp.float32),
            pltpu.VMEM((LOCAL, 8), jnp.int32),
            pltpu.VMEM((16, LOCAL), jnp.int32),
            pltpu.SemaphoreType.DMA((3,)),
            pltpu.SemaphoreType.DMA((3,)),
            pltpu.SemaphoreType.DMA((3,)),
            pltpu.SemaphoreType.DMA((3,)),
            pltpu.SemaphoreType.DMA((3,)),
            pltpu.SemaphoreType.DMA((3,)),
            pltpu.SemaphoreType.DMA((1,)),
        ],
        compiler_params=pltpu.CompilerParams(
            collective_id=0, has_side_effects=True, vmem_limit_bytes=60 * 1024 * 1024
        ),
    )(q, kv, jnp.concatenate(sends), slide_lengths, gain, bias)
    return from_token_major(out)


def solution(mesh):
    placed = (P("head", "seq"),) * 3 + (P(), P("head"), P("head"))
    return jax.shard_map(
        per_device, mesh=mesh, in_specs=placed, out_specs=P("head", "seq"), check_vma=False
    )
```

```python
import math

import jax
import jax.numpy as jnp
from jax import lax
from jax.experimental import pallas as pl
from jax.experimental.pallas import tpu as pltpu
from jax.sharding import PartitionSpec as P

D = 768
HD = 48
SEG = 1024
LOCAL = 1024
MESH = pl.DeviceIdType.MESH
BRANCHES = ((256, 4), (64, 16), (16, 64))
SHIFT = 64


def to_token_major(x):
    f = x.shape[0]
    x = x.reshape(f, 16, 4, 4, 4)
    x = jnp.transpose(x, (4, 3, 2, 1, 0))
    return x.reshape(LOCAL, f)


def from_token_major(x):
    f = x.shape[1]
    x = x.reshape(4, 4, 4, 16, f)
    x = jnp.transpose(x, (4, 3, 2, 1, 0))
    return x.reshape(f, LOCAL)


def pos_of(device, index):
    local = 64 * (index % 16) + 16 * (index // 16 % 4) + 4 * (index // 64 % 4) + index // 256
    return device * LOCAL + local


def slide_of(positions, slide_ends):
    return jnp.sum((positions[..., None] >= slide_ends).astype(jnp.int32), axis=-1)


def attention_kernel(
    q_ref, kv_ref, send_ref, len_ref, gain_ref, bias_ref,
    out_ref,
    kv1, kv2, kv3, m_acc, l_acc, o_acc, stats, ybuf, cols, sqcol, sk_ref,
    send_sem, recv_sem, local_sem, fwd_send, fwd_recv, y_send, y_recv,
):
    heads = 4
    me = lax.axis_index("seq")
    hy = lax.axis_index("head")
    devices = lax.axis_size("seq")
    scale = 1.0 / math.sqrt(HD)
    sends = (send_ref.at[pl.ds(0, 256)], send_ref.at[pl.ds(256, 64)], send_ref.at[pl.ds(320, 16)])
    bufs = (kv1, kv2, kv3)
    width = heads * HD

    barrier = pltpu.get_barrier_semaphore()

    side = me % 2
    halves = devices // 2

    def greet(o, carry):
        peer = 2 * lax.rem(me // 2 + o, halves) + side
        pl.semaphore_signal(barrier, inc=1, device_id=(peer, hy), device_id_type=MESH)
        return carry

    lax.fori_loop(1, halves, greet, 0)
    pl.semaphore_signal(barrier, inc=1, device_id=(me + 1 - 2 * side, hy), device_id_type=MESH)
    ys = lax.axis_size("head")
    for o in range(1, ys):
        pl.semaphore_signal(barrier, inc=1, device_id=(me, lax.rem(hy + o, ys)), device_id_type=MESH)

    row = lax.broadcasted_iota(jnp.int32, (16, LOCAL), 0)
    column = lax.broadcasted_iota(jnp.int32, (16, LOCAL), 1)
    shift = jnp.where(row == 0, 10, jnp.where(row <= 4, 8, jnp.where(row <= 8, 6, 4)))
    group = jnp.where(row == 0, 1, jnp.where(row <= 4, 4, jnp.where(row <= 8, 16, 64)))
    offset = jnp.where(row == 0, 0, ((row - 1) & 3) * 256 + jnp.where(row >= 5, hy * 64, 0))
    device = me - (me & (group - 1)) + (column >> shift)
    index = offset + (column & ((1 << shift) - 1))
    local = ((index & 15) << 6) + (((index >> 4) & 3) << 4) + (((index >> 6) & 3) << 2) + (index >> 8)
    position = device * LOCAL + local

    def count_ends(k, carry):
        end, acc = carry
        end = end + len_ref[k]
        return end, acc + jnp.where(position >= end, 1, 0)

    _, slide = lax.fori_loop(0, len_ref.shape[0], count_ends, (jnp.int32(0), jnp.zeros((16, LOCAL), jnp.int32)))
    sk_ref[...] = slide
    sqcol[...] = jnp.transpose(slide[0:8])

    def slot(b, half, pair):
        return bufs[b].at[pair, half]

    sibling = me + 1 - 2 * (me % 2)
    locals_ = []
    for b, (count, group) in enumerate(BRANCHES):
        member = lax.rem(me, group)
        cp = pltpu.make_async_copy(sends[b], slot(b, side, member // 2), local_sem.at[b])
        cp.start()
        locals_.append(cp)
    def start_pushes():
        for b, (count, group) in enumerate(BRANCHES):
            member = lax.rem(me, group)
            first = me - member
            pairs = group // 2

            def push(o, carry, b=b, pairs=pairs, member=member, first=first):
                target = first + 2 * lax.rem(member // 2 + o, pairs) + side
                pltpu.make_async_remote_copy(
                    src_ref=sends[b],
                    dst_ref=slot(b, side, member // 2),
                    send_sem=send_sem.at[b],
                    recv_sem=recv_sem.at[b],
                    device_id=(target, hy),
                    device_id_type=MESH,
                ).start()
                return carry

            lax.fori_loop(1, pairs, push, 0)


    q_lane = (lax.broadcasted_iota(jnp.int32, (1, 256), 1) - SHIFT) // HD
    o_lane = lax.broadcasted_iota(jnp.int32, (1, 256), 1) // HD

    def attend(q, j, kv, same):
        qz = jnp.where(q_lane == j, q, jnp.zeros_like(q))
        s = lax.dot_general(qz, kv[:, 128:], (((1,), (1,)), ((), ())), preferred_element_type=jnp.float32)
        s = jnp.where(same, s, -1e30)
        m = jnp.max(s, axis=-1, keepdims=True)
        p = jnp.exp((s - m) * scale)
        l = jnp.sum(p, axis=-1, keepdims=True)
        o = jnp.dot(p.astype(jnp.bfloat16), kv[:, :256], preferred_element_type=jnp.float32)
        return m * scale, l, o

    chunk = 256

    def branch0(i, carry):
        rows = pl.ds(pl.multiple_of(i * chunk, chunk), chunk)
        q = q_ref[rows]
        kv = kv_ref[...]
        same = sqcol[rows, 0:1] == sk_ref[pl.ds(0, 1), :]
        mm = ll = oo = None
        for j in range(heads):
            m, l, o = attend(q, j, kv, same)
            if j == 0:
                mm = jnp.broadcast_to(m, (chunk, 256))
                ll = jnp.broadcast_to(l, (chunk, 256))
                oo = o
            else:
                pick = o_lane == j
                mm = jnp.where(pick, m, mm)
                ll = jnp.where(pick, l, ll)
                oo = jnp.where(pick, o, oo)
        m_acc[rows] = mm
        l_acc[rows] = ll
        o_acc[rows] = oo
        return carry

    forwards = []

    def forward(b):
        count, group = BRANCHES[b]
        pairs = group // 2
        locals_[b].wait()
        if pairs > 1:
            got = bufs[b].at[pl.ds(0, pairs - 1), side]
            pltpu.make_async_copy(got, got, recv_sem.at[b]).wait()
        cp = pltpu.make_async_remote_copy(
            src_ref=bufs[b].at[:, side],
            dst_ref=bufs[b].at[:, side],
            send_sem=fwd_send.at[b],
            recv_sem=fwd_recv.at[b],
            device_id=(sibling, hy),
            device_id_type=MESH,
        )
        cp.start()
        forwards.append(cp)

    def later(b):
        count, group = BRANCHES[b]
        other = bufs[b].at[:, 1 - side]
        pltpu.make_async_copy(other, other, fwd_recv.at[b]).wait()

        def branch(j, carry):
            start = j * 256 + (hy * 64 if b >= 1 else 0)
            rows = pl.ds(pl.multiple_of(start, 16), count)
            same = sqcol[rows, 0:1] == sk_ref[pl.ds(1 + b * heads + j, 1), :]
            m_new, l_new, o_new = attend(q_ref[rows], j, bufs[b][...].reshape(LOCAL, 2 * width), same)
            m_old = m_acc[rows]
            mn = jnp.maximum(m_old, m_new)
            keep_old = jnp.exp(m_old - mn)
            keep_new = jnp.exp(m_new - mn)
            pick = o_lane == j
            m_acc[rows] = jnp.where(pick, mn, m_old)
            l_acc[rows] = jnp.where(pick, l_acc[rows] * keep_old + l_new * keep_new, l_acc[rows])
            o_acc[rows] = jnp.where(pick, o_acc[rows] * keep_old + o_new * keep_new, o_acc[rows])
            return carry

        lax.fori_loop(0, heads, branch, 0)

    lax.fori_loop(0, 1, branch0, 0)
    pl.semaphore_wait(barrier, halves + ys - 1)
    start_pushes()
    lax.fori_loop(1, LOCAL // chunk, branch0, 0)
    forward(0)
    later(0)
    forward(1)
    forward(2)
    later(1)
    later(2)

    feature = lax.broadcasted_iota(jnp.int32, (8, 256), 1) < heads * HD
    ones = jnp.where(feature, 1.0, 0.0).astype(jnp.float32)
    first_row = lax.broadcasted_iota(jnp.int32, (8, chunk), 0) == 0

    def finish(i, carry):
        rows = pl.ds(pl.multiple_of(i * chunk, chunk), chunk)
        att = o_acc[rows] / l_acc[rows]
        o_acc[rows] = att
        dims = (((1,), (1,)), ((), ()))
        total = lax.dot_general(ones, att, dims, precision=lax.Precision.HIGHEST, preferred_element_type=jnp.float32)
        square = lax.dot_general(ones, att * att, dims, precision=lax.Precision.HIGHEST, preferred_element_type=jnp.float32)
        stats[:, rows] = jnp.where(first_row, total, square)
        return carry

    lax.fori_loop(0, LOCAL // chunk, finish, 0)
    ybuf[hy] = stats[...]
    shares = []
    for o in range(1, ys):
        cp = pltpu.make_async_remote_copy(
            src_ref=stats.at[pl.ds(0, 2)],
            dst_ref=ybuf.at[hy, pl.ds(0, 2)],
            send_sem=y_send.at[o - 1],
            recv_sem=y_recv.at[0],
            device_id=(me, lax.rem(hy + o, ys)),
            device_id_type=MESH,
        )
        cp.start()
        shares.append(cp)
    arrived = ybuf.at[pl.ds(0, ys - 1), pl.ds(0, 2)]
    pltpu.make_async_copy(arrived, arrived, y_recv.at[0]).wait()
    for cp in shares:
        cp.wait_send()
    summed = ybuf[0]
    for h in range(1, ys):
        summed = summed + ybuf[h]
    mean = summed[0:1] / D
    var = summed[1:2] / D - mean * mean
    rstd = lax.rsqrt(var + 1e-05)
    pair = jnp.where(lax.broadcasted_iota(jnp.int32, (8, LOCAL), 0) == 0, mean, rstd)
    cols[...] = jnp.transpose(pair)

    def normalize(i, carry):
        rows = pl.ds(pl.multiple_of(i * chunk, chunk), chunk)
        col = cols[rows]
        normed = (o_acc[rows] - col[:, 0:1]) * col[:, 1:2]
        out_ref[rows] = (normed[:, : heads * HD] * gain_ref[...] + bias_ref[...]).astype(out_ref.dtype)
        return carry

    lax.fori_loop(0, LOCAL // chunk, normalize, 0)

    for b, (count, group) in enumerate(BRANCHES):
        pairs = group // 2
        if pairs > 1:
            went = bufs[b].at[pl.ds(0, pairs - 1), side]
            pltpu.make_async_copy(went, went, send_sem.at[b]).wait()
        forwards[b].wait_send()


def per_device(queries, keys, values, slide_lengths, norm_gain, norm_bias):
    heads = queries.shape[0] // HD
    width = heads * HD
    seq = lax.axis_index("seq")
    hy = lax.axis_index("head")
    q = to_token_major(jnp.concatenate([jnp.zeros((SHIFT, LOCAL), queries.dtype), queries]))
    kv = to_token_major(jnp.concatenate([values, keys]))
    kv_lane = jnp.arange(2 * width) % width // HD

    sends = []
    for b, (count, group) in enumerate(BRANCHES):
        starts = [j * 256 + (hy * 64 if b >= 1 else 0) for j in range(heads)]
        chunk = jnp.zeros((count, 2 * width), kv.dtype)
        for j in range(heads):
            piece = lax.dynamic_slice_in_dim(kv, starts[j], count, 0)
            chunk = jnp.where(kv_lane[None, :] == j, piece, chunk)
        sends.append(chunk)

    gain = norm_gain.reshape(1, width)
    bias = norm_bias.reshape(1, width)
    vmem = pl.BlockSpec(memory_space=pltpu.VMEM)
    out = pl.pallas_call(
        attention_kernel,
        out_shape=jax.ShapeDtypeStruct((LOCAL, width), jnp.bfloat16),
        in_specs=[vmem] * 3 + [pl.BlockSpec(memory_space=pltpu.SMEM)] + [vmem] * 2,
        out_specs=vmem,
        scratch_shapes=[
            *[pltpu.VMEM((group // 2, 2, count, 2 * width), jnp.bfloat16) for count, group in BRANCHES],
            pltpu.VMEM((LOCAL, 256), jnp.float32),
            pltpu.VMEM((LOCAL, 256), jnp.float32),
            pltpu.VMEM((LOCAL, 256), jnp.float32),
            pltpu.VMEM((8, LOCAL), jnp.float32),
            pltpu.VMEM((4, 8, LOCAL), jnp.float32),
            pltpu.VMEM((LOCAL, 8), jnp.float32),
            pltpu.VMEM((LOCAL, 8), jnp.int32),
            pltpu.VMEM((16, LOCAL), jnp.int32),
            pltpu.SemaphoreType.DMA((3,)),
            pltpu.SemaphoreType.DMA((3,)),
            pltpu.SemaphoreType.DMA((3,)),
            pltpu.SemaphoreType.DMA((3,)),
            pltpu.SemaphoreType.DMA((3,)),
            pltpu.SemaphoreType.DMA((3,)),
            pltpu.SemaphoreType.DMA((1,)),
        ],
        compiler_params=pltpu.CompilerParams(
            collective_id=0, has_side_effects=True, vmem_limit_bytes=60 * 1024 * 1024
        ),
    )(q, kv, jnp.concatenate(sends), slide_lengths, gain, bias)
    return from_token_major(out)


def solution(mesh):
    placed = (P("head", "seq"),) * 3 + (P(), P("head"), P("head"))
    return jax.shard_map(
        per_device, mesh=mesh, in_specs=placed, out_specs=P("head", "seq"), check_vma=False
    )
```
